32 devices in a mesh: ctx: 8 (over z, x), head: 4 (over y, core).
Axes of the slice: x: 2, y: 2, z: 4, core: 2. Of those that a mesh axis runs over, the one named last changes fastest.
Arguments:
- query: bfloat16 [4096, 1024], P('ctx', 'head'), may hold values from -7.5 to 7.5
- key: bfloat16 [4096, 1024], P('ctx', 'head'), may hold values from -7.5 to 7.5
- value: bfloat16 [4096, 1024], P('ctx', 'head'), may hold values from -6 to 6
- grad_out: bfloat16 [4096, 1024], P('ctx', 'head'), may hold values from -6 to 6
- picks: int32 [32, 16, 4], P('ctx', 'head'), may hold values from 0 to 7, as said below
Outputs:
- attn_out: bfloat16 [4096, 1024], P('ctx', 'head')
- grad_query: bfloat16 [4096, 1024], P('ctx', 'head')
- grad_key: bfloat16 [4096, 1024], P('ctx', 'head')
- grad_value: bfloat16 [4096, 1024], P('ctx', 'head')
The draws below stay inside these ranges and needn't reach their ends.
Inputs may be any that keep to these rules, and one draw needn't show every extreme that they name: picks[g, h, 0] is the block that holds tile g; every other entry is that block again (no further block) or an earlier block. Among the tiles of one block and one group of 4 consecutive heads, no earlier block is named twice.
All inputs are finite; a program needn't handle non-finite values.
Results may differ from the reference program's by a relative error of at most 0.017.
Values may be sent and summed in bfloat16 or wider, within the bound.
No kernel may reach another device: no remote copies, remote signals or barrier semaphores. Data moves between devices by JAX's collectives and lax.ppermute only.
A program may use at most 64 MiB of HBM per device.

```python
import math
import jax
import jax.numpy as jnp
from jax import lax

HEAD_DIM = 64
HEADS = 16
BLOCK = 512
TILE = 128
TOPK = 4
NBLOCKS = 8
HEAD_GROUPS = 4
HEADS_GRP = 4
TILES_DEV = 4
TOKENS = 4096
TILES = 32


def draw_query(key, part):
    noise = jax.random.normal(jax.random.fold_in(key, 11), (TOKENS, HEADS, HEAD_DIM), jnp.float32)
    noise = 1.5 * noise
    noise = jnp.clip(noise, -7.5, 7.5)
    return noise.reshape(TOKENS, HEADS * HEAD_DIM).astype(jnp.bfloat16)


def draw_key(key, part):
    noise = jax.random.normal(jax.random.fold_in(key, 21), (TOKENS, HEADS, HEAD_DIM), jnp.float32)
    noise = jnp.clip(noise, -7.5, 7.5)
    return noise.reshape(TOKENS, HEADS * HEAD_DIM).astype(jnp.bfloat16)


def draw_picks(key, part):
    tasks = TILES_DEV * HEADS_GRP * (TOPK - 1)
    cap_tasks = max(2 * tasks // 3, 1)
    base = jax.random.fold_in(key, 301)
    key_rank, key_slot = jax.random.split(base)
    owner = jnp.arange(NBLOCKS, dtype=jnp.int32)
    columns = jnp.arange(NBLOCKS, dtype=jnp.int32)
    raw = jax.random.randint(key_rank, (NBLOCKS, HEAD_GROUPS, NBLOCKS), 0, 4096, dtype=jnp.int32)
    score = raw * NBLOCKS + columns[None, None, :]
    score = jnp.where(columns[None, None, :] == 0, 4096 * NBLOCKS + 1, score)
    score = jnp.where(columns[None, None, :] < owner[:, None, None], score, -1 - columns[None, None, :])
    ranking = jnp.argsort(-score, axis=-1).astype(jnp.int32)
    extra = max(tasks - NBLOCKS, 0)
    if extra > 0:
        ranking = jnp.concatenate([ranking, jnp.zeros((NBLOCKS, HEAD_GROUPS, extra), jnp.int32)], axis=-1)
    candidate = ranking[..., :tasks]
    slot_raw = jax.random.randint(key_slot, (NBLOCKS, HEAD_GROUPS, tasks), 0, 4096, dtype=jnp.int32)
    slot_keys = slot_raw * tasks + jnp.arange(tasks, dtype=jnp.int32)[None, None, :]
    permuted = jnp.argsort(slot_keys, axis=-1).astype(jnp.int32)
    chosen = jnp.take_along_axis(candidate, permuted, axis=-1)
    limit = jnp.minimum(owner, cap_tasks)
    active = permuted < limit[:, None, None]
    target = jnp.where(active, chosen, owner[:, None, None])
    target = target.reshape(NBLOCKS, HEAD_GROUPS, TILES_DEV, HEADS_GRP, TOPK - 1)
    leading = jnp.broadcast_to(owner[:, None, None, None, None], (NBLOCKS, HEAD_GROUPS, TILES_DEV, HEADS_GRP, 1))
    full = jnp.concatenate([leading, target], axis=-1)
    full = full.transpose(0, 2, 1, 3, 4).reshape(NBLOCKS * TILES_DEV, HEAD_GROUPS * HEADS_GRP, TOPK)
    return full.astype(jnp.int32)


def level_of(rng, shape, cuts, low, largest):
    loudness, own = 1.0, jax.random.fold_in(rng, 6)
    for dim, shards_of in cuts:
        heights = jnp.exp(jax.random.uniform(jax.random.fold_in(own, dim), (shards_of,), jnp.float32, low / len(cuts), largest / len(cuts)))
        loudness = loudness * jnp.repeat(heights, shape[dim] // shards_of).reshape([-1 if axis == dim else 1 for axis in range(len(shape))])
    return loudness


def gaussian(own_key, extent, scale, bound, pieces=(), kind=jnp.bfloat16):
    drawn = jax.random.normal(own_key, extent, jnp.float32) * scale
    if len(pieces) > 0:
        drawn = level_of(own_key, extent, pieces, -0.22, 0.18) * drawn
    return jnp.clip(drawn, min=-bound, max=bound).astype(kind)


def setup_inputs(seed: int = 0) -> dict:
    streams_of = jax.random.split(jax.random.key(seed), 6)
    return {
        "query": draw_query(jax.random.fold_in(streams_of[5], 71), 0),
        "key": draw_key(jax.random.fold_in(streams_of[5], 71), 0),
        "value": gaussian(streams_of[2], (TOKENS, HEADS * HEAD_DIM), 1.0, 6.0, ((0, 8), (1, 4))),
        "grad_out": gaussian(streams_of[3], (TOKENS, HEADS * HEAD_DIM), 1.0, 6.0, ((0, 8), (1, 4))),
        "picks": draw_picks(jax.random.fold_in(streams_of[5], 71), 0),
    }


masked_value = -1e+30

def reference(query, key, value, grad_out, picks):
    scaling = 1.0 / math.sqrt(HEAD_DIM)
    per_block = BLOCK // TILE
    q_tiles = query.reshape(TILES, TILE, HEADS, HEAD_DIM).transpose(0, 2, 1, 3)
    do_tiles = grad_out.reshape(TILES, TILE, HEADS, HEAD_DIM).transpose(0, 2, 1, 3)
    k_blocks = key.reshape(NBLOCKS, BLOCK, HEADS, HEAD_DIM).transpose(2, 0, 1, 3)
    v_blocks = value.reshape(NBLOCKS, BLOCK, HEADS, HEAD_DIM).transpose(2, 0, 1, 3)
    head_ids = jnp.arange(HEADS, dtype=jnp.int32)[:, None]
    is_first = jnp.arange(TOPK, dtype=jnp.int32) == 0
    key_pos = jnp.arange(BLOCK, dtype=jnp.int32)

    def advance(totals, inputs):
        grad_k, grad_v = totals
        tile_id, q_tile, do_tile, blocks = inputs
        own_block = tile_id // per_block
        is_valid = is_first[None, :] | (blocks != own_block)
        valid_mask = is_valid[:, :, None, None]
        key_rows = k_blocks[head_ids, blocks].astype(jnp.float32)
        value_rows = v_blocks[head_ids, blocks].astype(jnp.float32)
        query_pos = tile_id % per_block * TILE + jnp.arange(TILE, dtype=jnp.int32)
        causal = key_pos[None, :] <= query_pos[:, None]
        allowed = jnp.logical_or(jnp.logical_not(is_first)[:, None, None], causal[None])
        query_wide = q_tile.astype(jnp.float32)
        scores = jnp.einsum('hqd,hikd->hiqk', query_wide, key_rows) * scaling
        scores = jnp.where(allowed[None], scores, masked_value)
        peak_score = lax.optimization_barrier(jnp.max(scores, axis=-1, keepdims=True))
        part_lse = peak_score + jnp.log(lax.optimization_barrier(jnp.sum(jnp.exp(scores - peak_score), axis=-1, keepdims=True)))
        attend = jnp.exp(scores - part_lse)
        attend_low = lax.optimization_barrier(attend.astype(jnp.bfloat16)).astype(jnp.float32)
        part_out = jnp.einsum('hiqk,hikd->hiqd', attend_low, value_rows)
        lse_valid = jnp.where(valid_mask, part_lse, masked_value)
        peak_lse = lax.optimization_barrier(jnp.max(lse_valid, axis=1, keepdims=True))
        total_lse = peak_lse + jnp.log(lax.optimization_barrier(jnp.sum(jnp.exp(lse_valid - peak_lse), axis=1, keepdims=True)))
        weight = jnp.where(valid_mask, jnp.exp(part_lse - total_lse), 0.0)
        out_low = lax.optimization_barrier(lax.optimization_barrier(jnp.sum(weight * part_out, axis=1)).astype(jnp.bfloat16))
        row_delta = lax.optimization_barrier(jnp.sum(do_tile.astype(jnp.float32) * out_low.astype(jnp.float32), axis=-1, keepdims=True))
        scaled = weight * do_tile.astype(jnp.float32)[:, None]
        scaled = lax.optimization_barrier(scaled.astype(jnp.bfloat16)).astype(jnp.float32)
        row_shift = weight * row_delta[:, None]
        part_dv = jnp.einsum('hiqk,hiqd->hikd', attend_low, scaled)
        grad_prob = jnp.einsum('hiqd,hikd->hiqk', scaled, value_rows)
        dscore = attend * (grad_prob - row_shift)
        dscore = lax.optimization_barrier(dscore.astype(jnp.bfloat16)).astype(jnp.float32)
        part_dk = jnp.einsum('hiqk,hqd->hikd', dscore, query_wide) * scaling
        part_dq = lax.optimization_barrier(jnp.sum(jnp.einsum('hiqk,hikd->hiqd', dscore, key_rows) * scaling, axis=1))
        grad_k = grad_k.at[head_ids, blocks].add(part_dk)
        grad_v = grad_v.at[head_ids, blocks].add(part_dv)
        return ((grad_k, grad_v), (out_low, part_dq))
    zeros_kv = jnp.zeros((HEADS, NBLOCKS, BLOCK, HEAD_DIM), jnp.float32)
    tile_ids = jnp.arange(TILES, dtype=jnp.int32)
    totals, outputs = lax.scan(advance, (zeros_kv, zeros_kv), (tile_ids, q_tiles, do_tiles, picks))
    grad_k, grad_v = totals
    out_tiles, dq_tiles = outputs
    attn_out = out_tiles.transpose(0, 2, 1, 3).reshape(TOKENS, HEADS * HEAD_DIM)
    grad_query = dq_tiles.transpose(0, 2, 1, 3).reshape(TOKENS, HEADS * HEAD_DIM).astype(jnp.bfloat16)
    grad_key = grad_k.transpose(1, 2, 0, 3).reshape(TOKENS, HEADS * HEAD_DIM).astype(jnp.bfloat16)
    grad_value = grad_v.transpose(1, 2, 0, 3).reshape(TOKENS, HEADS * HEAD_DIM).astype(jnp.bfloat16)
    return (attn_out, grad_query, grad_key, grad_value)
```

```python
import math

import jax
import jax.numpy as jnp
from jax import lax
from jax.experimental import pallas as pl
from jax.experimental.pallas import tpu as pltpu
from jax.sharding import PartitionSpec as P

masked_value = -1e30
highest = lax.Precision.HIGHEST
LOG2E = math.log2(math.e)
pair_budget = 8 << 20


def attend_slots(q_slots, head_ids, k_heads, v_heads, scaling):
    key_rows = jnp.take(k_heads, head_ids, axis=0)
    value_rows = jnp.take(v_heads, head_ids, axis=0)
    scores = (
        jnp.einsum("ndq,nkd->nqk", q_slots, key_rows, preferred_element_type=jnp.float32) * scaling
    )
    peak_score = jnp.max(scores, axis=-1, keepdims=True)
    log_total = peak_score + jnp.log(jnp.sum(jnp.exp(scores - peak_score), axis=-1, keepdims=True))
    attend_low = jnp.exp(scores - log_total).astype(jnp.bfloat16)
    outputs = jnp.einsum("nqk,nkd->ndq", attend_low, value_rows, preferred_element_type=jnp.float32)
    return (outputs, log_total[..., 0])


def slot_grads(q_slots, g_slots, c_slots, lse_slots, head_ids, k_heads, v_heads, scaling):
    key_rows = jnp.take(k_heads, head_ids, axis=0)
    value_rows = jnp.take(v_heads, head_ids, axis=0)
    scores = (
        jnp.einsum("ndq,nkd->nqk", q_slots, key_rows, preferred_element_type=jnp.float32) * scaling
    )
    attend = jnp.exp(scores - lse_slots[..., None])
    attend_low = attend.astype(jnp.bfloat16)
    grad_v = jnp.einsum("nqk,ndq->nkd", attend_low, g_slots, preferred_element_type=jnp.float32)
    grad_prob = jnp.einsum("ndq,nkd->nqk", g_slots, value_rows, preferred_element_type=jnp.float32)
    dscore = (attend * (grad_prob - c_slots[..., None])).astype(jnp.bfloat16)
    grad_k = (
        jnp.einsum("nqk,ndq->nkd", dscore, q_slots, preferred_element_type=jnp.float32) * scaling
    )
    grad_q = (
        jnp.einsum("nqk,nkd->ndq", dscore, key_rows, preferred_element_type=jnp.float32) * scaling
    )
    return (grad_k, grad_v, grad_q)


def local(query, key, value, grad_out, picks):
    row_count, columns = query.shape
    tiles_dev, groups, picked = picks.shape
    head_dim = columns // groups
    tile_rows = row_count // tiles_dev
    others = picked - 1
    scaling = 1.0 / math.sqrt(head_dim)
    devices = lax.axis_size("ctx")
    own_block = lax.axis_index("ctx")
    per_group = min(8, devices)
    all_picks = lax.all_gather(picks, "ctx", axis=0, tiled=True)
    q_heads = query.reshape(row_count, groups, head_dim).transpose(1, 0, 2)
    k_heads = key.reshape(row_count, groups, head_dim).transpose(1, 0, 2)
    v_heads = value.reshape(row_count, groups, head_dim).transpose(1, 0, 2)
    q_tiles = query.reshape(tiles_dev, tile_rows, groups, head_dim)
    do_tiles = grad_out.reshape(tiles_dev, tile_rows, groups, head_dim)
    do_major = do_tiles.transpose(0, 2, 1, 3)
    positions = jnp.arange(row_count, dtype=jnp.int32)
    tile_masks = []
    for tile_step in range(tiles_dev):
        span = (tile_step + 1) * tile_rows
        query_pos = positions[tile_step * tile_rows : span]
        tile_masks.append(positions[None, :span] <= query_pos[:, None])
    targets = picks[:, :, 1:]
    active = targets != own_block
    lookup = jnp.where(active, targets, own_block).reshape(-1)
    peer_ids = jnp.arange(devices, dtype=jnp.int32)
    routing = ((targets[None] == peer_ids[:, None, None, None]) & active[None]).astype(jnp.float32)
    routing_low = routing.astype(jnp.bfloat16)
    send_q = jnp.einsum(
        "jtgi,tqgd->jdq", routing_low, q_tiles, preferred_element_type=jnp.float32
    ).astype(jnp.bfloat16)
    recv_q = lax.all_to_all(send_q, "ctx", split_axis=0, concat_axis=0, tiled=True)

    def own_forward(inputs):
        q_head, k_head, v_head = inputs
        out_list = []
        lse_list = []
        for tile_step in range(tiles_dev):
            span = (tile_step + 1) * tile_rows
            q_part = q_head[tile_step * tile_rows : span]
            scores = (
                jnp.einsum("qd,kd->qk", q_part, k_head[:span], preferred_element_type=jnp.float32)
                * scaling
            )
            scores = jnp.where(tile_masks[tile_step], scores, masked_value)
            peak_score = jnp.max(scores, axis=-1, keepdims=True)
            log_total = peak_score + jnp.log(
                jnp.sum(jnp.exp(scores - peak_score), axis=-1, keepdims=True)
            )
            attend_low = jnp.exp(scores - log_total).astype(jnp.bfloat16)
            out_list.append(jnp.dot(attend_low, v_head[:span], preferred_element_type=jnp.float32))
            lse_list.append(log_total[:, 0])
        return (jnp.concatenate(out_list, axis=0), jnp.concatenate(lse_list, axis=0))

    own_out, own_lse = lax.map(own_forward, (q_heads, k_heads, v_heads))
    sources = all_picks.reshape(devices, tiles_dev, groups, picked)[..., 1:]
    incoming = (sources == own_block) & (peer_ids[:, None, None, None] != own_block)
    live_in = jnp.any(incoming, axis=(1, 2, 3))
    group_ids = jnp.arange(groups, dtype=jnp.int32)
    head_of = jnp.sum(jnp.where(incoming, group_ids[None, None, :, None], 0), axis=(1, 2, 3))
    ranking = jnp.argsort(jnp.where(live_in, 0, 1) * devices + peer_ids)
    inverse = jnp.argsort(ranking)
    rounds = (jnp.sum(live_in.astype(jnp.int32)) + per_group - 1) // per_group
    heads_sorted = jnp.take(head_of, ranking, axis=0)
    q_sorted = jnp.take(recv_q, ranking, axis=0)

    def forward_turn(turn, totals):
        served_out, served_lse = totals
        offset = turn * per_group
        query_part = lax.dynamic_slice_in_dim(q_sorted, offset, per_group, 0)
        head_part = lax.dynamic_slice_in_dim(heads_sorted, offset, per_group, 0)
        out_part, lse_part = attend_slots(query_part, head_part, k_heads, v_heads, scaling)
        served_out = lax.dynamic_update_slice_in_dim(served_out, out_part, offset, 0)
        served_lse = lax.dynamic_update_slice_in_dim(served_lse, lse_part, offset, 0)
        return (served_out, served_lse)

    start_fwd = (
        jnp.zeros((devices, head_dim, tile_rows), jnp.float32),
        jnp.zeros((devices, tile_rows), jnp.float32),
    )
    served_out, served_lse = lax.fori_loop(0, rounds, forward_turn, start_fwd)
    back_out, back_lse = (
        lax.all_to_all(
            jnp.take(served_out, inverse, axis=0), "ctx", split_axis=0, concat_axis=0, tiled=True
        ),
        lax.all_to_all(
            jnp.take(served_lse, inverse, axis=0), "ctx", split_axis=0, concat_axis=0, tiled=True
        ),
    )
    task_out = jnp.take(back_out, lookup, axis=0).reshape(
        tiles_dev, groups, others, head_dim, tile_rows
    )
    task_lse = jnp.take(back_lse, lookup, axis=0).reshape(tiles_dev, groups, others, tile_rows)
    own_out_t = own_out.reshape(groups, tiles_dev, tile_rows, head_dim).transpose(1, 0, 2, 3)
    own_lse_t = own_lse.reshape(groups, tiles_dev, tile_rows).transpose(1, 0, 2)
    active_rows = active[..., None]
    rem_lse = jnp.where(active_rows, task_lse, masked_value)
    ceiling = jnp.maximum(own_lse_t, jnp.max(rem_lse, axis=2))
    log_total = ceiling + jnp.log(
        jnp.exp(own_lse_t - ceiling) + jnp.sum(jnp.exp(rem_lse - ceiling[:, :, None]), axis=2)
    )
    own_weight = jnp.exp(own_lse_t - log_total)
    rem_weight = jnp.where(active_rows, jnp.exp(rem_lse - log_total[:, :, None]), 0.0)
    mixed = own_weight[..., None] * own_out_t + jnp.einsum(
        "tgiq,tgidq->tgqd", rem_weight, task_out, precision=highest
    )
    out_low = mixed.astype(jnp.bfloat16)
    attn_out = out_low.transpose(0, 2, 1, 3).reshape(row_count, columns)
    row_delta = jnp.sum(do_major.astype(jnp.float32) * out_low.astype(jnp.float32), axis=-1)
    own_scaled = (own_weight[..., None] * do_major.astype(jnp.float32)).astype(jnp.bfloat16)
    own_shift = own_weight * row_delta
    g_heads = own_scaled.transpose(1, 0, 2, 3).reshape(groups, row_count, head_dim)
    c_heads = own_shift.transpose(1, 0, 2).reshape(groups, row_count)

    def own_backward(inputs):
        q_head, k_head, v_head, g_head, c_head, lse_head = inputs
        grad_k = jnp.zeros((row_count, head_dim), jnp.float32)
        grad_v = jnp.zeros((row_count, head_dim), jnp.float32)
        dq_list = []
        for tile_step in range(tiles_dev):
            first = tile_step * tile_rows
            span = (tile_step + 1) * tile_rows
            q_part = q_head[first:span]
            g_part = g_head[first:span]
            k_part = k_head[:span]
            scores = (
                jnp.einsum("qd,kd->qk", q_part, k_part, preferred_element_type=jnp.float32)
                * scaling
            )
            scores = jnp.where(tile_masks[tile_step], scores, masked_value)
            attend = jnp.exp(scores - lse_head[first:span, None])
            attend_low = attend.astype(jnp.bfloat16)
            part_dv = jnp.einsum(
                "qk,qd->kd", attend_low, g_part, preferred_element_type=jnp.float32
            )
            grad_prob = jnp.einsum(
                "qd,kd->qk", g_part, v_head[:span], preferred_element_type=jnp.float32
            )
            dscore = (attend * (grad_prob - c_head[first:span, None])).astype(jnp.bfloat16)
            part_dk = (
                jnp.einsum("qk,qd->kd", dscore, q_part, preferred_element_type=jnp.float32)
                * scaling
            )
            dq_list.append(jnp.dot(dscore, k_part, preferred_element_type=jnp.float32) * scaling)
            padding = ((0, row_count - span), (0, 0))
            grad_k = grad_k + jnp.pad(part_dk, padding)
            grad_v = grad_v + jnp.pad(part_dv, padding)
        return (grad_k, grad_v, jnp.concatenate(dq_list, axis=0))

    own_dk, own_dv, own_dq = lax.map(
        own_backward, (q_heads, k_heads, v_heads, g_heads, c_heads, own_lse)
    )
    rem_shift = rem_weight * row_delta[:, :, None]
    rem_scaled = (rem_weight[..., None] * do_major[:, :, None].astype(jnp.float32)).astype(
        jnp.bfloat16
    )
    send_g = jnp.einsum(
        "jtgi,tgiqd->jdq", routing_low, rem_scaled, preferred_element_type=jnp.float32
    )
    send_c = jnp.einsum("jtgi,tgiq->jq", routing, rem_shift, precision=highest)
    recv_g, recv_c = (
        lax.all_to_all(send_g, "ctx", split_axis=0, concat_axis=0, tiled=True),
        lax.all_to_all(send_c, "ctx", split_axis=0, concat_axis=0, tiled=True),
    )
    g_sorted = jnp.take(recv_g, ranking, axis=0).astype(jnp.bfloat16)
    c_sorted = jnp.take(recv_c, ranking, axis=0)

    def backward_turn(turn, totals):
        grad_k, grad_v, served_dq = totals
        offset = turn * per_group
        query_part = lax.dynamic_slice_in_dim(q_sorted, offset, per_group, 0)
        cot_part = lax.dynamic_slice_in_dim(g_sorted, offset, per_group, 0)
        shift_part = lax.dynamic_slice_in_dim(c_sorted, offset, per_group, 0)
        lse_part = lax.dynamic_slice_in_dim(served_lse, offset, per_group, 0)
        head_part = lax.dynamic_slice_in_dim(heads_sorted, offset, per_group, 0)
        part_dk, part_dv, part_dq = slot_grads(
            query_part, cot_part, shift_part, lse_part, head_part, k_heads, v_heads, scaling
        )
        head_onehot = (head_part[:, None] == group_ids[None, :]).astype(jnp.float32)
        grad_k = grad_k + jnp.einsum("ng,nkd->gkd", head_onehot, part_dk, precision=highest)
        grad_v = grad_v + jnp.einsum("ng,nkd->gkd", head_onehot, part_dv, precision=highest)
        served_dq = lax.dynamic_update_slice_in_dim(served_dq, part_dq, offset, 0)
        return (grad_k, grad_v, served_dq)

    zeros_heads = jnp.zeros((groups, row_count, head_dim), jnp.float32)
    start_bwd = (zeros_heads, zeros_heads, jnp.zeros((devices, head_dim, tile_rows), jnp.float32))
    rem_dk, rem_dv, served_dq = lax.fori_loop(0, rounds, backward_turn, start_bwd)
    back_dq = lax.all_to_all(
        jnp.take(served_dq, inverse, axis=0).astype(jnp.bfloat16),
        "ctx",
        split_axis=0,
        concat_axis=0,
        tiled=True,
    ).astype(jnp.float32)
    task_dq = jnp.take(back_dq, lookup, axis=0).reshape(
        tiles_dev, groups, others, head_dim, tile_rows
    )
    rem_dq = jnp.sum(jnp.where(active[..., None, None], task_dq, 0.0), axis=2)
    own_dq_t = own_dq.reshape(groups, tiles_dev, tile_rows, head_dim).transpose(1, 0, 2, 3)
    total_dq = own_dq_t + rem_dq.transpose(0, 1, 3, 2)
    grad_query = total_dq.transpose(0, 2, 1, 3).reshape(row_count, columns).astype(jnp.bfloat16)
    grad_key = (own_dk + rem_dk).transpose(1, 0, 2).reshape(row_count, columns).astype(jnp.bfloat16)
    grad_value = (
        (own_dv + rem_dv).transpose(1, 0, 2).reshape(row_count, columns).astype(jnp.bfloat16)
    )
    return (attn_out, grad_query, grad_key, grad_value)


def pack_kernel(tiles_dev, groups, picked, tile_rows, head_dim, devices):
    def body(picks_ref, q_ref, g_ref, send_ref, task_ref):
        own = picks_ref[0, 0, 0]
        meta_rows = send_ref.shape[1] - tile_rows
        lanes = send_ref.shape[2]
        row = lax.broadcasted_iota(jnp.int32, (meta_rows, lanes), 0)
        blank = jnp.zeros((meta_rows, lanes), jnp.bfloat16)
        for peer in range(devices):
            send_ref[peer, tile_rows:, :] = blank
            task_ref[peer] = -1
        for tile in range(tiles_dev):
            rows = slice(tile * tile_rows, (tile + 1) * tile_rows)
            for head in range(groups):
                cols = slice(head * head_dim, (head + 1) * head_dim)
                block = jnp.concatenate([q_ref[rows, cols], g_ref[rows, cols]], axis=1)
                code = tile * groups + head
                meta = jnp.where(row == 0, code + 1, 0)
                for entry in range(1, picked):
                    meta = jnp.where(row == entry, picks_ref[tile, head, entry], meta)
                meta = meta.astype(jnp.float32).astype(jnp.bfloat16)
                for entry in range(1, picked):
                    target = picks_ref[tile, head, entry]
                    send_ref[target, :tile_rows, :] = block
                    send_ref[target, tile_rows:, :] = meta
                    task_ref[target] = code
        task_ref[own] = -1

    return body


def soft_parts(scores, grads):
    peak = jnp.max(scores, axis=0, keepdims=True)
    powers = jnp.exp2(scores - peak)
    total = jnp.sum(powers, axis=0, keepdims=True)
    inverse = 1.0 / total
    mean_grad = jnp.sum(powers * grads, axis=0, keepdims=True) * inverse
    spread = powers * (grads - mean_grad)
    both = jnp.concatenate([powers.astype(jnp.bfloat16), spread.astype(jnp.bfloat16)], axis=1)
    return both, peak + jnp.log2(total), mean_grad, inverse


def split_low(x):
    high = x.astype(jnp.bfloat16).astype(jnp.float32)
    return high, x - high


def paired(block, head_dim):
    lane = lax.broadcasted_iota(jnp.int32, block.shape, 1)
    zero = jnp.zeros_like(block)
    left = jnp.where(lane < head_dim, block, zero)
    right = jnp.where(lane < head_dim, zero, block)
    return jnp.concatenate([left, right], axis=0)


def dot_t(a, b):
    return lax.dot_general(a, b, (((1,), (1,)), ((), ())), preferred_element_type=jnp.float32)


def own_kernel(tiles_dev, groups, tile_rows, head_dim, devices):
    scale = LOG2E / math.sqrt(head_dim)

    def body(q_ref, k_ref, v_ref, g_ref, kv_ref, vkt_ref, qgt_ref, mix_ref, dot_ref, stat_ref,
             table_ref, *pd_refs):
        sub = lax.broadcasted_iota(jnp.int32, (tile_rows, tile_rows), 0)
        lane = lax.broadcasted_iota(jnp.int32, (tile_rows, tile_rows), 1)
        causal = sub <= lane
        for head in range(groups):
            cols = slice(head * head_dim, (head + 1) * head_dim)
            k_head = k_ref[:, cols]
            v_head = v_ref[:, cols]
            kv_ref[head] = jnp.concatenate([k_head, v_head], axis=1)
            vkt_ref[head] = jnp.concatenate([v_head, k_head], axis=1).T
            qgt_ref[head] = jnp.concatenate([q_ref[:, cols], g_ref[:, cols]], axis=1).T
            for tile in range(tiles_dev):
                rows = slice(tile * tile_rows, (tile + 1) * tile_rows)
                span = (tile + 1) * tile_rows
                code = tile * groups + head
                block = jnp.concatenate([q_ref[rows, cols], g_ref[rows, cols]], axis=1)
                both = dot_t(kv_ref[head, :span, :], paired(block, head_dim))
                scores = both[:, :tile_rows] * scale
                last = jnp.where(causal, scores[span - tile_rows :], masked_value)
                if tile:
                    scores = jnp.concatenate([scores[: span - tile_rows], last], axis=0)
                else:
                    scores = last
                pair, lse, mean_grad, inverse = soft_parts(scores, both[:, tile_rows:])
                for part in range(tile + 1):
                    pd_refs[part][head, :, (tile - part) * 2 * tile_rows : (tile - part + 1) * 2 * tile_rows] = (
                        pair[part * tile_rows : (part + 1) * tile_rows]
                    )
                result = jnp.dot(vkt_ref[head, :, :span], pair, preferred_element_type=jnp.float32)
                mix_ref[code] = result[:, :tile_rows] * inverse
                dot_ref[code] = result[head_dim:, tile_rows:] * inverse
                stat_ref[0, code : code + 1, :] = lse
                stat_ref[1, code : code + 1, :] = mean_grad
                stat_ref[2, code : code + 1, :] = inverse
                parts = split_low(lse) + split_low(mean_grad)
                table_ref[code] = jnp.concatenate(
                    [jnp.broadcast_to(p, (devices, tile_rows)) for p in parts], axis=0
                )

    return body


def serve_kernel(groups, tile_rows, head_dim, devices):
    scale = LOG2E / math.sqrt(head_dim)

    def body(picks_ref, task_ref, recv_ref, kv_ref, vkt_ref, table_ref, send_ref, pd_ref, inv_ref, st_ref):
        own = picks_ref[0, 0, 0]
        st_ref[...] = jnp.zeros_like(st_ref)
        inv_ref[...] = jnp.zeros_like(inv_ref)

        def turn(source, carry):
            code = jnp.max(recv_ref[source, tile_rows:, :].astype(jnp.float32)[0:1, :]).astype(jnp.int32) - 1

            @pl.when(code >= 0)
            def _():
                head = lax.rem(code, groups)
                block = recv_ref[source, :tile_rows, :]
                both = dot_t(kv_ref[head], paired(block, head_dim))
                pair, lse, mean_grad, inverse = soft_parts(both[:, :tile_rows] * scale, both[:, tile_rows:])
                pd_ref[source] = pair
                result = jnp.dot(vkt_ref[head], pair, preferred_element_type=jnp.float32)
                send_ref[source, : 2 * head_dim, :] = (result[:, :tile_rows] * inverse).astype(jnp.bfloat16)
                send_ref[source, 2 * head_dim : 3 * head_dim, :] = (
                    result[head_dim:, tile_rows:] * inverse
                ).astype(jnp.bfloat16)
                parts = split_low(lse) + split_low(mean_grad)
                for index in range(4):
                    st_ref[pl.ds(index * devices + source, 1), :] = parts[index]
                inv_ref[pl.ds(source, 1), :] = inverse

            return carry

        lax.fori_loop(own + 1, devices, turn, 0)
        table = st_ref[...]
        row = lax.broadcasted_iota(jnp.int32, table.shape, 0)
        mine = lax.rem(row, devices) == own
        for peer in range(devices):
            code = jnp.maximum(task_ref[peer], 0)
            send_ref[peer, 3 * head_dim :, :] = jnp.where(mine, table_ref[code], table).astype(jnp.bfloat16)

    return body


def flip_kernel(devices, tile_rows):
    def body(recv_ref, qgt_ref):
        for source in range(1, devices):
            qgt_ref[source] = recv_ref[source, :tile_rows, :].T

    return body


def final_kernel(tiles_dev, groups, picked, tile_rows, head_dim, devices):
    scaling = 1.0 / math.sqrt(head_dim)

    def body(picks_ref, task_ref, recv_ref, back_ref, qgt_ref, qgt_in_ref, mix_ref, dot_ref, stat_ref,
             inv_ref, pd_in_ref, *rest):
        pd_refs = rest[:tiles_dev]
        out_ref, dq_ref, dk_ref, dv_ref, acc_ref, grad_ref, lse_sc, gd_sc, w_sc, d_sc, x_ref = rest[tiles_dev:]
        own = picks_ref[0, 0, 0]
        tasks = tiles_dev * groups
        base = 3 * head_dim

        lse_of = []
        gd_of = []
        for peer in range(devices):
            table = back_ref[peer, base : base + 4 * devices, :].astype(jnp.float32)
            lse_of.append(table[:devices] + table[devices : 2 * devices])
            gd_of.append(table[2 * devices : 3 * devices] + table[3 * devices :])
            lse_sc[peer] = lse_of[peer]
            gd_sc[peer] = gd_of[peer]

        ids = lax.broadcasted_iota(jnp.int32, (devices, tile_rows), 0)
        metas = [recv_ref[source, tile_rows : tile_rows + 16, :].astype(jnp.float32) for source in range(devices)]
        lists = [
            jnp.concatenate([metas[source][entry : entry + 1] for source in range(devices)], axis=0).astype(jnp.int32)
            for entry in range(1, picked)
        ]
        chosen = []
        for peer in range(devices):
            active = ids == peer
            for entry in lists:
                active = active | (entry == peer)
            chosen.append(active)
        peak = jnp.full((devices, tile_rows), masked_value, jnp.float32)
        for peer in range(devices):
            peak = jnp.maximum(peak, jnp.where(chosen[peer], lse_of[peer], masked_value))
        total = jnp.zeros_like(peak)
        delta = jnp.zeros_like(peak)
        for peer in range(devices):
            power = jnp.where(chosen[peer], jnp.exp2(lse_of[peer] - peak), 0.0)
            total = total + power
            delta = delta + jnp.where(chosen[peer], power * gd_of[peer], 0.0)
        delta = delta / total
        mine_gd = gd_sc[own]
        weight = jnp.exp2(lse_sc[own] - peak) / total * inv_ref[...]
        w_sc[0] = weight
        w_sc[1] = weight * (mine_gd - delta)

        code_ids = lax.broadcasted_iota(jnp.int32, (tasks, tile_rows), 0)
        own_lse = stat_ref[0]
        own_gd = stat_ref[1]
        peak = own_lse
        rows_lse = [lse_sc[peer, pl.ds(own, 1), :] for peer in range(devices)]
        rows_gd = [gd_sc[peer, pl.ds(own, 1), :] for peer in range(devices)]
        for peer in range(devices):
            peak = jnp.maximum(peak, jnp.where(code_ids == task_ref[peer], rows_lse[peer], masked_value))
        own_power = jnp.exp2(own_lse - peak)
        total = own_power
        delta = own_power * own_gd
        for peer in range(devices):
            here = code_ids == task_ref[peer]
            power = jnp.where(here, jnp.exp2(rows_lse[peer] - peak), 0.0)
            total = total + power
            delta = delta + jnp.where(here, power * rows_gd[peer], 0.0)
        inverse = 1.0 / total
        delta = delta * inverse
        own_weight = own_power * inverse
        d_sc[0] = peak
        d_sc[1] = inverse
        d_sc[2] = delta
        d_sc[3] = own_weight
        d_sc[4] = own_weight * stat_ref[2]
        d_sc[5] = own_weight * stat_ref[2] * (own_gd - delta)
        d_sc[6] = own_weight * (own_gd - delta)

        for code in range(tasks):
            mix = mix_ref[code]
            acc_ref[code, :head_dim, :] = mix[:head_dim] * d_sc[3, code : code + 1, :]
            acc_ref[code, head_dim:, :] = (
                dot_ref[code] * d_sc[3, code : code + 1, :] + mix[head_dim:] * d_sc[6, code : code + 1, :]
            )

        def gather(peer, carry):
            code = task_ref[peer]

            @pl.when(code >= 0)
            def _():
                at = pl.ds(code, 1)
                part_w = jnp.exp2(lse_sc[peer, pl.ds(own, 1), :] - d_sc[0, at, :]) * d_sc[1, at, :]
                shift = part_w * (gd_sc[peer, pl.ds(own, 1), :] - d_sc[2, at, :])
                mix = back_ref[peer, : 2 * head_dim, :].astype(jnp.float32)
                low = back_ref[peer, 2 * head_dim : 3 * head_dim, :].astype(jnp.float32)
                acc_ref[code, :head_dim, :] += mix[:head_dim] * part_w
                acc_ref[code, head_dim:, :] += low * part_w + mix[head_dim:] * shift

            return carry

        lax.fori_loop(0, own, gather, 0)

        for head in range(groups):
            for tile in range(tiles_dev):
                code = tile * groups + head
                first = d_sc[4, code : code + 1, :]
                second = d_sc[5, code : code + 1, :]
                turned = qgt_ref[head, :, tile * tile_rows : (tile + 1) * tile_rows].astype(jnp.float32)
                at = tile * 2 * tile_rows
                x_ref[:head_dim, at : at + tile_rows] = (turned[head_dim:] * first).astype(jnp.bfloat16)
                x_ref[:head_dim, at + tile_rows : at + 2 * tile_rows] = jnp.zeros((head_dim, tile_rows), jnp.bfloat16)
                x_ref[head_dim:, at : at + tile_rows] = (turned[:head_dim] * second).astype(jnp.bfloat16)
                x_ref[head_dim:, at + tile_rows : at + 2 * tile_rows] = (turned[:head_dim] * first).astype(jnp.bfloat16)
            for part in range(tiles_dev):
                grad_ref[head, part * tile_rows : (part + 1) * tile_rows, :] = dot_t(
                    pd_refs[part][head], x_ref[:, part * 2 * tile_rows :]
                )

        def spread(source, carry):
            code = jnp.max(recv_ref[source, tile_rows:, :].astype(jnp.float32)[0:1, :]).astype(jnp.int32) - 1

            @pl.when(code >= 0)
            def _():
                head = lax.rem(code, groups)
                first = w_sc[0, pl.ds(source, 1), :]
                second = w_sc[1, pl.ds(source, 1), :]
                turned = qgt_in_ref[source].astype(jnp.float32)
                top = jnp.concatenate([turned[head_dim:] * first, jnp.zeros((head_dim, tile_rows), jnp.float32)], axis=1)
                low = jnp.concatenate([turned[:head_dim] * second, turned[:head_dim] * first], axis=1)
                factor = jnp.concatenate([top, low], axis=0).astype(jnp.bfloat16)
                grad_ref[head] += dot_t(pd_in_ref[source], factor)

            return carry

        lax.fori_loop(own + 1, devices, spread, 0)

        for head in range(groups):
            cols = slice(head * head_dim, (head + 1) * head_dim)
            dv_ref[:, cols] = grad_ref[head, :, :head_dim].astype(jnp.bfloat16)
            dk_ref[:, cols] = (grad_ref[head, :, head_dim:] * scaling).astype(jnp.bfloat16)
            for tile in range(tiles_dev):
                rows = slice(tile * tile_rows, (tile + 1) * tile_rows)
                turned = acc_ref[tile * groups + head].T
                out_ref[rows, cols] = turned[:, :head_dim].astype(jnp.bfloat16)
                dq_ref[rows, cols] = (turned[:, head_dim:] * scaling).astype(jnp.bfloat16)

    return body


def fast_local(query, key, value, grad_out, picks):
    row_count, columns = query.shape
    tiles_dev, groups, picked = picks.shape
    head_dim = columns // groups
    tile_rows = row_count // tiles_dev
    devices = lax.axis_size("ctx")
    tasks = tiles_dev * groups
    smem = pl.BlockSpec(memory_space=pltpu.SMEM)
    vmem = pl.BlockSpec(memory_space=pltpu.VMEM)
    low = jnp.bfloat16
    wide = jnp.float32
    width = 2 * head_dim
    shape = jax.ShapeDtypeStruct

    send_q, task_of = pl.pallas_call(
        pack_kernel(tiles_dev, groups, picked, tile_rows, head_dim, devices),
        out_shape=(shape((devices, tile_rows + 16, width), low), shape((devices,), jnp.int32)),
        in_specs=[smem, vmem, vmem],
        out_specs=(vmem, smem),
        name="pack",
    )(picks, query, grad_out)
    recv_q = lax.all_to_all(send_q, "ctx", split_axis=0, concat_axis=0, tiled=True)

    own_shapes = (
        shape((groups, row_count, width), low),
        shape((groups, width, row_count), low),
        shape((groups, width, row_count), low),
        shape((tasks, width, tile_rows), wide),
        shape((tasks, head_dim, tile_rows), wide),
        shape((3, tasks, tile_rows), wide),
        shape((tasks, 4 * devices, tile_rows), wide),
    ) + tuple(
        shape((groups, tile_rows, (tiles_dev - part) * 2 * tile_rows), low) for part in range(tiles_dev)
    )
    kv, vkt, qgt, mix, dots, stats, table, *pairs = pl.pallas_call(
        own_kernel(tiles_dev, groups, tile_rows, head_dim, devices),
        out_shape=own_shapes,
        in_specs=[vmem] * 4,
        out_specs=tuple([vmem] * len(own_shapes)),
        name="own",
    )(query, key, value, grad_out)

    slot = 3 * head_dim + 4 * devices
    send_b, pairs_in, inverse_in = pl.pallas_call(
        serve_kernel(groups, tile_rows, head_dim, devices),
        out_shape=(
            shape((devices, slot, tile_rows), low),
            shape((devices, row_count, 2 * tile_rows), low),
            shape((devices, tile_rows), wide),
        ),
        in_specs=[smem, smem, vmem, vmem, vmem, vmem],
        out_specs=(vmem, vmem, vmem),
        scratch_shapes=[pltpu.VMEM((4 * devices, tile_rows), wide)],
        name="serve",
    )(picks, task_of, recv_q, kv, vkt, table)
    recv_b = lax.all_to_all(send_b, "ctx", split_axis=0, concat_axis=0, tiled=True)

    qgt_in = pl.pallas_call(
        flip_kernel(devices, tile_rows),
        out_shape=shape((devices, width, tile_rows), low),
        in_specs=[vmem],
        out_specs=vmem,
        name="flip",
    )(recv_q)

    return pl.pallas_call(
        final_kernel(tiles_dev, groups, picked, tile_rows, head_dim, devices),
        out_shape=tuple([shape((row_count, columns), low)] * 4),
        in_specs=[smem, smem] + [vmem] * (9 + tiles_dev),
        out_specs=tuple([vmem] * 4),
        scratch_shapes=[
            pltpu.VMEM((tasks, width, tile_rows), wide),
            pltpu.VMEM((groups, row_count, width), wide),
            pltpu.VMEM((devices, devices, tile_rows), wide),
            pltpu.VMEM((devices, devices, tile_rows), wide),
            pltpu.VMEM((2, devices, tile_rows), wide),
            pltpu.VMEM((7, tasks, tile_rows), wide),
            pltpu.VMEM((width, 2 * row_count), low),
        ],
        name="final",
    )(picks, task_of, recv_q, recv_b, qgt, qgt_in, mix, dots, stats, inverse_in, pairs_in, *pairs)


def choose(query, key, value, grad_out, picks):
    pair_bytes = lax.axis_size("ctx") * query.shape[0] * (query.shape[0] // picks.shape[0]) * 4
    plan = fast_local if pair_bytes <= pair_budget else local
    return plan(query, key, value, grad_out, picks)


def solution(mesh):
    placed = (
        P("ctx", "head"),
        P("ctx", "head"),
        P("ctx", "head"),
        P("ctx", "head"),
        P("ctx", "head", None),
    )
    return jax.shard_map(
        choose,
        mesh=mesh,
        in_specs=placed,
        out_specs=(P("ctx", "head"), P("ctx", "head"), P("ctx", "head"), P("ctx", "head")),
        check_vma=False,
    )
```

```python
import math

import jax
import jax.numpy as jnp
from jax import lax
from jax.experimental import pallas as pl
from jax.experimental.pallas import tpu as pltpu
from jax.sharding import PartitionSpec as P

masked_value = -1e30
highest = lax.Precision.HIGHEST
LOG2E = math.log2(math.e)
pair_budget = 8 << 20
vmem_grant = 57 << 20
vmem_whole = 65400 << 10


def attend_slots(q_slots, head_ids, k_heads, v_heads, scaling):
    key_rows = jnp.take(k_heads, head_ids, axis=0)
    value_rows = jnp.take(v_heads, head_ids, axis=0)
    scores = (
        jnp.einsum("ndq,nkd->nqk", q_slots, key_rows, preferred_element_type=jnp.float32) * scaling
    )
    peak_score = jnp.max(scores, axis=-1, keepdims=True)
    log_total = peak_score + jnp.log(jnp.sum(jnp.exp(scores - peak_score), axis=-1, keepdims=True))
    attend_low = jnp.exp(scores - log_total).astype(jnp.bfloat16)
    outputs = jnp.einsum("nqk,nkd->ndq", attend_low, value_rows, preferred_element_type=jnp.float32)
    return (outputs, log_total[..., 0])


def slot_grads(q_slots, g_slots, c_slots, lse_slots, head_ids, k_heads, v_heads, scaling):
    key_rows = jnp.take(k_heads, head_ids, axis=0)
    value_rows = jnp.take(v_heads, head_ids, axis=0)
    scores = (
        jnp.einsum("ndq,nkd->nqk", q_slots, key_rows, preferred_element_type=jnp.float32) * scaling
    )
    attend = jnp.exp(scores - lse_slots[..., None])
    attend_low = attend.astype(jnp.bfloat16)
    grad_v = jnp.einsum("nqk,ndq->nkd", attend_low, g_slots, preferred_element_type=jnp.float32)
    grad_prob = jnp.einsum("ndq,nkd->nqk", g_slots, value_rows, preferred_element_type=jnp.float32)
    dscore = (attend * (grad_prob - c_slots[..., None])).astype(jnp.bfloat16)
    grad_k = (
        jnp.einsum("nqk,ndq->nkd", dscore, q_slots, preferred_element_type=jnp.float32) * scaling
    )
    grad_q = (
        jnp.einsum("nqk,nkd->ndq", dscore, key_rows, preferred_element_type=jnp.float32) * scaling
    )
    return (grad_k, grad_v, grad_q)


def local(query, key, value, grad_out, picks):
    row_count, columns = query.shape
    tiles_dev, groups, picked = picks.shape
    head_dim = columns // groups
    tile_rows = row_count // tiles_dev
    others = picked - 1
    scaling = 1.0 / math.sqrt(head_dim)
    devices = lax.axis_size("ctx")
    own_block = lax.axis_index("ctx")
    per_group = min(8, devices)
    all_picks = lax.all_gather(picks, "ctx", axis=0, tiled=True)
    q_heads = query.reshape(row_count, groups, head_dim).transpose(1, 0, 2)
    k_heads = key.reshape(row_count, groups, head_dim).transpose(1, 0, 2)
    v_heads = value.reshape(row_count, groups, head_dim).transpose(1, 0, 2)
    q_tiles = query.reshape(tiles_dev, tile_rows, groups, head_dim)
    do_tiles = grad_out.reshape(tiles_dev, tile_rows, groups, head_dim)
    do_major = do_tiles.transpose(0, 2, 1, 3)
    positions = jnp.arange(row_count, dtype=jnp.int32)
    tile_masks = []
    for tile_step in range(tiles_dev):
        span = (tile_step + 1) * tile_rows
        query_pos = positions[tile_step * tile_rows : span]
        tile_masks.append(positions[None, :span] <= query_pos[:, None])
    targets = picks[:, :, 1:]
    active = targets != own_block
    lookup = jnp.where(active, targets, own_block).reshape(-1)
    peer_ids = jnp.arange(devices, dtype=jnp.int32)
    routing = ((targets[None] == peer_ids[:, None, None, None]) & active[None]).astype(jnp.float32)
    routing_low = routing.astype(jnp.bfloat16)
    send_q = jnp.einsum(
        "jtgi,tqgd->jdq", routing_low, q_tiles, preferred_element_type=jnp.float32
    ).astype(jnp.bfloat16)
    recv_q = lax.all_to_all(send_q, "ctx", split_axis=0, concat_axis=0, tiled=True)

    def own_forward(inputs):
        q_head, k_head, v_head = inputs
        out_list = []
        lse_list = []
        for tile_step in range(tiles_dev):
            span = (tile_step + 1) * tile_rows
            q_part = q_head[tile_step * tile_rows : span]
            scores = (
                jnp.einsum("qd,kd->qk", q_part, k_head[:span], preferred_element_type=jnp.float32)
                * scaling
            )
            scores = jnp.where(tile_masks[tile_step], scores, masked_value)
            peak_score = jnp.max(scores, axis=-1, keepdims=True)
            log_total = peak_score + jnp.log(
                jnp.sum(jnp.exp(scores - peak_score), axis=-1, keepdims=True)
            )
            attend_low = jnp.exp(scores - log_total).astype(jnp.bfloat16)
            out_list.append(jnp.dot(attend_low, v_head[:span], preferred_element_type=jnp.float32))
            lse_list.append(log_total[:, 0])
        return (jnp.concatenate(out_list, axis=0), jnp.concatenate(lse_list, axis=0))

    own_out, own_lse = lax.map(own_forward, (q_heads, k_heads, v_heads))
    sources = all_picks.reshape(devices, tiles_dev, groups, picked)[..., 1:]
    incoming = (sources == own_block) & (peer_ids[:, None, None, None] != own_block)
    live_in = jnp.any(incoming, axis=(1, 2, 3))
    group_ids = jnp.arange(groups, dtype=jnp.int32)
    head_of = jnp.sum(jnp.where(incoming, group_ids[None, None, :, None], 0), axis=(1, 2, 3))
    ranking = jnp.argsort(jnp.where(live_in, 0, 1) * devices + peer_ids)
    inverse = jnp.argsort(ranking)
    rounds = (jnp.sum(live_in.astype(jnp.int32)) + per_group - 1) // per_group
    heads_sorted = jnp.take(head_of, ranking, axis=0)
    q_sorted = jnp.take(recv_q, ranking, axis=0)

    def forward_turn(turn, totals):
        served_out, served_lse = totals
        offset = turn * per_group
        query_part = lax.dynamic_slice_in_dim(q_sorted, offset, per_group, 0)
        head_part = lax.dynamic_slice_in_dim(heads_sorted, offset, per_group, 0)
        out_part, lse_part = attend_slots(query_part, head_part, k_heads, v_heads, scaling)
        served_out = lax.dynamic_update_slice_in_dim(served_out, out_part, offset, 0)
        served_lse = lax.dynamic_update_slice_in_dim(served_lse, lse_part, offset, 0)
        return (served_out, served_lse)

    start_fwd = (
        jnp.zeros((devices, head_dim, tile_rows), jnp.float32),
        jnp.zeros((devices, tile_rows), jnp.float32),
    )
    served_out, served_lse = lax.fori_loop(0, rounds, forward_turn, start_fwd)
    back_out, back_lse = (
        lax.all_to_all(
            jnp.take(served_out, inverse, axis=0), "ctx", split_axis=0, concat_axis=0, tiled=True
        ),
        lax.all_to_all(
            jnp.take(served_lse, inverse, axis=0), "ctx", split_axis=0, concat_axis=0, tiled=True
        ),
    )
    task_out = jnp.take(back_out, lookup, axis=0).reshape(
        tiles_dev, groups, others, head_dim, tile_rows
    )
    task_lse = jnp.take(back_lse, lookup, axis=0).reshape(tiles_dev, groups, others, tile_rows)
    own_out_t = own_out.reshape(groups, tiles_dev, tile_rows, head_dim).transpose(1, 0, 2, 3)
    own_lse_t = own_lse.reshape(groups, tiles_dev, tile_rows).transpose(1, 0, 2)
    active_rows = active[..., None]
    rem_lse = jnp.where(active_rows, task_lse, masked_value)
    ceiling = jnp.maximum(own_lse_t, jnp.max(rem_lse, axis=2))
    log_total = ceiling + jnp.log(
        jnp.exp(own_lse_t - ceiling) + jnp.sum(jnp.exp(rem_lse - ceiling[:, :, None]), axis=2)
    )
    own_weight = jnp.exp(own_lse_t - log_total)
    rem_weight = jnp.where(active_rows, jnp.exp(rem_lse - log_total[:, :, None]), 0.0)
    mixed = own_weight[..., None] * own_out_t + jnp.einsum(
        "tgiq,tgidq->tgqd", rem_weight, task_out, precision=highest
    )
    out_low = mixed.astype(jnp.bfloat16)
    attn_out = out_low.transpose(0, 2, 1, 3).reshape(row_count, columns)
    row_delta = jnp.sum(do_major.astype(jnp.float32) * out_low.astype(jnp.float32), axis=-1)
    own_scaled = (own_weight[..., None] * do_major.astype(jnp.float32)).astype(jnp.bfloat16)
    own_shift = own_weight * row_delta
    g_heads = own_scaled.transpose(1, 0, 2, 3).reshape(groups, row_count, head_dim)
    c_heads = own_shift.transpose(1, 0, 2).reshape(groups, row_count)

    def own_backward(inputs):
        q_head, k_head, v_head, g_head, c_head, lse_head = inputs
        grad_k = jnp.zeros((row_count, head_dim), jnp.float32)
        grad_v = jnp.zeros((row_count, head_dim), jnp.float32)
        dq_list = []
        for tile_step in range(tiles_dev):
            first = tile_step * tile_rows
            span = (tile_step + 1) * tile_rows
            q_part = q_head[first:span]
            g_part = g_head[first:span]
            k_part = k_head[:span]
            scores = (
                jnp.einsum("qd,kd->qk", q_part, k_part, preferred_element_type=jnp.float32)
                * scaling
            )
            scores = jnp.where(tile_masks[tile_step], scores, masked_value)
            attend = jnp.exp(scores - lse_head[first:span, None])
            attend_low = attend.astype(jnp.bfloat16)
            part_dv = jnp.einsum(
                "qk,qd->kd", attend_low, g_part, preferred_element_type=jnp.float32
            )
            grad_prob = jnp.einsum(
                "qd,kd->qk", g_part, v_head[:span], preferred_element_type=jnp.float32
            )
            dscore = (attend * (grad_prob - c_head[first:span, None])).astype(jnp.bfloat16)
            part_dk = (
                jnp.einsum("qk,qd->kd", dscore, q_part, preferred_element_type=jnp.float32)
                * scaling
            )
            dq_list.append(jnp.dot(dscore, k_part, preferred_element_type=jnp.float32) * scaling)
            padding = ((0, row_count - span), (0, 0))
            grad_k = grad_k + jnp.pad(part_dk, padding)
            grad_v = grad_v + jnp.pad(part_dv, padding)
        return (grad_k, grad_v, jnp.concatenate(dq_list, axis=0))

    own_dk, own_dv, own_dq = lax.map(
        own_backward, (q_heads, k_heads, v_heads, g_heads, c_heads, own_lse)
    )
    rem_shift = rem_weight * row_delta[:, :, None]
    rem_scaled = (rem_weight[..., None] * do_major[:, :, None].astype(jnp.float32)).astype(
        jnp.bfloat16
    )
    send_g = jnp.einsum(
        "jtgi,tgiqd->jdq", routing_low, rem_scaled, preferred_element_type=jnp.float32
    )
    send_c = jnp.einsum("jtgi,tgiq->jq", routing, rem_shift, precision=highest)
    recv_g, recv_c = (
        lax.all_to_all(send_g, "ctx", split_axis=0, concat_axis=0, tiled=True),
        lax.all_to_all(send_c, "ctx", split_axis=0, concat_axis=0, tiled=True),
    )
    g_sorted = jnp.take(recv_g, ranking, axis=0).astype(jnp.bfloat16)
    c_sorted = jnp.take(recv_c, ranking, axis=0)

    def backward_turn(turn, totals):
        grad_k, grad_v, served_dq = totals
        offset = turn * per_group
        query_part = lax.dynamic_slice_in_dim(q_sorted, offset, per_group, 0)
        cot_part = lax.dynamic_slice_in_dim(g_sorted, offset, per_group, 0)
        shift_part = lax.dynamic_slice_in_dim(c_sorted, offset, per_group, 0)
        lse_part = lax.dynamic_slice_in_dim(served_lse, offset, per_group, 0)
        head_part = lax.dynamic_slice_in_dim(heads_sorted, offset, per_group, 0)
        part_dk, part_dv, part_dq = slot_grads(
            query_part, cot_part, shift_part, lse_part, head_part, k_heads, v_heads, scaling
        )
        head_onehot = (head_part[:, None] == group_ids[None, :]).astype(jnp.float32)
        grad_k = grad_k + jnp.einsum("ng,nkd->gkd", head_onehot, part_dk, precision=highest)
        grad_v = grad_v + jnp.einsum("ng,nkd->gkd", head_onehot, part_dv, precision=highest)
        served_dq = lax.dynamic_update_slice_in_dim(served_dq, part_dq, offset, 0)
        return (grad_k, grad_v, served_dq)

    zeros_heads = jnp.zeros((groups, row_count, head_dim), jnp.float32)
    start_bwd = (zeros_heads, zeros_heads, jnp.zeros((devices, head_dim, tile_rows), jnp.float32))
    rem_dk, rem_dv, served_dq = lax.fori_loop(0, rounds, backward_turn, start_bwd)
    back_dq = lax.all_to_all(
        jnp.take(served_dq, inverse, axis=0).astype(jnp.bfloat16),
        "ctx",
        split_axis=0,
        concat_axis=0,
        tiled=True,
    ).astype(jnp.float32)
    task_dq = jnp.take(back_dq, lookup, axis=0).reshape(
        tiles_dev, groups, others, head_dim, tile_rows
    )
    rem_dq = jnp.sum(jnp.where(active[..., None, None], task_dq, 0.0), axis=2)
    own_dq_t = own_dq.reshape(groups, tiles_dev, tile_rows, head_dim).transpose(1, 0, 2, 3)
    total_dq = own_dq_t + rem_dq.transpose(0, 1, 3, 2)
    grad_query = total_dq.transpose(0, 2, 1, 3).reshape(row_count, columns).astype(jnp.bfloat16)
    grad_key = (own_dk + rem_dk).transpose(1, 0, 2).reshape(row_count, columns).astype(jnp.bfloat16)
    grad_value = (
        (own_dv + rem_dv).transpose(1, 0, 2).reshape(row_count, columns).astype(jnp.bfloat16)
    )
    return (attn_out, grad_query, grad_key, grad_value)


def offsets_of(tiles_dev, tile_rows):
    starts = [0]
    for part in range(tiles_dev):
        starts.append(starts[-1] + (tiles_dev - part) * 2 * tile_rows)
    return starts


def dot_t(a, b):
    return lax.dot_general(a, b, (((1,), (1,)), ((), ())), preferred_element_type=jnp.float32)


def split_low(x):
    high = x.astype(jnp.bfloat16).astype(jnp.float32)
    return high, x - high


def halves(block, head_dim):
    lane = lax.broadcasted_iota(jnp.int32, block.shape, 1)
    zero = jnp.zeros_like(block)
    return jnp.where(lane < head_dim, block, zero), jnp.where(lane < head_dim, zero, block)


def pack_kernel(tiles_dev, groups, picked, tile_rows, head_dim, devices):
    def body(picks_ref, q_ref, g_ref, send_ref, task_ref):
        own = picks_ref[0, 0, 0]
        meta_rows = send_ref.shape[1] - tile_rows
        lanes = send_ref.shape[2]
        row = lax.broadcasted_iota(jnp.int32, (meta_rows, lanes), 0)
        blank = jnp.zeros((meta_rows, lanes), jnp.bfloat16)
        for peer in range(devices):
            send_ref[peer, tile_rows:, :] = blank
            task_ref[peer] = -1
        for tile in range(tiles_dev):
            rows = slice(tile * tile_rows, (tile + 1) * tile_rows)
            for head in range(groups):
                cols = slice(head * head_dim, (head + 1) * head_dim)
                block = jnp.concatenate([q_ref[rows, cols], g_ref[rows, cols]], axis=1)
                code = tile * groups + head
                meta = jnp.where(row == 0, code + 1, 0)
                for entry in range(1, picked):
                    meta = jnp.where(row == entry, picks_ref[tile, head, entry], meta)
                meta = meta.astype(jnp.float32).astype(jnp.bfloat16)
                for entry in range(1, picked):
                    target = picks_ref[tile, head, entry]
                    send_ref[target, :tile_rows, :] = block
                    send_ref[target, tile_rows:, :] = meta
                    task_ref[target] = code
        task_ref[own] = -1

    return body


def own_kernel(tiles_dev, groups, tile_rows, head_dim, devices):
    scale = LOG2E / math.sqrt(head_dim)
    starts = offsets_of(tiles_dev, tile_rows)

    def body(q_hbm, k_hbm, v_hbm, g_hbm, kv_ref, vkt_ref, qgt_ref, stat_ref, table_ref, mix_hbm,
             pd_hbm, q_ref, k_ref, v_ref, g_ref, mix_ref, pd_ref, in_sem, out_sem):
        loads = [
            pltpu.make_async_copy(src, dst, in_sem.at[index])
            for index, (src, dst) in enumerate(((k_hbm, k_ref), (v_hbm, v_ref), (q_hbm, q_ref), (g_hbm, g_ref)))
        ]
        for load in loads:
            load.start()
        for load in loads:
            load.wait()
        sub = lax.broadcasted_iota(jnp.int32, (tile_rows, tile_rows), 0)
        lane = lax.broadcasted_iota(jnp.int32, (tile_rows, tile_rows), 1)
        causal = sub <= lane
        stores = []
        for head in range(groups):
            cols = slice(head * head_dim, (head + 1) * head_dim)
            k_head = k_ref[:, cols]
            v_head = v_ref[:, cols]
            kv_ref[head] = jnp.concatenate([k_head, v_head], axis=1)
            vkt_ref[head] = jnp.concatenate([v_head, k_head], axis=1).T
            block_all = jnp.concatenate([q_ref[:, cols], g_ref[:, cols]], axis=1)
            qgt_ref[head] = block_all.T
            for tile in range(tiles_dev):
                rows = slice(tile * tile_rows, (tile + 1) * tile_rows)
                span = (tile + 1) * tile_rows
                code = tile * groups + head
                q_half, g_half = halves(block_all[rows], head_dim)
                scores = dot_t(kv_ref[head, :span, :], q_half)
                last = jnp.where(causal, scores[span - tile_rows :], masked_value)
                peak = jnp.max(last, axis=0, keepdims=True)
                if tile:
                    peak = jnp.maximum(peak, jnp.max(scores[: span - tile_rows], axis=0, keepdims=True))
                peak = peak * scale
                total = jnp.zeros((1, tile_rows), jnp.float32)
                mean_grad = jnp.zeros((1, tile_rows), jnp.float32)
                for part in range(tile + 1):
                    chunk = slice(part * tile_rows, (part + 1) * tile_rows)
                    piece = last if part == tile else scores[chunk]
                    powers = jnp.exp2(piece * scale - peak)
                    spread = powers * dot_t(kv_ref[head, chunk, :], g_half)
                    total = total + jnp.sum(powers, axis=0, keepdims=True)
                    mean_grad = mean_grad + jnp.sum(spread, axis=0, keepdims=True)
                    at = starts[part] + (tile - part) * 2 * tile_rows
                    pd_ref[head, :, at : at + tile_rows] = powers.astype(jnp.bfloat16)
                    pd_ref[head, :, at + tile_rows : at + 2 * tile_rows] = spread.astype(jnp.bfloat16)
                inverse = 1.0 / total
                mean_grad = mean_grad * inverse
                lse = peak + jnp.log2(total)
                top = jnp.zeros((2 * head_dim, tile_rows), jnp.float32)
                low = jnp.zeros((head_dim, tile_rows), jnp.float32)
                for part in range(tile + 1):
                    chunk = slice(part * tile_rows, (part + 1) * tile_rows)
                    at = starts[part] + (tile - part) * 2 * tile_rows
                    top = top + jnp.dot(vkt_ref[head, :, chunk], pd_ref[head, :, at : at + tile_rows],
                                        preferred_element_type=jnp.float32)
                    low = low + jnp.dot(vkt_ref[head, head_dim:, chunk], pd_ref[head, :, at + tile_rows : at + 2 * tile_rows],
                                        preferred_element_type=jnp.float32)
                mix_ref[head, tile, : 2 * head_dim, :] = (top * inverse).astype(jnp.bfloat16)
                mix_ref[head, tile, 2 * head_dim :, :] = (low * inverse).astype(jnp.bfloat16)
                stat_ref[0, code : code + 1, :] = lse
                stat_ref[1, code : code + 1, :] = mean_grad
                stat_ref[2, code : code + 1, :] = inverse
                parts = split_low(lse) + split_low(mean_grad)
                table_ref[code] = jnp.concatenate(
                    [jnp.broadcast_to(p, (devices, tile_rows)) for p in parts], axis=0
                )
            stores.append(pltpu.make_async_copy(pd_ref.at[head], pd_hbm.at[head], out_sem.at[0, head]))
            stores.append(pltpu.make_async_copy(mix_ref.at[head], mix_hbm.at[head], out_sem.at[1, head]))
            stores[-2].start()
            stores[-1].start()
        for store in stores:
            store.wait()

    return body


def parts_of(block, kv_head, tile_rows, head_dim, scale):
    both = dot_t(kv_head, jnp.concatenate(halves(block, head_dim), axis=0))
    scores = both[:, :tile_rows]
    peak = jnp.max(scores, axis=0, keepdims=True) * scale
    powers = jnp.exp2(scores * scale - peak)
    spread = powers * both[:, tile_rows:]
    return peak, powers, spread


def serve_kernel(groups, tile_rows, head_dim, devices):
    scale = LOG2E / math.sqrt(head_dim)

    def body(picks_ref, task_ref, recv_hbm, kv_hbm, vkt_hbm, table_hbm, send_hbm, inv_hbm,
             send_ref, inv_ref, st_ref, recv_ref, kv_ref, vkt_ref, table_ref, in_sem, out_sem):
        own = picks_ref[0, 0, 0]
        loads = [
            pltpu.make_async_copy(src, dst, in_sem.at[index])
            for index, (src, dst) in enumerate(
                ((recv_hbm, recv_ref), (kv_hbm, kv_ref), (vkt_hbm, vkt_ref), (table_hbm, table_ref))
            )
        ]
        for load in loads:
            load.start()
        st_ref[...] = jnp.zeros_like(st_ref)
        inv_ref[...] = jnp.zeros_like(inv_ref)
        for load in loads:
            load.wait()
        heads = [None]
        blocks = [None]
        for source in range(1, devices):
            code = jnp.max(recv_ref[source, tile_rows:, :].astype(jnp.float32)[0:1, :]).astype(jnp.int32) - 1
            block = recv_ref[source, :tile_rows, :]
            heads.append(lax.rem(jnp.maximum(code, 0), groups))
            blocks.append(jnp.where((code >= 0) & (own != source), block, jnp.zeros_like(block)))
        ahead = parts_of(blocks[1], kv_ref[heads[1]], tile_rows, head_dim, scale)
        for source in range(1, devices):
            peak, powers, spread = ahead
            if source + 1 < devices:
                ahead = parts_of(blocks[source + 1], kv_ref[heads[source + 1]], tile_rows, head_dim, scale)
            total = jnp.sum(powers, axis=0, keepdims=True)
            inverse = 1.0 / total
            mean_grad = jnp.sum(spread, axis=0, keepdims=True) * inverse
            both = jnp.concatenate([powers.astype(jnp.bfloat16), spread.astype(jnp.bfloat16)], axis=1)
            result = jnp.dot(vkt_ref[heads[source]], both, preferred_element_type=jnp.float32)
            send_ref[source, : 2 * head_dim, :] = (result[:, :tile_rows] * inverse).astype(jnp.bfloat16)
            send_ref[source, 2 * head_dim : 3 * head_dim, :] = (result[head_dim:, tile_rows:] * inverse).astype(jnp.bfloat16)
            parts = split_low(peak + jnp.log2(total)) + split_low(mean_grad)
            for index in range(4):
                st_ref[index * devices + source : index * devices + source + 1, :] = parts[index]
            inv_ref[source : source + 1, :] = inverse
        table = st_ref[...]
        row = lax.broadcasted_iota(jnp.int32, table.shape, 0)
        mine = lax.rem(row, devices) == own
        for peer in range(devices):
            code = jnp.maximum(task_ref[peer], 0)
            send_ref[peer, 3 * head_dim :, :] = jnp.where(mine, table_ref[code], table).astype(jnp.bfloat16)
        stores = [
            pltpu.make_async_copy(send_ref, send_hbm, out_sem.at[0]),
            pltpu.make_async_copy(inv_ref, inv_hbm, out_sem.at[1]),
        ]
        for store in stores:
            store.start()
        for store in stores:
            store.wait()

    return body


def again_kernel(groups, tile_rows, head_dim, devices):
    scale = LOG2E / math.sqrt(head_dim)

    def body(picks_ref, recv_ref, kv_ref, pd_ref, qgt_ref):
        own = picks_ref[0, 0, 0]

        def turn(source, carry):
            code = jnp.max(recv_ref[source, tile_rows:, :].astype(jnp.float32)[0:1, :]).astype(jnp.int32) - 1
            block = recv_ref[source, :tile_rows, :]
            block = jnp.where((code >= 0) & (own != source), block, jnp.zeros_like(block))
            head = lax.rem(jnp.maximum(code, 0), groups)
            _, powers, spread = parts_of(block, kv_ref[head], tile_rows, head_dim, scale)
            pd_ref[source, :, :tile_rows] = powers.astype(jnp.bfloat16)
            pd_ref[source, :, tile_rows:] = spread.astype(jnp.bfloat16)
            qgt_ref[source] = block.T
            return carry

        lax.fori_loop(1, devices, turn, 0)

    return body


def final_kernel(tiles_dev, groups, picked, tile_rows, head_dim, devices):
    scaling = 1.0 / math.sqrt(head_dim)
    starts = offsets_of(tiles_dev, tile_rows)
    pair = 2 * tile_rows

    def body(picks_ref, task_ref, recv_hbm, back_hbm, qgt_hbm, qgt_in_hbm, stat_hbm, inv_hbm,
             mix_hbm, pd_in_hbm, pd_hbm, out_hbm, dq_hbm, dk_hbm, dv_hbm,
             meta_ref, back_ref, qgt_ref, qgt_in_ref, stat_ref, inv_ref,
             mix_ref, pd_in_ref, pd_ref, out_ref, dq_ref, dk_ref, dv_ref, acc_ref, grad_ref, more_ref,
             lse_sc, gd_sc, w_sc, d_sc, x_ref, xin_ref, load_sem, pd_sem, in_sem, out_sem):
        own = picks_ref[0, 0, 0]
        tasks = tiles_dev * groups
        base = 3 * head_dim
        loads = [
            pltpu.make_async_copy(src, dst, load_sem.at[index])
            for index, (src, dst) in enumerate(
                (
                    (back_hbm, back_ref),
                    (recv_hbm.at[:, tile_rows : tile_rows + 16, :], meta_ref),
                    (stat_hbm, stat_ref),
                    (inv_hbm, inv_ref),
                    (mix_hbm, mix_ref),
                    (qgt_hbm, qgt_ref),
                    (qgt_in_hbm, qgt_in_ref),
                )
            )
        ]
        owns = [
            [
                pltpu.make_async_copy(
                    pd_hbm.at[head, :, starts[part] : starts[part + 1]],
                    pd_ref.at[head, part * tile_rows : (part + 1) * tile_rows, part * pair :],
                    pd_sem.at[head, part],
                )
                for part in range(tiles_dev)
            ]
            for head in range(groups)
        ]
        ins = [None] + [
            pltpu.make_async_copy(pd_in_hbm.at[s], pd_in_ref.at[s], in_sem.at[s]) for s in range(1, devices)
        ]
        for copy in loads + [copy for row in owns for copy in row] + ins[1:]:
            copy.start()
        more_ref[...] = jnp.zeros_like(more_ref)
        for head in range(groups):
            for part in range(1, tiles_dev, 2):
                pd_ref[head, part * tile_rows : (part + 1) * tile_rows, (part - 1) * pair : part * pair] = jnp.zeros(
                    (tile_rows, pair), jnp.bfloat16
                )
        for load in loads[:4]:
            load.wait()

        lse_of = []
        gd_of = []
        for peer in range(devices):
            table = back_ref[peer, base : base + 4 * devices, :].astype(jnp.float32)
            lse_of.append(table[:devices] + table[devices : 2 * devices])
            gd_of.append(table[2 * devices : 3 * devices] + table[3 * devices :])
            lse_sc[peer] = lse_of[peer]
            gd_sc[peer] = gd_of[peer]

        ids = lax.broadcasted_iota(jnp.int32, (devices, tile_rows), 0)
        metas = [meta_ref[source].astype(jnp.float32) for source in range(devices)]
        rows_of = [
            jnp.concatenate([metas[source][entry : entry + 1] for source in range(devices)], axis=0).astype(jnp.int32)
            for entry in range(picked)
        ]
        codes = [None] + [jnp.max(metas[source][0:1, :]).astype(jnp.int32) - 1 for source in range(1, devices)]
        live = (rows_of[0] > 0) & (ids != own)
        chosen = []
        for peer in range(devices):
            active = ids == peer
            for entry in rows_of[1:]:
                active = active | (entry == peer)
            chosen.append(active)
        peak = jnp.full((devices, tile_rows), masked_value, jnp.float32)
        for peer in range(devices):
            peak = jnp.maximum(peak, jnp.where(chosen[peer], lse_of[peer], masked_value))
        total = jnp.zeros_like(peak)
        delta = jnp.zeros_like(peak)
        for peer in range(devices):
            power = jnp.where(chosen[peer], jnp.exp2(lse_of[peer] - peak), 0.0)
            total = total + power
            delta = delta + jnp.where(chosen[peer], power * gd_of[peer], 0.0)
        delta = delta / total
        weight = jnp.exp2(lse_sc[own] - peak) / total * inv_ref[...]
        w_sc[0] = jnp.where(live, weight, 0.0)
        w_sc[1] = jnp.where(live, -weight * delta, 0.0)

        code_ids = lax.broadcasted_iota(jnp.int32, (tasks, tile_rows), 0)
        own_lse = stat_ref[0]
        own_gd = stat_ref[1]
        peak = own_lse
        rows_lse = [lse_sc[peer, pl.ds(own, 1), :] for peer in range(devices)]
        rows_gd = [gd_sc[peer, pl.ds(own, 1), :] for peer in range(devices)]
        for peer in range(devices):
            peak = jnp.maximum(peak, jnp.where(code_ids == task_ref[peer], rows_lse[peer], masked_value))
        own_power = jnp.exp2(own_lse - peak)
        total = own_power
        delta = own_power * own_gd
        for peer in range(devices):
            here = code_ids == task_ref[peer]
            power = jnp.where(here, jnp.exp2(rows_lse[peer] - peak), 0.0)
            total = total + power
            delta = delta + jnp.where(here, power * rows_gd[peer], 0.0)
        inverse = 1.0 / total
        delta = delta * inverse
        own_weight = own_power * inverse
        d_sc[0] = peak
        d_sc[1] = inverse
        d_sc[2] = delta
        d_sc[3] = own_weight
        d_sc[4] = own_weight * stat_ref[2]
        d_sc[5] = -own_weight * stat_ref[2] * delta
        d_sc[6] = -own_weight * delta

        loads[4].wait()
        for head in range(groups):
            for tile in range(tiles_dev):
                code = tile * groups + head
                first = d_sc[3, code : code + 1, :]
                second = d_sc[6, code : code + 1, :]
                mix = mix_ref[head, tile].astype(jnp.float32)
                acc_ref[0, code] = mix[:head_dim] * first
                acc_ref[1, code] = mix[2 * head_dim :] * first + mix[head_dim : 2 * head_dim] * second

        def gather(peer, carry):
            code = task_ref[peer]

            @pl.when(code >= 0)
            def _():
                at = pl.ds(code, 1)
                part_w = jnp.exp2(lse_sc[peer, pl.ds(own, 1), :] - d_sc[0, at, :]) * d_sc[1, at, :]
                shift = -part_w * d_sc[2, at, :]
                mix = back_ref[peer, : 3 * head_dim, :].astype(jnp.float32)
                acc_ref[0, code] += mix[:head_dim] * part_w
                acc_ref[1, code] += mix[2 * head_dim :] * part_w + mix[head_dim : 2 * head_dim] * shift

            return carry

        lax.fori_loop(0, own, gather, 0)

        sub = lax.broadcasted_iota(jnp.int32, (tile_rows, tile_rows), 0)
        lane = lax.broadcasted_iota(jnp.int32, (tile_rows, tile_rows), 1)
        unit = jnp.where(sub == lane, 1.0, 0.0).astype(jnp.bfloat16)
        for tile in range(tiles_dev):
            rows = slice(tile * tile_rows, (tile + 1) * tile_rows)
            for head in range(0, groups, 2):
                cols = slice(head * head_dim, (head + 2) * head_dim)
                code = tile * groups + head
                both = jnp.concatenate([acc_ref[0, code], acc_ref[0, code + 1]], axis=0).astype(jnp.bfloat16)
                out_ref[rows, cols] = dot_t(unit, both).astype(jnp.bfloat16)
                both = jnp.concatenate([acc_ref[1, code], acc_ref[1, code + 1]], axis=0)
                dq_ref[rows, cols] = dot_t(unit, (both * scaling).astype(jnp.bfloat16)).astype(jnp.bfloat16)
        stores = [
            pltpu.make_async_copy(src, dst, out_sem.at[index])
            for index, (src, dst) in enumerate(((out_ref, out_hbm), (dq_ref, dq_hbm), (dk_ref, dk_hbm), (dv_ref, dv_hbm)))
        ]
        stores[0].start()
        stores[1].start()

        for copy in loads[5:] + [copy for row in owns for copy in row] + ins[1:]:
            copy.wait()
        nothing = jnp.zeros((head_dim, tile_rows), jnp.bfloat16)
        for head in range(groups):
            v_rows = slice(0, head_dim) if head % 2 == 0 else slice(head_dim, 2 * head_dim)
            k_rows = slice(head_dim, 2 * head_dim) if head % 2 == 0 else slice(0, head_dim)
            for tile in range(tiles_dev):
                code = tile * groups + head
                first = d_sc[4, code : code + 1, :]
                second = d_sc[5, code : code + 1, :]
                turned = qgt_ref[head, :, tile * tile_rows : (tile + 1) * tile_rows].astype(jnp.float32)
                early = slice(tile * pair, tile * pair + tile_rows)
                late = slice(tile * pair + tile_rows, (tile + 1) * pair)
                x_ref[head, v_rows, early] = (turned[head_dim:] * first).astype(jnp.bfloat16)
                x_ref[head, v_rows, late] = nothing
                x_ref[head, k_rows, early] = (turned[:head_dim] * second).astype(jnp.bfloat16)
                x_ref[head, k_rows, late] = (turned[:head_dim] * first).astype(jnp.bfloat16)
        for source in range(1, devices):
            odd = lax.rem(jnp.maximum(codes[source], 0), 2) == 1
            first = w_sc[0, source : source + 1, :]
            second = w_sc[1, source : source + 1, :]
            turned = qgt_in_ref[source].astype(jnp.float32)
            g_first = (turned[head_dim:] * first).astype(jnp.bfloat16)
            q_first = (turned[:head_dim] * first).astype(jnp.bfloat16)
            q_second = (turned[:head_dim] * second).astype(jnp.bfloat16)
            xin_ref[source, :head_dim, :tile_rows] = jnp.where(odd, q_second, g_first)
            xin_ref[source, :head_dim, tile_rows:] = jnp.where(odd, q_first, nothing)
            xin_ref[source, head_dim:, :tile_rows] = jnp.where(odd, g_first, q_second)
            xin_ref[source, head_dim:, tile_rows:] = jnp.where(odd, nothing, q_first)
        for head in range(groups):
            for first in range(0, tiles_dev, 2):
                rows = slice(first * tile_rows, (first + 2) * tile_rows)
                grad_ref[head, rows, :] = dot_t(pd_ref[head, rows, first * pair :], x_ref[head, :, first * pair :])
        for source in range(1, devices):
            head = lax.rem(jnp.maximum(codes[source], 0), groups)
            target = grad_ref if source % 2 else more_ref
            target[head] += dot_t(pd_in_ref[source], xin_ref[source])
        lane = lax.broadcasted_iota(jnp.int32, (tile_rows, 2 * head_dim), 1)
        for head in range(0, groups, 2):
            cols = slice(head * head_dim, (head + 2) * head_dim)
            for part in range(tiles_dev):
                rows = slice(part * tile_rows, (part + 1) * tile_rows)
                even = grad_ref[head, rows, :] + more_ref[head, rows, :]
                odd = grad_ref[head + 1, rows, :] + more_ref[head + 1, rows, :]
                dv_ref[rows, cols] = jnp.where(lane < head_dim, even, odd).astype(jnp.bfloat16)
                swapped = jnp.where(lane < head_dim, odd, even) * scaling
                dk_ref[rows, cols] = pltpu.roll(swapped, head_dim, 1).astype(jnp.bfloat16)
        stores[2].start()
        stores[3].start()
        for store in stores:
            store.wait()

    return body


def fast_local(query, key, value, grad_out, picks):
    row_count, columns = query.shape
    tiles_dev, groups, picked = picks.shape
    head_dim = columns // groups
    tile_rows = row_count // tiles_dev
    devices = lax.axis_size("ctx")
    tasks = tiles_dev * groups
    smem = pl.BlockSpec(memory_space=pltpu.SMEM)
    vmem = pl.BlockSpec(memory_space=pltpu.VMEM)
    far = pl.BlockSpec(memory_space=pltpu.HBM)
    low = jnp.bfloat16
    wide = jnp.float32
    width = 2 * head_dim
    shape = jax.ShapeDtypeStruct
    dma = pltpu.SemaphoreType.DMA
    small = pltpu.CompilerParams(vmem_limit_bytes=vmem_grant)
    large = pltpu.CompilerParams(vmem_limit_bytes=vmem_whole)
    pair_cols = offsets_of(tiles_dev, tile_rows)[-1]

    send_q, task_of = pl.pallas_call(
        pack_kernel(tiles_dev, groups, picked, tile_rows, head_dim, devices),
        out_shape=(shape((devices, tile_rows + 16, width), low), shape((devices,), jnp.int32)),
        in_specs=[smem, vmem, vmem],
        out_specs=(vmem, smem),
        name="pack",
    )(picks, query, grad_out)
    recv_q = lax.all_to_all(send_q, "ctx", split_axis=0, concat_axis=0, tiled=True)

    mix_shape = (groups, tiles_dev, 3 * head_dim, tile_rows)
    pair_shape = (groups, tile_rows, pair_cols)
    kv, vkt, qgt, stats, table, mix, pairs = pl.pallas_call(
        own_kernel(tiles_dev, groups, tile_rows, head_dim, devices),
        out_shape=(
            shape((groups, row_count, width), low),
            shape((groups, width, row_count), low),
            shape((groups, width, row_count), low),
            shape((3, tasks, tile_rows), wide),
            shape((tasks, 4 * devices, tile_rows), wide),
            shape(mix_shape, low),
            shape(pair_shape, low),
        ),
        in_specs=[far] * 4,
        out_specs=(vmem, vmem, vmem, vmem, vmem, far, far),
        scratch_shapes=[pltpu.VMEM((row_count, columns), low)] * 4
        + [pltpu.VMEM(mix_shape, low), pltpu.VMEM(pair_shape, low), dma((4,)), dma((2, groups))],
        compiler_params=large,
        name="own",
    )(query, key, value, grad_out)

    slot = 3 * head_dim + 4 * devices
    in_shape = (devices, row_count, 2 * tile_rows)
    send_b, inverse_in = pl.pallas_call(
        serve_kernel(groups, tile_rows, head_dim, devices),
        out_shape=(shape((devices, slot, tile_rows), low), shape((devices, tile_rows), wide)),
        in_specs=[smem, smem, far, far, far, far],
        out_specs=(far, far),
        scratch_shapes=[
            pltpu.VMEM((devices, slot, tile_rows), low),
            pltpu.VMEM((devices, tile_rows), wide),
            pltpu.VMEM((4 * devices, tile_rows), wide),
            pltpu.VMEM(send_q.shape, low),
            pltpu.VMEM(kv.shape, low),
            pltpu.VMEM(vkt.shape, low),
            pltpu.VMEM(table.shape, wide),
            dma((4,)),
            dma((2,)),
        ],
        compiler_params=small,
        name="serve",
    )(picks, task_of, recv_q, kv, vkt, table)
    recv_b = lax.all_to_all(send_b, "ctx", split_axis=0, concat_axis=0, tiled=True)

    pairs_in, qgt_in = pl.pallas_call(
        again_kernel(groups, tile_rows, head_dim, devices),
        out_shape=(shape(in_shape, low), shape((devices, width, tile_rows), low)),
        in_specs=[smem, vmem, vmem],
        out_specs=(vmem, vmem),
        compiler_params=large,
        name="again",
    )(picks, recv_q, kv)

    square = (groups, row_count, 2 * row_count)
    return pl.pallas_call(
        final_kernel(tiles_dev, groups, picked, tile_rows, head_dim, devices),
        out_shape=tuple([shape((row_count, columns), low)] * 4),
        in_specs=[smem, smem] + [far] * 9,
        out_specs=tuple([far] * 4),
        scratch_shapes=[
            pltpu.VMEM((devices, 16, width), low),
            pltpu.VMEM((devices, slot, tile_rows), low),
            pltpu.VMEM(qgt.shape, low),
            pltpu.VMEM(qgt_in.shape, low),
            pltpu.VMEM(stats.shape, wide),
            pltpu.VMEM(inverse_in.shape, wide),
            pltpu.VMEM(mix_shape, low),
            pltpu.VMEM(in_shape, low),
            pltpu.VMEM(square, low),
        ]
        + [pltpu.VMEM((row_count, columns), low)] * 4
        + [
            pltpu.VMEM((2, tasks, head_dim, tile_rows), wide),
            pltpu.VMEM((groups, row_count, width), wide),
            pltpu.VMEM((groups, row_count, width), wide),
            pltpu.VMEM((devices, devices, tile_rows), wide),
            pltpu.VMEM((devices, devices, tile_rows), wide),
            pltpu.VMEM((2, devices, tile_rows), wide),
            pltpu.VMEM((7, tasks, tile_rows), wide),
            pltpu.VMEM((groups, width, 2 * row_count), low),
            pltpu.VMEM((devices, width, 2 * tile_rows), low),
            dma((7,)),
            dma((groups, tiles_dev)),
            dma((devices,)),
            dma((4,)),
        ],
        compiler_params=small,
        name="final",
    )(picks, task_of, recv_q, recv_b, qgt, qgt_in, stats, inverse_in, mix, pairs_in, pairs)


def choose(query, key, value, grad_out, picks):
    pair_bytes = lax.axis_size("ctx") * query.shape[0] * (query.shape[0] // picks.shape[0]) * 4
    plan = fast_local if pair_bytes <= pair_budget else local
    return plan(query, key, value, grad_out, picks)


def solution(mesh):
    placed = (
        P("ctx", "head"),
        P("ctx", "head"),
        P("ctx", "head"),
        P("ctx", "head"),
        P("ctx", "head", None),
    )
    return jax.shard_map(
        choose,
        mesh=mesh,
        in_specs=placed,
        out_specs=(P("ctx", "head"), P("ctx", "head"), P("ctx", "head"), P("ctx", "head")),
        check_vma=False,
    )
```

```python
import math

import jax
import jax.numpy as jnp
from jax import lax
from jax.experimental import pallas as pl
from jax.experimental.pallas import tpu as pltpu
from jax.sharding import PartitionSpec as P

masked_value = -1e30
highest = lax.Precision.HIGHEST
LOG2E = math.log2(math.e)
pair_budget = 8 << 20
vmem_grant = 32 << 20


def attend_slots(q_slots, head_ids, k_heads, v_heads, scaling):
    key_rows = jnp.take(k_heads, head_ids, axis=0)
    value_rows = jnp.take(v_heads, head_ids, axis=0)
    scores = (
        jnp.einsum("ndq,nkd->nqk", q_slots, key_rows, preferred_element_type=jnp.float32) * scaling
    )
    peak_score = jnp.max(scores, axis=-1, keepdims=True)
    log_total = peak_score + jnp.log(jnp.sum(jnp.exp(scores - peak_score), axis=-1, keepdims=True))
    attend_low = jnp.exp(scores - log_total).astype(jnp.bfloat16)
    outputs = jnp.einsum("nqk,nkd->ndq", attend_low, value_rows, preferred_element_type=jnp.float32)
    return (outputs, log_total[..., 0])


def slot_grads(q_slots, g_slots, c_slots, lse_slots, head_ids, k_heads, v_heads, scaling):
    key_rows = jnp.take(k_heads, head_ids, axis=0)
    value_rows = jnp.take(v_heads, head_ids, axis=0)
    scores = (
        jnp.einsum("ndq,nkd->nqk", q_slots, key_rows, preferred_element_type=jnp.float32) * scaling
    )
    attend = jnp.exp(scores - lse_slots[..., None])
    attend_low = attend.astype(jnp.bfloat16)
    grad_v = jnp.einsum("nqk,ndq->nkd", attend_low, g_slots, preferred_element_type=jnp.float32)
    grad_prob = jnp.einsum("ndq,nkd->nqk", g_slots, value_rows, preferred_element_type=jnp.float32)
    dscore = (attend * (grad_prob - c_slots[..., None])).astype(jnp.bfloat16)
    grad_k = (
        jnp.einsum("nqk,ndq->nkd", dscore, q_slots, preferred_element_type=jnp.float32) * scaling
    )
    grad_q = (
        jnp.einsum("nqk,nkd->ndq", dscore, key_rows, preferred_element_type=jnp.float32) * scaling
    )
    return (grad_k, grad_v, grad_q)


def local(query, key, value, grad_out, picks):
    row_count, columns = query.shape
    tiles_dev, groups, picked = picks.shape
    head_dim = columns // groups
    tile_rows = row_count // tiles_dev
    others = picked - 1
    scaling = 1.0 / math.sqrt(head_dim)
    devices = lax.axis_size("ctx")
    own_block = lax.axis_index("ctx")
    per_group = min(8, devices)
    all_picks = lax.all_gather(picks, "ctx", axis=0, tiled=True)
    q_heads = query.reshape(row_count, groups, head_dim).transpose(1, 0, 2)
    k_heads = key.reshape(row_count, groups, head_dim).transpose(1, 0, 2)
    v_heads = value.reshape(row_count, groups, head_dim).transpose(1, 0, 2)
    q_tiles = query.reshape(tiles_dev, tile_rows, groups, head_dim)
    do_tiles = grad_out.reshape(tiles_dev, tile_rows, groups, head_dim)
    do_major = do_tiles.transpose(0, 2, 1, 3)
    positions = jnp.arange(row_count, dtype=jnp.int32)
    tile_masks = []
    for tile_step in range(tiles_dev):
        span = (tile_step + 1) * tile_rows
        query_pos = positions[tile_step * tile_rows : span]
        tile_masks.append(positions[None, :span] <= query_pos[:, None])
    targets = picks[:, :, 1:]
    active = targets != own_block
    lookup = jnp.where(active, targets, own_block).reshape(-1)
    peer_ids = jnp.arange(devices, dtype=jnp.int32)
    routing = ((targets[None] == peer_ids[:, None, None, None]) & active[None]).astype(jnp.float32)
    routing_low = routing.astype(jnp.bfloat16)
    send_q = jnp.einsum(
        "jtgi,tqgd->jdq", routing_low, q_tiles, preferred_element_type=jnp.float32
    ).astype(jnp.bfloat16)
    recv_q = lax.all_to_all(send_q, "ctx", split_axis=0, concat_axis=0, tiled=True)

    def own_forward(inputs):
        q_head, k_head, v_head = inputs
        out_list = []
        lse_list = []
        for tile_step in range(tiles_dev):
            span = (tile_step + 1) * tile_rows
            q_part = q_head[tile_step * tile_rows : span]
            scores = (
                jnp.einsum("qd,kd->qk", q_part, k_head[:span], preferred_element_type=jnp.float32)
                * scaling
            )
            scores = jnp.where(tile_masks[tile_step], scores, masked_value)
            peak_score = jnp.max(scores, axis=-1, keepdims=True)
            log_total = peak_score + jnp.log(
                jnp.sum(jnp.exp(scores - peak_score), axis=-1, keepdims=True)
            )
            attend_low = jnp.exp(scores - log_total).astype(jnp.bfloat16)
            out_list.append(jnp.dot(attend_low, v_head[:span], preferred_element_type=jnp.float32))
            lse_list.append(log_total[:, 0])
        return (jnp.concatenate(out_list, axis=0), jnp.concatenate(lse_list, axis=0))

    own_out, own_lse = lax.map(own_forward, (q_heads, k_heads, v_heads))
    sources = all_picks.reshape(devices, tiles_dev, groups, picked)[..., 1:]
    incoming = (sources == own_block) & (peer_ids[:, None, None, None] != own_block)
    live_in = jnp.any(incoming, axis=(1, 2, 3))
    group_ids = jnp.arange(groups, dtype=jnp.int32)
    head_of = jnp.sum(jnp.where(incoming, group_ids[None, None, :, None], 0), axis=(1, 2, 3))
    ranking = jnp.argsort(jnp.where(live_in, 0, 1) * devices + peer_ids)
    inverse = jnp.argsort(ranking)
    rounds = (jnp.sum(live_in.astype(jnp.int32)) + per_group - 1) // per_group
    heads_sorted = jnp.take(head_of, ranking, axis=0)
    q_sorted = jnp.take(recv_q, ranking, axis=0)

    def forward_turn(turn, totals):
        served_out, served_lse = totals
        offset = turn * per_group
        query_part = lax.dynamic_slice_in_dim(q_sorted, offset, per_group, 0)
        head_part = lax.dynamic_slice_in_dim(heads_sorted, offset, per_group, 0)
        out_part, lse_part = attend_slots(query_part, head_part, k_heads, v_heads, scaling)
        served_out = lax.dynamic_update_slice_in_dim(served_out, out_part, offset, 0)
        served_lse = lax.dynamic_update_slice_in_dim(served_lse, lse_part, offset, 0)
        return (served_out, served_lse)

    start_fwd = (
        jnp.zeros((devices, head_dim, tile_rows), jnp.float32),
        jnp.zeros((devices, tile_rows), jnp.float32),
    )
    served_out, served_lse = lax.fori_loop(0, rounds, forward_turn, start_fwd)
    back_out, back_lse = (
        lax.all_to_all(
            jnp.take(served_out, inverse, axis=0), "ctx", split_axis=0, concat_axis=0, tiled=True
        ),
        lax.all_to_all(
            jnp.take(served_lse, inverse, axis=0), "ctx", split_axis=0, concat_axis=0, tiled=True
        ),
    )
    task_out = jnp.take(back_out, lookup, axis=0).reshape(
        tiles_dev, groups, others, head_dim, tile_rows
    )
    task_lse = jnp.take(back_lse, lookup, axis=0).reshape(tiles_dev, groups, others, tile_rows)
    own_out_t = own_out.reshape(groups, tiles_dev, tile_rows, head_dim).transpose(1, 0, 2, 3)
    own_lse_t = own_lse.reshape(groups, tiles_dev, tile_rows).transpose(1, 0, 2)
    active_rows = active[..., None]
    rem_lse = jnp.where(active_rows, task_lse, masked_value)
    ceiling = jnp.maximum(own_lse_t, jnp.max(rem_lse, axis=2))
    log_total = ceiling + jnp.log(
        jnp.exp(own_lse_t - ceiling) + jnp.sum(jnp.exp(rem_lse - ceiling[:, :, None]), axis=2)
    )
    own_weight = jnp.exp(own_lse_t - log_total)
    rem_weight = jnp.where(active_rows, jnp.exp(rem_lse - log_total[:, :, None]), 0.0)
    mixed = own_weight[..., None] * own_out_t + jnp.einsum(
        "tgiq,tgidq->tgqd", rem_weight, task_out, precision=highest
    )
    out_low = mixed.astype(jnp.bfloat16)
    attn_out = out_low.transpose(0, 2, 1, 3).reshape(row_count, columns)
    row_delta = jnp.sum(do_major.astype(jnp.float32) * out_low.astype(jnp.float32), axis=-1)
    own_scaled = (own_weight[..., None] * do_major.astype(jnp.float32)).astype(jnp.bfloat16)
    own_shift = own_weight * row_delta
    g_heads = own_scaled.transpose(1, 0, 2, 3).reshape(groups, row_count, head_dim)
    c_heads = own_shift.transpose(1, 0, 2).reshape(groups, row_count)

    def own_backward(inputs):
        q_head, k_head, v_head, g_head, c_head, lse_head = inputs
        grad_k = jnp.zeros((row_count, head_dim), jnp.float32)
        grad_v = jnp.zeros((row_count, head_dim), jnp.float32)
        dq_list = []
        for tile_step in range(tiles_dev):
            first = tile_step * tile_rows
            span = (tile_step + 1) * tile_rows
            q_part = q_head[first:span]
            g_part = g_head[first:span]
            k_part = k_head[:span]
            scores = (
                jnp.einsum("qd,kd->qk", q_part, k_part, preferred_element_type=jnp.float32)
                * scaling
            )
            scores = jnp.where(tile_masks[tile_step], scores, masked_value)
            attend = jnp.exp(scores - lse_head[first:span, None])
            attend_low = attend.astype(jnp.bfloat16)
            part_dv = jnp.einsum(
                "qk,qd->kd", attend_low, g_part, preferred_element_type=jnp.float32
            )
            grad_prob = jnp.einsum(
                "qd,kd->qk", g_part, v_head[:span], preferred_element_type=jnp.float32
            )
            dscore = (attend * (grad_prob - c_head[first:span, None])).astype(jnp.bfloat16)
            part_dk = (
                jnp.einsum("qk,qd->kd", dscore, q_part, preferred_element_type=jnp.float32)
                * scaling
            )
            dq_list.append(jnp.dot(dscore, k_part, preferred_element_type=jnp.float32) * scaling)
            padding = ((0, row_count - span), (0, 0))
            grad_k = grad_k + jnp.pad(part_dk, padding)
            grad_v = grad_v + jnp.pad(part_dv, padding)
        return (grad_k, grad_v, jnp.concatenate(dq_list, axis=0))

    own_dk, own_dv, own_dq = lax.map(
        own_backward, (q_heads, k_heads, v_heads, g_heads, c_heads, own_lse)
    )
    rem_shift = rem_weight * row_delta[:, :, None]
    rem_scaled = (rem_weight[..., None] * do_major[:, :, None].astype(jnp.float32)).astype(
        jnp.bfloat16
    )
    send_g = jnp.einsum(
        "jtgi,tgiqd->jdq", routing_low, rem_scaled, preferred_element_type=jnp.float32
    )
    send_c = jnp.einsum("jtgi,tgiq->jq", routing, rem_shift, precision=highest)
    recv_g, recv_c = (
        lax.all_to_all(send_g, "ctx", split_axis=0, concat_axis=0, tiled=True),
        lax.all_to_all(send_c, "ctx", split_axis=0, concat_axis=0, tiled=True),
    )
    g_sorted = jnp.take(recv_g, ranking, axis=0).astype(jnp.bfloat16)
    c_sorted = jnp.take(recv_c, ranking, axis=0)

    def backward_turn(turn, totals):
        grad_k, grad_v, served_dq = totals
        offset = turn * per_group
        query_part = lax.dynamic_slice_in_dim(q_sorted, offset, per_group, 0)
        cot_part = lax.dynamic_slice_in_dim(g_sorted, offset, per_group, 0)
        shift_part = lax.dynamic_slice_in_dim(c_sorted, offset, per_group, 0)
        lse_part = lax.dynamic_slice_in_dim(served_lse, offset, per_group, 0)
        head_part = lax.dynamic_slice_in_dim(heads_sorted, offset, per_group, 0)
        part_dk, part_dv, part_dq = slot_grads(
            query_part, cot_part, shift_part, lse_part, head_part, k_heads, v_heads, scaling
        )
        head_onehot = (head_part[:, None] == group_ids[None, :]).astype(jnp.float32)
        grad_k = grad_k + jnp.einsum("ng,nkd->gkd", head_onehot, part_dk, precision=highest)
        grad_v = grad_v + jnp.einsum("ng,nkd->gkd", head_onehot, part_dv, precision=highest)
        served_dq = lax.dynamic_update_slice_in_dim(served_dq, part_dq, offset, 0)
        return (grad_k, grad_v, served_dq)

    zeros_heads = jnp.zeros((groups, row_count, head_dim), jnp.float32)
    start_bwd = (zeros_heads, zeros_heads, jnp.zeros((devices, head_dim, tile_rows), jnp.float32))
    rem_dk, rem_dv, served_dq = lax.fori_loop(0, rounds, backward_turn, start_bwd)
    back_dq = lax.all_to_all(
        jnp.take(served_dq, inverse, axis=0).astype(jnp.bfloat16),
        "ctx",
        split_axis=0,
        concat_axis=0,
        tiled=True,
    ).astype(jnp.float32)
    task_dq = jnp.take(back_dq, lookup, axis=0).reshape(
        tiles_dev, groups, others, head_dim, tile_rows
    )
    rem_dq = jnp.sum(jnp.where(active[..., None, None], task_dq, 0.0), axis=2)
    own_dq_t = own_dq.reshape(groups, tiles_dev, tile_rows, head_dim).transpose(1, 0, 2, 3)
    total_dq = own_dq_t + rem_dq.transpose(0, 1, 3, 2)
    grad_query = total_dq.transpose(0, 2, 1, 3).reshape(row_count, columns).astype(jnp.bfloat16)
    grad_key = (own_dk + rem_dk).transpose(1, 0, 2).reshape(row_count, columns).astype(jnp.bfloat16)
    grad_value = (
        (own_dv + rem_dv).transpose(1, 0, 2).reshape(row_count, columns).astype(jnp.bfloat16)
    )
    return (attn_out, grad_query, grad_key, grad_value)


def pair_parts(near, far, tiles_dev, tile_rows):
    for part in range(tiles_dev):
        rows = slice(part * tile_rows, (part + 1) * tile_rows)
        cols = slice(part * 2 * tile_rows, tiles_dev * 2 * tile_rows)
        yield near.at[:, rows, cols], far.at[:, rows, cols]


def dot_t(a, b):
    return lax.dot_general(a, b, (((1,), (1,)), ((), ())), preferred_element_type=jnp.float32)


def split_low(x):
    high = x.astype(jnp.bfloat16).astype(jnp.float32)
    return high, x - high


def halves(block, head_dim):
    lane = lax.broadcasted_iota(jnp.int32, block.shape, 1)
    zero = jnp.zeros_like(block)
    return jnp.where(lane < head_dim, block, zero), jnp.where(lane < head_dim, zero, block)


def pack_kernel(tiles_dev, groups, picked, tile_rows, head_dim, devices):
    def body(picks_ref, q_ref, g_ref, send_ref, task_ref):
        own = picks_ref[0, 0, 0]
        meta_rows = send_ref.shape[1] - tile_rows
        lanes = send_ref.shape[2]
        row = lax.broadcasted_iota(jnp.int32, (meta_rows, lanes), 0)
        blank = jnp.zeros((meta_rows, lanes), jnp.bfloat16)
        for peer in range(devices):
            send_ref[peer, tile_rows:, :] = blank
            task_ref[peer] = -1
        for tile in range(tiles_dev):
            rows = slice(tile * tile_rows, (tile + 1) * tile_rows)
            for head in range(groups):
                cols = slice(head * head_dim, (head + 1) * head_dim)
                block = jnp.concatenate([q_ref[rows, cols], g_ref[rows, cols]], axis=1)
                code = tile * groups + head
                meta = jnp.where(row == 0, code + 1, 0)
                for entry in range(1, picked):
                    meta = jnp.where(row == entry, picks_ref[tile, head, entry], meta)
                meta = meta.astype(jnp.float32).astype(jnp.bfloat16)
                for entry in range(1, picked):
                    target = picks_ref[tile, head, entry]
                    send_ref[target, :tile_rows, :] = block
                    send_ref[target, tile_rows:, :] = meta
                    task_ref[target] = code
        task_ref[own] = -1

    return body


def own_kernel(tiles_dev, groups, tile_rows, head_dim, devices):
    scale = LOG2E / math.sqrt(head_dim)

    def body(q_hbm, k_hbm, v_hbm, g_hbm, kv_ref, vkt_ref, stat_ref, table_ref, qgt_hbm, mix_hbm,
             pd_hbm, q_ref, k_ref, v_ref, g_ref, qgt_ref, mix_ref, pd_ref, in_sem, out_sem):
        loads = [
            pltpu.make_async_copy(src, dst, in_sem.at[index])
            for index, (src, dst) in enumerate(((k_hbm, k_ref), (v_hbm, v_ref), (q_hbm, q_ref), (g_hbm, g_ref)))
        ]
        for load in loads:
            load.start()
        for load in loads:
            load.wait()
        sub = lax.broadcasted_iota(jnp.int32, (tile_rows, tile_rows), 0)
        lane = lax.broadcasted_iota(jnp.int32, (tile_rows, tile_rows), 1)
        causal = sub <= lane
        for head in range(groups):
            cols = slice(head * head_dim, (head + 1) * head_dim)
            k_head = k_ref[:, cols]
            v_head = v_ref[:, cols]
            kv_ref[head] = jnp.concatenate([k_head, v_head], axis=1)
            vkt_ref[head] = jnp.concatenate([v_head, k_head], axis=1).T
            block_all = jnp.concatenate([q_ref[:, cols], g_ref[:, cols]], axis=1)
            qgt_ref[head] = block_all.T
            for tile in range(tiles_dev):
                rows = slice(tile * tile_rows, (tile + 1) * tile_rows)
                span = (tile + 1) * tile_rows
                code = tile * groups + head
                at = tile * 2 * tile_rows
                both = dot_t(kv_ref[head, :span, :], jnp.concatenate(halves(block_all[rows], head_dim), axis=0))
                scores = both[:, :tile_rows]
                last = jnp.where(causal, scores[span - tile_rows :], masked_value)
                peak = jnp.max(last, axis=0, keepdims=True)
                if tile:
                    peak = jnp.maximum(peak, jnp.max(scores[: span - tile_rows], axis=0, keepdims=True))
                peak = peak * scale
                total = jnp.zeros((1, tile_rows), jnp.float32)
                mean_grad = jnp.zeros((1, tile_rows), jnp.float32)
                for part in range(tile + 1):
                    chunk = slice(part * tile_rows, (part + 1) * tile_rows)
                    piece = last if part == tile else scores[chunk]
                    powers = jnp.exp2(piece * scale - peak)
                    spread = powers * both[chunk, tile_rows:]
                    total = total + jnp.sum(powers, axis=0, keepdims=True)
                    mean_grad = mean_grad + jnp.sum(spread, axis=0, keepdims=True)
                    pd_ref[head, chunk, at : at + tile_rows] = powers.astype(jnp.bfloat16)
                    pd_ref[head, chunk, at + tile_rows : at + 2 * tile_rows] = spread.astype(jnp.bfloat16)
                inverse = 1.0 / total
                mean_grad = mean_grad * inverse
                lse = peak + jnp.log2(total)
                result = jnp.dot(vkt_ref[head, :, :span], pd_ref[head, :span, at : at + 2 * tile_rows],
                                 preferred_element_type=jnp.float32)
                top = result[:, :tile_rows]
                low = result[head_dim:, tile_rows:]
                mix_ref[head, tile, : 2 * head_dim, :] = (top * inverse).astype(jnp.bfloat16)
                mix_ref[head, tile, 2 * head_dim :, :] = (low * inverse).astype(jnp.bfloat16)
                stat_ref[0, code : code + 1, :] = lse
                stat_ref[1, code : code + 1, :] = mean_grad
                stat_ref[2, code : code + 1, :] = inverse
                parts = split_low(lse) + (mean_grad,)
                for index in range(3):
                    table_ref[code, index : index + 1, :] = parts[index]
        stores = [
            pltpu.make_async_copy(mix_ref, mix_hbm, out_sem.at[tiles_dev]),
            pltpu.make_async_copy(qgt_ref, qgt_hbm, out_sem.at[tiles_dev + 1]),
        ] + [
            pltpu.make_async_copy(src, dst, out_sem.at[index])
            for index, (src, dst) in enumerate(pair_parts(pd_ref, pd_hbm, tiles_dev, tile_rows))
        ]
        for store in stores:
            store.start()
        for store in stores:
            store.wait()

    return body


def parts_of(block, kv_head, tile_rows, head_dim, scale):
    both = dot_t(kv_head, jnp.concatenate(halves(block, head_dim), axis=0))
    scores = both[:, :tile_rows]
    peak = jnp.max(scores, axis=0, keepdims=True) * scale
    powers = jnp.exp2(scores * scale - peak)
    spread = powers * both[:, tile_rows:]
    return peak, powers, spread


def serve_kernel(groups, tile_rows, head_dim, devices):
    scale = LOG2E / math.sqrt(head_dim)

    def body(picks_ref, task_ref, recv_ref, kv_ref, vkt_ref, table_ref, send_hbm, inv_ref,
             send_ref, st_ref, out_sem):
        own = picks_ref[0, 0, 0]
        st_ref[...] = jnp.zeros_like(st_ref)
        inv_ref[...] = jnp.zeros_like(inv_ref)
        heads = [None]
        blocks = [None]
        for source in range(1, devices):
            code = jnp.max(recv_ref[source, tile_rows:, :].astype(jnp.float32)[0:1, :]).astype(jnp.int32) - 1
            block = recv_ref[source, :tile_rows, :]
            heads.append(lax.rem(jnp.maximum(code, 0), groups))
            blocks.append(jnp.where((code >= 0) & (own != source), block, jnp.zeros_like(block)))
        ahead = parts_of(blocks[1], kv_ref[heads[1]], tile_rows, head_dim, scale)
        for source in range(1, devices):
            peak, powers, spread = ahead
            if source + 1 < devices:
                ahead = parts_of(blocks[source + 1], kv_ref[heads[source + 1]], tile_rows, head_dim, scale)
            total = jnp.sum(powers, axis=0, keepdims=True)
            inverse = 1.0 / total
            mean_grad = jnp.sum(spread, axis=0, keepdims=True) * inverse
            both = jnp.concatenate([powers.astype(jnp.bfloat16), spread.astype(jnp.bfloat16)], axis=1)
            result = jnp.dot(vkt_ref[heads[source]], both, preferred_element_type=jnp.float32)
            send_ref[source, : 2 * head_dim, :] = (result[:, :tile_rows] * inverse).astype(jnp.bfloat16)
            send_ref[source, 2 * head_dim : 3 * head_dim, :] = (result[head_dim:, tile_rows:] * inverse).astype(jnp.bfloat16)
            parts = split_low(peak + jnp.log2(total)) + (mean_grad,)
            for index in range(3):
                st_ref[index * devices + source : index * devices + source + 1, :] = parts[index]
            inv_ref[source : source + 1, :] = inverse
        table = st_ref[...]
        row = lax.broadcasted_iota(jnp.int32, table.shape, 0)
        mine = lax.rem(row, devices) == own
        for peer in range(devices):
            code = jnp.maximum(task_ref[peer], 0)
            entry = table_ref[code]
            wide = jnp.concatenate(
                [jnp.broadcast_to(entry[index : index + 1], (devices, tile_rows)) for index in range(3)], axis=0
            )
            send_ref[peer, 3 * head_dim :, :] = jnp.where(mine, wide, table).astype(jnp.bfloat16)
        store = pltpu.make_async_copy(send_ref, send_hbm, out_sem)
        store.start()
        store.wait()

    return body


def again_kernel(groups, tile_rows, head_dim, devices):
    scale = LOG2E / math.sqrt(head_dim)

    def body(picks_ref, recv_ref, kv_ref, pd_ref, qgt_ref, meta_ref):
        own = picks_ref[0, 0, 0]
        for source in range(devices):
            meta_ref[source] = recv_ref[source, tile_rows:, :].astype(jnp.float32)

        def turn(source, carry):
            code = jnp.max(recv_ref[source, tile_rows:, :].astype(jnp.float32)[0:1, :]).astype(jnp.int32) - 1
            block = recv_ref[source, :tile_rows, :]
            block = jnp.where((code >= 0) & (own != source), block, jnp.zeros_like(block))
            head = lax.rem(jnp.maximum(code, 0), groups)
            _, powers, spread = parts_of(block, kv_ref[head], tile_rows, head_dim, scale)
            pd_ref[source - 1, :, :tile_rows] = powers.astype(jnp.bfloat16)
            pd_ref[source - 1, :, tile_rows:] = spread.astype(jnp.bfloat16)
            qgt_ref[source - 1] = block.T
            return carry

        lax.fori_loop(1, devices, turn, 0)

    return body


def final_kernel(tiles_dev, groups, picked, tile_rows, head_dim, devices):
    scaling = 1.0 / math.sqrt(head_dim)
    pair = 2 * tile_rows

    def body(picks_ref, task_ref, meta_ref, back_ref, qgt_in_ref, stat_ref, inv_ref,
             pd_in_ref, qgt_hbm, mix_hbm, pd_hbm, out_hbm, dq_hbm, dk_hbm, dv_hbm,
             qgt_ref, mix_ref, pd_ref, out_ref, dq_ref, dk_ref, dv_ref, acc_ref, grad_ref, more_ref,
             lse_sc, gd_sc, w_sc, d_sc, x_ref, xin_ref, in_sem, out_sem):
        own = picks_ref[0, 0, 0]
        tasks = tiles_dev * groups
        base = 3 * head_dim
        loads = [
            pltpu.make_async_copy(mix_hbm, mix_ref, in_sem.at[tiles_dev]),
            pltpu.make_async_copy(qgt_hbm, qgt_ref, in_sem.at[tiles_dev + 1]),
        ] + [
            pltpu.make_async_copy(src, dst, in_sem.at[index])
            for index, (dst, src) in enumerate(pair_parts(pd_ref, pd_hbm, tiles_dev, tile_rows))
        ]
        for load in loads:
            load.start()
        grad_ref[...] = jnp.zeros_like(grad_ref)
        more_ref[...] = jnp.zeros_like(more_ref)
        for part in range(1, tiles_dev, 2):
            rows = slice(part * tile_rows, (part + 1) * tile_rows)
            pd_ref[:, rows, (part - 1) * pair : part * pair] = jnp.zeros((groups, tile_rows, pair), jnp.bfloat16)

        lse_of = []
        gd_of = []
        for peer in range(devices):
            table = back_ref[peer, base:, :].astype(jnp.float32)
            lse_of.append(table[:devices] + table[devices : 2 * devices])
            gd_of.append(table[2 * devices :])
            lse_sc[peer] = lse_of[peer]
            gd_sc[peer] = gd_of[peer]

        ids = lax.broadcasted_iota(jnp.int32, (devices, tile_rows), 0)
        metas = [meta_ref[source] for source in range(devices)]
        rows_of = [
            jnp.concatenate([metas[source][entry : entry + 1] for source in range(devices)], axis=0).astype(jnp.int32)
            for entry in range(picked)
        ]
        codes = [None] + [jnp.max(metas[source][0:1, :]).astype(jnp.int32) - 1 for source in range(1, devices)]
        live = (rows_of[0] > 0) & (ids != own)
        chosen = []
        for peer in range(devices):
            active = ids == peer
            for entry in rows_of[1:]:
                active = active | (entry == peer)
            chosen.append(active)
        peak = jnp.full((devices, tile_rows), masked_value, jnp.float32)
        for peer in range(devices):
            peak = jnp.maximum(peak, jnp.where(chosen[peer], lse_of[peer], masked_value))
        total = jnp.zeros_like(peak)
        delta = jnp.zeros_like(peak)
        for peer in range(devices):
            power = jnp.where(chosen[peer], jnp.exp2(lse_of[peer] - peak), 0.0)
            total = total + power
            delta = delta + jnp.where(chosen[peer], power * gd_of[peer], 0.0)
        delta = delta / total
        weight = jnp.exp2(lse_sc[own] - peak) / total * inv_ref[...]
        w_sc[0] = jnp.where(live, weight, 0.0)
        w_sc[1] = jnp.where(live, -weight * delta, 0.0)

        code_ids = lax.broadcasted_iota(jnp.int32, (tasks, tile_rows), 0)
        own_lse = stat_ref[0]
        own_gd = stat_ref[1]
        peak = own_lse
        rows_lse = [lse_sc[peer, pl.ds(own, 1), :] for peer in range(devices)]
        rows_gd = [gd_sc[peer, pl.ds(own, 1), :] for peer in range(devices)]
        for peer in range(devices):
            peak = jnp.maximum(peak, jnp.where(code_ids == task_ref[peer], rows_lse[peer], masked_value))
        own_power = jnp.exp2(own_lse - peak)
        total = own_power
        delta = own_power * own_gd
        for peer in range(devices):
            here = code_ids == task_ref[peer]
            power = jnp.where(here, jnp.exp2(rows_lse[peer] - peak), 0.0)
            total = total + power
            delta = delta + jnp.where(here, power * rows_gd[peer], 0.0)
        inverse = 1.0 / total
        delta = delta * inverse
        own_weight = own_power * inverse
        d_sc[0] = peak
        d_sc[1] = inverse
        d_sc[2] = delta
        d_sc[3] = own_weight
        d_sc[4] = own_weight * stat_ref[2]
        d_sc[5] = -own_weight * stat_ref[2] * delta
        d_sc[6] = -own_weight * delta

        nothing = jnp.zeros((head_dim, tile_rows), jnp.bfloat16)
        for source in range(1, devices):
            odd = lax.rem(jnp.maximum(codes[source], 0), 2) == 1
            first = w_sc[0, source : source + 1, :]
            second = w_sc[1, source : source + 1, :]
            turned = qgt_in_ref[source - 1].astype(jnp.float32)
            g_first = (turned[head_dim:] * first).astype(jnp.bfloat16)
            q_first = (turned[:head_dim] * first).astype(jnp.bfloat16)
            q_second = (turned[:head_dim] * second).astype(jnp.bfloat16)
            xin_ref[source, :head_dim, :tile_rows] = jnp.where(odd, q_second, g_first)
            xin_ref[source, :head_dim, tile_rows:] = jnp.where(odd, q_first, nothing)
            xin_ref[source, head_dim:, :tile_rows] = jnp.where(odd, g_first, q_second)
            xin_ref[source, head_dim:, tile_rows:] = jnp.where(odd, nothing, q_first)
        for source in range(1, devices):
            head = lax.rem(jnp.maximum(codes[source], 0), groups)
            target = grad_ref if source % 2 else more_ref
            target[head] += dot_t(pd_in_ref[source - 1], xin_ref[source])

        for load in loads:
            load.wait()
        for head in range(groups):
            v_rows = slice(0, head_dim) if head % 2 == 0 else slice(head_dim, 2 * head_dim)
            k_rows = slice(head_dim, 2 * head_dim) if head % 2 == 0 else slice(0, head_dim)
            for tile in range(tiles_dev):
                code = tile * groups + head
                first = d_sc[4, code : code + 1, :]
                second = d_sc[5, code : code + 1, :]
                turned = qgt_ref[head, :, tile * tile_rows : (tile + 1) * tile_rows].astype(jnp.float32)
                early = slice(tile * pair, tile * pair + tile_rows)
                late = slice(tile * pair + tile_rows, (tile + 1) * pair)
                x_ref[head, v_rows, early] = (turned[head_dim:] * first).astype(jnp.bfloat16)
                x_ref[head, v_rows, late] = nothing
                x_ref[head, k_rows, early] = (turned[:head_dim] * second).astype(jnp.bfloat16)
                x_ref[head, k_rows, late] = (turned[:head_dim] * first).astype(jnp.bfloat16)
        for head in range(groups):
            for tile in range(tiles_dev):
                code = tile * groups + head
                first = d_sc[3, code : code + 1, :]
                second = d_sc[6, code : code + 1, :]
                mix = mix_ref[head, tile].astype(jnp.float32)
                acc_ref[0, code] = mix[:head_dim] * first
                acc_ref[1, code] = mix[2 * head_dim :] * first + mix[head_dim : 2 * head_dim] * second

        def gather(peer, carry):
            code = task_ref[peer]

            @pl.when(code >= 0)
            def _():
                at = pl.ds(code, 1)
                part_w = jnp.exp2(lse_sc[peer, pl.ds(own, 1), :] - d_sc[0, at, :]) * d_sc[1, at, :]
                shift = -part_w * d_sc[2, at, :]
                mix = back_ref[peer, : 3 * head_dim, :].astype(jnp.float32)
                acc_ref[0, code] += mix[:head_dim] * part_w
                acc_ref[1, code] += mix[2 * head_dim :] * part_w + mix[head_dim : 2 * head_dim] * shift

            return carry

        lax.fori_loop(0, own, gather, 0)

        sub = lax.broadcasted_iota(jnp.int32, (tile_rows, tile_rows), 0)
        lane = lax.broadcasted_iota(jnp.int32, (tile_rows, tile_rows), 1)
        unit = jnp.where(sub == lane, 1.0, 0.0).astype(jnp.bfloat16)
        for tile in range(tiles_dev):
            rows = slice(tile * tile_rows, (tile + 1) * tile_rows)
            for head in range(0, groups, 2):
                cols = slice(head * head_dim, (head + 2) * head_dim)
                code = tile * groups + head
                both = jnp.concatenate([acc_ref[0, code], acc_ref[0, code + 1]], axis=0).astype(jnp.bfloat16)
                out_ref[rows, cols] = dot_t(unit, both).astype(jnp.bfloat16)
                both = jnp.concatenate([acc_ref[1, code], acc_ref[1, code + 1]], axis=0)
                dq_ref[rows, cols] = dot_t(unit, (both * scaling).astype(jnp.bfloat16)).astype(jnp.bfloat16)
        stores = [
            pltpu.make_async_copy(src, dst, out_sem.at[index])
            for index, (src, dst) in enumerate(((out_ref, out_hbm), (dq_ref, dq_hbm), (dk_ref, dk_hbm), (dv_ref, dv_hbm)))
        ]
        stores[0].start()
        stores[1].start()

        for head in range(groups):
            for first in range(0, tiles_dev, 2):
                rows = slice(first * tile_rows, (first + 2) * tile_rows)
                grad_ref[head, rows, :] += dot_t(pd_ref[head, rows, first * pair :], x_ref[head, :, first * pair :])
        lane = lax.broadcasted_iota(jnp.int32, (tile_rows, 2 * head_dim), 1)
        for head in range(0, groups, 2):
            cols = slice(head * head_dim, (head + 2) * head_dim)
            for part in range(tiles_dev):
                rows = slice(part * tile_rows, (part + 1) * tile_rows)
                even = grad_ref[head, rows, :] + more_ref[head, rows, :]
                odd = grad_ref[head + 1, rows, :] + more_ref[head + 1, rows, :]
                dv_ref[rows, cols] = jnp.where(lane < head_dim, even, odd).astype(jnp.bfloat16)
                swapped = jnp.where(lane < head_dim, odd, even) * scaling
                dk_ref[rows, cols] = pltpu.roll(swapped, head_dim, 1).astype(jnp.bfloat16)
        stores[2].start()
        stores[3].start()
        for store in stores:
            store.wait()

    return body


def fast_local(query, key, value, grad_out, picks):
    row_count, columns = query.shape
    tiles_dev, groups, picked = picks.shape
    head_dim = columns // groups
    tile_rows = row_count // tiles_dev
    devices = lax.axis_size("ctx")
    tasks = tiles_dev * groups
    smem = pl.BlockSpec(memory_space=pltpu.SMEM)
    vmem = pl.BlockSpec(memory_space=pltpu.VMEM)
    far = pl.BlockSpec(memory_space=pltpu.HBM)
    low = jnp.bfloat16
    wide = jnp.float32
    width = 2 * head_dim
    shape = jax.ShapeDtypeStruct
    dma = pltpu.SemaphoreType.DMA
    small = pltpu.CompilerParams(vmem_limit_bytes=vmem_grant)
    near = pltpu.VMEM

    def away(*arrays):
        return tuple(pltpu.with_memory_space_constraint(x, pltpu.HBM) for x in arrays)

    def keep(*arrays):
        return tuple(pltpu.with_memory_space_constraint(x, pltpu.VMEM) for x in arrays)


    send_q, task_of = pl.pallas_call(
        pack_kernel(tiles_dev, groups, picked, tile_rows, head_dim, devices),
        out_shape=(shape((devices, tile_rows + 8, width), low), shape((devices,), jnp.int32)),
        in_specs=[smem, vmem, vmem],
        out_specs=(vmem, smem),
        name="pack",
    )(picks, query, grad_out)
    recv_q = lax.all_to_all(send_q, "ctx", split_axis=0, concat_axis=0, tiled=True)

    mix_shape = (groups, tiles_dev, 3 * head_dim, tile_rows)
    pair_shape = (groups, row_count, 2 * row_count)
    kv, vkt, stats, table, qgt, mix, pairs = pl.pallas_call(
        own_kernel(tiles_dev, groups, tile_rows, head_dim, devices),
        out_shape=(
            near((groups, row_count, width), low),
            near((groups, width, row_count), low),
            near((3, tasks, tile_rows), wide),
            near((tasks, 8, tile_rows), wide),
            pltpu.HBM((groups, width, row_count), low),
            pltpu.HBM(mix_shape, low),
            pltpu.HBM(pair_shape, low),
        ),
        in_specs=[far] * 4,
        out_specs=tuple([vmem] * 4 + [far] * 3),
        scratch_shapes=[pltpu.VMEM((row_count, columns), low)] * 4
        + [
            pltpu.VMEM((groups, width, row_count), low),
            pltpu.VMEM(mix_shape, low),
            pltpu.VMEM(pair_shape, low),
            dma((4,)),
            dma((tiles_dev + 2,)),
        ],
        compiler_params=small,
        name="own",
    )(*away(query, key, value, grad_out))

    slot = 3 * head_dim + 3 * devices
    in_shape = (devices - 1, row_count, 2 * tile_rows)
    send_b, inverse_in = pl.pallas_call(
        serve_kernel(groups, tile_rows, head_dim, devices),
        out_shape=(pltpu.HBM((devices, slot, tile_rows), low), near((devices, tile_rows), wide)),
        in_specs=[smem, smem, vmem, vmem, vmem, vmem],
        out_specs=(far, vmem),
        scratch_shapes=[
            pltpu.VMEM((devices, slot, tile_rows), low),
            pltpu.VMEM((3 * devices, tile_rows), wide),
            dma(()),
        ],
        compiler_params=small,
        name="serve",
    )(*away(picks, task_of), *keep(recv_q, kv, vkt, table))
    recv_b = lax.all_to_all(send_b, "ctx", split_axis=0, concat_axis=0, tiled=True)

    pairs_in, qgt_in, lists_in = pl.pallas_call(
        again_kernel(groups, tile_rows, head_dim, devices),
        out_shape=(near(in_shape, low), near((devices - 1, width, tile_rows), low), near((devices, 8, width), wide)),
        in_specs=[smem, vmem, vmem],
        out_specs=(vmem, vmem, vmem),
        compiler_params=small,
        name="again",
    )(*away(picks), *keep(recv_q, kv))

    return pl.pallas_call(
        final_kernel(tiles_dev, groups, picked, tile_rows, head_dim, devices),
        out_shape=tuple([shape((row_count, columns), low)] * 4),
        in_specs=[smem, smem] + [vmem] * 6 + [far] * 3,
        out_specs=tuple([far] * 4),
        scratch_shapes=[
            pltpu.VMEM((groups, width, row_count), low),
            pltpu.VMEM(mix_shape, low),
            pltpu.VMEM(pair_shape, low),
        ]
        + [pltpu.VMEM((row_count, columns), low)] * 4
        + [
            pltpu.VMEM((2, tasks, head_dim, tile_rows), wide),
            pltpu.VMEM((groups, row_count, width), wide),
            pltpu.VMEM((groups, row_count, width), wide),
            pltpu.VMEM((devices, devices, tile_rows), wide),
            pltpu.VMEM((devices, devices, tile_rows), wide),
            pltpu.VMEM((2, devices, tile_rows), wide),
            pltpu.VMEM((7, tasks, tile_rows), wide),
            pltpu.VMEM((groups, width, 2 * row_count), low),
            pltpu.VMEM((devices, width, 2 * tile_rows), low),
            dma((tiles_dev + 2,)),
            dma((4,)),
        ],
        compiler_params=small,
        name="final",
    )(*away(picks, task_of), *keep(lists_in, recv_b, qgt_in, stats, inverse_in, pairs_in), *away(qgt, mix, pairs))


def choose(query, key, value, grad_out, picks):
    pair_bytes = lax.axis_size("ctx") * query.shape[0] * (query.shape[0] // picks.shape[0]) * 4
    plan = fast_local if pair_bytes <= pair_budget else local
    return plan(query, key, value, grad_out, picks)


def solution(mesh):
    placed = (
        P("ctx", "head"),
        P("ctx", "head"),
        P("ctx", "head"),
        P("ctx", "head"),
        P("ctx", "head", None),
    )
    return jax.shard_map(
        choose,
        mesh=mesh,
        in_specs=placed,
        out_specs=(P("ctx", "head"), P("ctx", "head"), P("ctx", "head"), P("ctx", "head")),
        check_vma=False,
    )
```

```python
import math

import jax
import jax.numpy as jnp
from jax import lax
from jax.experimental import pallas as pl
from jax.experimental.pallas import tpu as pltpu
from jax.sharding import PartitionSpec as P

masked_value = -1e30
highest = lax.Precision.HIGHEST
LOG2E = math.log2(math.e)
pair_budget = 8 << 20
vmem_grant = 32 << 20


def attend_slots(q_slots, head_ids, k_heads, v_heads, scaling):
    key_rows = jnp.take(k_heads, head_ids, axis=0)
    value_rows = jnp.take(v_heads, head_ids, axis=0)
    scores = (
        jnp.einsum("ndq,nkd->nqk", q_slots, key_rows, preferred_element_type=jnp.float32) * scaling
    )
    peak_score = jnp.max(scores, axis=-1, keepdims=True)
    log_total = peak_score + jnp.log(jnp.sum(jnp.exp(scores - peak_score), axis=-1, keepdims=True))
    attend_low = jnp.exp(scores - log_total).astype(jnp.bfloat16)
    outputs = jnp.einsum("nqk,nkd->ndq", attend_low, value_rows, preferred_element_type=jnp.float32)
    return (outputs, log_total[..., 0])


def slot_grads(q_slots, g_slots, c_slots, lse_slots, head_ids, k_heads, v_heads, scaling):
    key_rows = jnp.take(k_heads, head_ids, axis=0)
    value_rows = jnp.take(v_heads, head_ids, axis=0)
    scores = (
        jnp.einsum("ndq,nkd->nqk", q_slots, key_rows, preferred_element_type=jnp.float32) * scaling
    )
    attend = jnp.exp(scores - lse_slots[..., None])
    attend_low = attend.astype(jnp.bfloat16)
    grad_v = jnp.einsum("nqk,ndq->nkd", attend_low, g_slots, preferred_element_type=jnp.float32)
    grad_prob = jnp.einsum("ndq,nkd->nqk", g_slots, value_rows, preferred_element_type=jnp.float32)
    dscore = (attend * (grad_prob - c_slots[..., None])).astype(jnp.bfloat16)
    grad_k = (
        jnp.einsum("nqk,ndq->nkd", dscore, q_slots, preferred_element_type=jnp.float32) * scaling
    )
    grad_q = (
        jnp.einsum("nqk,nkd->ndq", dscore, key_rows, preferred_element_type=jnp.float32) * scaling
    )
    return (grad_k, grad_v, grad_q)


def local(query, key, value, grad_out, picks):
    row_count, columns = query.shape
    tiles_dev, groups, picked = picks.shape
    head_dim = columns // groups
    tile_rows = row_count // tiles_dev
    others = picked - 1
    scaling = 1.0 / math.sqrt(head_dim)
    devices = lax.axis_size("ctx")
    own_block = lax.axis_index("ctx")
    per_group = min(8, devices)
    all_picks = lax.all_gather(picks, "ctx", axis=0, tiled=True)
    q_heads = query.reshape(row_count, groups, head_dim).transpose(1, 0, 2)
    k_heads = key.reshape(row_count, groups, head_dim).transpose(1, 0, 2)
    v_heads = value.reshape(row_count, groups, head_dim).transpose(1, 0, 2)
    q_tiles = query.reshape(tiles_dev, tile_rows, groups, head_dim)
    do_tiles = grad_out.reshape(tiles_dev, tile_rows, groups, head_dim)
    do_major = do_tiles.transpose(0, 2, 1, 3)
    positions = jnp.arange(row_count, dtype=jnp.int32)
    tile_masks = []
    for tile_step in range(tiles_dev):
        span = (tile_step + 1) * tile_rows
        query_pos = positions[tile_step * tile_rows : span]
        tile_masks.append(positions[None, :span] <= query_pos[:, None])
    targets = picks[:, :, 1:]
    active = targets != own_block
    lookup = jnp.where(active, targets, own_block).reshape(-1)
    peer_ids = jnp.arange(devices, dtype=jnp.int32)
    routing = ((targets[None] == peer_ids[:, None, None, None]) & active[None]).astype(jnp.float32)
    routing_low = routing.astype(jnp.bfloat16)
    send_q = jnp.einsum(
        "jtgi,tqgd->jdq", routing_low, q_tiles, preferred_element_type=jnp.float32
    ).astype(jnp.bfloat16)
    recv_q = lax.all_to_all(send_q, "ctx", split_axis=0, concat_axis=0, tiled=True)

    def own_forward(inputs):
        q_head, k_head, v_head = inputs
        out_list = []
        lse_list = []
        for tile_step in range(tiles_dev):
            span = (tile_step + 1) * tile_rows
            q_part = q_head[tile_step * tile_rows : span]
            scores = (
                jnp.einsum("qd,kd->qk", q_part, k_head[:span], preferred_element_type=jnp.float32)
                * scaling
            )
            scores = jnp.where(tile_masks[tile_step], scores, masked_value)
            peak_score = jnp.max(scores, axis=-1, keepdims=True)
            log_total = peak_score + jnp.log(
                jnp.sum(jnp.exp(scores - peak_score), axis=-1, keepdims=True)
            )
            attend_low = jnp.exp(scores - log_total).astype(jnp.bfloat16)
            out_list.append(jnp.dot(attend_low, v_head[:span], preferred_element_type=jnp.float32))
            lse_list.append(log_total[:, 0])
        return (jnp.concatenate(out_list, axis=0), jnp.concatenate(lse_list, axis=0))

    own_out, own_lse = lax.map(own_forward, (q_heads, k_heads, v_heads))
    sources = all_picks.reshape(devices, tiles_dev, groups, picked)[..., 1:]
    incoming = (sources == own_block) & (peer_ids[:, None, None, None] != own_block)
    live_in = jnp.any(incoming, axis=(1, 2, 3))
    group_ids = jnp.arange(groups, dtype=jnp.int32)
    head_of = jnp.sum(jnp.where(incoming, group_ids[None, None, :, None], 0), axis=(1, 2, 3))
    ranking = jnp.argsort(jnp.where(live_in, 0, 1) * devices + peer_ids)
    inverse = jnp.argsort(ranking)
    rounds = (jnp.sum(live_in.astype(jnp.int32)) + per_group - 1) // per_group
    heads_sorted = jnp.take(head_of, ranking, axis=0)
    q_sorted = jnp.take(recv_q, ranking, axis=0)

    def forward_turn(turn, totals):
        served_out, served_lse = totals
        offset = turn * per_group
        query_part = lax.dynamic_slice_in_dim(q_sorted, offset, per_group, 0)
        head_part = lax.dynamic_slice_in_dim(heads_sorted, offset, per_group, 0)
        out_part, lse_part = attend_slots(query_part, head_part, k_heads, v_heads, scaling)
        served_out = lax.dynamic_update_slice_in_dim(served_out, out_part, offset, 0)
        served_lse = lax.dynamic_update_slice_in_dim(served_lse, lse_part, offset, 0)
        return (served_out, served_lse)

    start_fwd = (
        jnp.zeros((devices, head_dim, tile_rows), jnp.float32),
        jnp.zeros((devices, tile_rows), jnp.float32),
    )
    served_out, served_lse = lax.fori_loop(0, rounds, forward_turn, start_fwd)
    back_out, back_lse = (
        lax.all_to_all(
            jnp.take(served_out, inverse, axis=0), "ctx", split_axis=0, concat_axis=0, tiled=True
        ),
        lax.all_to_all(
            jnp.take(served_lse, inverse, axis=0), "ctx", split_axis=0, concat_axis=0, tiled=True
        ),
    )
    task_out = jnp.take(back_out, lookup, axis=0).reshape(
        tiles_dev, groups, others, head_dim, tile_rows
    )
    task_lse = jnp.take(back_lse, lookup, axis=0).reshape(tiles_dev, groups, others, tile_rows)
    own_out_t = own_out.reshape(groups, tiles_dev, tile_rows, head_dim).transpose(1, 0, 2, 3)
    own_lse_t = own_lse.reshape(groups, tiles_dev, tile_rows).transpose(1, 0, 2)
    active_rows = active[..., None]
    rem_lse = jnp.where(active_rows, task_lse, masked_value)
    ceiling = jnp.maximum(own_lse_t, jnp.max(rem_lse, axis=2))
    log_total = ceiling + jnp.log(
        jnp.exp(own_lse_t - ceiling) + jnp.sum(jnp.exp(rem_lse - ceiling[:, :, None]), axis=2)
    )
    own_weight = jnp.exp(own_lse_t - log_total)
    rem_weight = jnp.where(active_rows, jnp.exp(rem_lse - log_total[:, :, None]), 0.0)
    mixed = own_weight[..., None] * own_out_t + jnp.einsum(
        "tgiq,tgidq->tgqd", rem_weight, task_out, precision=highest
    )
    out_low = mixed.astype(jnp.bfloat16)
    attn_out = out_low.transpose(0, 2, 1, 3).reshape(row_count, columns)
    row_delta = jnp.sum(do_major.astype(jnp.float32) * out_low.astype(jnp.float32), axis=-1)
    own_scaled = (own_weight[..., None] * do_major.astype(jnp.float32)).astype(jnp.bfloat16)
    own_shift = own_weight * row_delta
    g_heads = own_scaled.transpose(1, 0, 2, 3).reshape(groups, row_count, head_dim)
    c_heads = own_shift.transpose(1, 0, 2).reshape(groups, row_count)

    def own_backward(inputs):
        q_head, k_head, v_head, g_head, c_head, lse_head = inputs
        grad_k = jnp.zeros((row_count, head_dim), jnp.float32)
        grad_v = jnp.zeros((row_count, head_dim), jnp.float32)
        dq_list = []
        for tile_step in range(tiles_dev):
            first = tile_step * tile_rows
            span = (tile_step + 1) * tile_rows
            q_part = q_head[first:span]
            g_part = g_head[first:span]
            k_part = k_head[:span]
            scores = (
                jnp.einsum("qd,kd->qk", q_part, k_part, preferred_element_type=jnp.float32)
                * scaling
            )
            scores = jnp.where(tile_masks[tile_step], scores, masked_value)
            attend = jnp.exp(scores - lse_head[first:span, None])
            attend_low = attend.astype(jnp.bfloat16)
            part_dv = jnp.einsum(
                "qk,qd->kd", attend_low, g_part, preferred_element_type=jnp.float32
            )
            grad_prob = jnp.einsum(
                "qd,kd->qk", g_part, v_head[:span], preferred_element_type=jnp.float32
            )
            dscore = (attend * (grad_prob - c_head[first:span, None])).astype(jnp.bfloat16)
            part_dk = (
                jnp.einsum("qk,qd->kd", dscore, q_part, preferred_element_type=jnp.float32)
                * scaling
            )
            dq_list.append(jnp.dot(dscore, k_part, preferred_element_type=jnp.float32) * scaling)
            padding = ((0, row_count - span), (0, 0))
            grad_k = grad_k + jnp.pad(part_dk, padding)
            grad_v = grad_v + jnp.pad(part_dv, padding)
        return (grad_k, grad_v, jnp.concatenate(dq_list, axis=0))

    own_dk, own_dv, own_dq = lax.map(
        own_backward, (q_heads, k_heads, v_heads, g_heads, c_heads, own_lse)
    )
    rem_shift = rem_weight * row_delta[:, :, None]
    rem_scaled = (rem_weight[..., None] * do_major[:, :, None].astype(jnp.float32)).astype(
        jnp.bfloat16
    )
    send_g = jnp.einsum(
        "jtgi,tgiqd->jdq", routing_low, rem_scaled, preferred_element_type=jnp.float32
    )
    send_c = jnp.einsum("jtgi,tgiq->jq", routing, rem_shift, precision=highest)
    recv_g, recv_c = (
        lax.all_to_all(send_g, "ctx", split_axis=0, concat_axis=0, tiled=True),
        lax.all_to_all(send_c, "ctx", split_axis=0, concat_axis=0, tiled=True),
    )
    g_sorted = jnp.take(recv_g, ranking, axis=0).astype(jnp.bfloat16)
    c_sorted = jnp.take(recv_c, ranking, axis=0)

    def backward_turn(turn, totals):
        grad_k, grad_v, served_dq = totals
        offset = turn * per_group
        query_part = lax.dynamic_slice_in_dim(q_sorted, offset, per_group, 0)
        cot_part = lax.dynamic_slice_in_dim(g_sorted, offset, per_group, 0)
        shift_part = lax.dynamic_slice_in_dim(c_sorted, offset, per_group, 0)
        lse_part = lax.dynamic_slice_in_dim(served_lse, offset, per_group, 0)
        head_part = lax.dynamic_slice_in_dim(heads_sorted, offset, per_group, 0)
        part_dk, part_dv, part_dq = slot_grads(
            query_part, cot_part, shift_part, lse_part, head_part, k_heads, v_heads, scaling
        )
        head_onehot = (head_part[:, None] == group_ids[None, :]).astype(jnp.float32)
        grad_k = grad_k + jnp.einsum("ng,nkd->gkd", head_onehot, part_dk, precision=highest)
        grad_v = grad_v + jnp.einsum("ng,nkd->gkd", head_onehot, part_dv, precision=highest)
        served_dq = lax.dynamic_update_slice_in_dim(served_dq, part_dq, offset, 0)
        return (grad_k, grad_v, served_dq)

    zeros_heads = jnp.zeros((groups, row_count, head_dim), jnp.float32)
    start_bwd = (zeros_heads, zeros_heads, jnp.zeros((devices, head_dim, tile_rows), jnp.float32))
    rem_dk, rem_dv, served_dq = lax.fori_loop(0, rounds, backward_turn, start_bwd)
    back_dq = lax.all_to_all(
        jnp.take(served_dq, inverse, axis=0).astype(jnp.bfloat16),
        "ctx",
        split_axis=0,
        concat_axis=0,
        tiled=True,
    ).astype(jnp.float32)
    task_dq = jnp.take(back_dq, lookup, axis=0).reshape(
        tiles_dev, groups, others, head_dim, tile_rows
    )
    rem_dq = jnp.sum(jnp.where(active[..., None, None], task_dq, 0.0), axis=2)
    own_dq_t = own_dq.reshape(groups, tiles_dev, tile_rows, head_dim).transpose(1, 0, 2, 3)
    total_dq = own_dq_t + rem_dq.transpose(0, 1, 3, 2)
    grad_query = total_dq.transpose(0, 2, 1, 3).reshape(row_count, columns).astype(jnp.bfloat16)
    grad_key = (own_dk + rem_dk).transpose(1, 0, 2).reshape(row_count, columns).astype(jnp.bfloat16)
    grad_value = (
        (own_dv + rem_dv).transpose(1, 0, 2).reshape(row_count, columns).astype(jnp.bfloat16)
    )
    return (attn_out, grad_query, grad_key, grad_value)


def pair_parts(near, far, tiles_dev, tile_rows):
    for part in range(tiles_dev):
        rows = slice(part * tile_rows, (part + 1) * tile_rows)
        cols = slice(part * 2 * tile_rows, tiles_dev * 2 * tile_rows)
        yield near.at[:, rows, cols], far.at[:, rows, cols]


def dot_t(a, b):
    return lax.dot_general(a, b, (((1,), (1,)), ((), ())), preferred_element_type=jnp.float32)


def split_low(x):
    high = x.astype(jnp.bfloat16).astype(jnp.float32)
    return high, x - high


def halves(block, head_dim):
    lane = lax.broadcasted_iota(jnp.int32, block.shape, 1)
    zero = jnp.zeros_like(block)
    return jnp.where(lane < head_dim, block, zero), jnp.where(lane < head_dim, zero, block)


def pack_kernel(tiles_dev, groups, picked, tile_rows, head_dim, devices):
    def body(picks_ref, q_ref, g_ref, send_ref, task_ref):
        own = picks_ref[0, 0, 0]
        meta_rows = send_ref.shape[1] - tile_rows
        lanes = send_ref.shape[2]
        row = lax.broadcasted_iota(jnp.int32, (meta_rows, lanes), 0)
        blank = jnp.zeros((meta_rows, lanes), jnp.bfloat16)
        for peer in range(devices):
            send_ref[peer, tile_rows:, :] = blank
            task_ref[peer] = -1
        for tile in range(tiles_dev):
            rows = slice(tile * tile_rows, (tile + 1) * tile_rows)
            for head in range(groups):
                cols = slice(head * head_dim, (head + 1) * head_dim)
                block = jnp.concatenate([q_ref[rows, cols], g_ref[rows, cols]], axis=1)
                code = tile * groups + head
                meta = jnp.where(row == 0, code + 1, 0)
                for entry in range(1, picked):
                    meta = jnp.where(row == entry, picks_ref[tile, head, entry], meta)
                meta = meta.astype(jnp.float32).astype(jnp.bfloat16)
                for entry in range(1, picked):
                    target = picks_ref[tile, head, entry]
                    send_ref[target, :tile_rows, :] = block
                    send_ref[target, tile_rows:, :] = meta
                    task_ref[target] = code
        task_ref[own] = -1

    return body


def own_kernel(tiles_dev, groups, tile_rows, head_dim):
    scale = LOG2E / math.sqrt(head_dim)

    def body(q_hbm, k_hbm, v_hbm, g_hbm, kv_ref, vkt_ref, stat_ref, table_ref,
             q_ref, k_ref, v_ref, g_ref, in_sem):
        loads = [
            pltpu.make_async_copy(src, dst, in_sem.at[index])
            for index, (src, dst) in enumerate(((k_hbm, k_ref), (v_hbm, v_ref), (q_hbm, q_ref), (g_hbm, g_ref)))
        ]
        for load in loads:
            load.start()
        for load in loads:
            load.wait()
        sub = lax.broadcasted_iota(jnp.int32, (tile_rows, tile_rows), 0)
        lane = lax.broadcasted_iota(jnp.int32, (tile_rows, tile_rows), 1)
        causal = sub <= lane
        for head in range(groups):
            cols = slice(head * head_dim, (head + 1) * head_dim)
            kv_ref[head] = jnp.concatenate([k_ref[:, cols], v_ref[:, cols]], axis=1)

        def product(code):
            tile, head = code // groups, code % groups
            cols = slice(head * head_dim, (head + 1) * head_dim)
            rows = slice(tile * tile_rows, (tile + 1) * tile_rows)
            block = jnp.concatenate([q_ref[rows, cols], g_ref[rows, cols]], axis=1)
            return dot_t(kv_ref[head, : rows.stop, :], jnp.concatenate(halves(block, head_dim), axis=0))

        ahead = product(0)
        for code in range(tiles_dev * groups):
            both = ahead
            if code + 1 < tiles_dev * groups:
                ahead = product(code + 1)
            tile = code // groups
            split = tile * tile_rows
            last = jnp.where(causal, both[split:, :tile_rows], masked_value)
            peak = jnp.max(last, axis=0, keepdims=True)
            if tile:
                peak = jnp.maximum(peak, jnp.max(both[:split, :tile_rows], axis=0, keepdims=True))
            peak = peak * scale
            powers = jnp.exp2(last * scale - peak)
            total = jnp.sum(powers, axis=0, keepdims=True)
            mean_grad = jnp.sum(powers * both[split:, tile_rows:], axis=0, keepdims=True)
            if tile:
                powers = jnp.exp2(both[:split, :tile_rows] * scale - peak)
                total = total + jnp.sum(powers, axis=0, keepdims=True)
                mean_grad = mean_grad + jnp.sum(powers * both[:split, tile_rows:], axis=0, keepdims=True)
            inverse = 1.0 / total
            mean_grad = mean_grad * inverse
            lse = peak + jnp.log2(total)
            for index, value in enumerate((lse, mean_grad, inverse, peak)):
                stat_ref[index, code : code + 1, :] = value
            for index, value in enumerate(split_low(lse) + (mean_grad,)):
                table_ref[code, index : index + 1, :] = value
        for head in range(groups):
            cols = slice(head * head_dim, (head + 1) * head_dim)
            vkt_ref[head] = jnp.concatenate([v_ref[:, cols], k_ref[:, cols]], axis=1).T

    return body


def rest_kernel(tiles_dev, groups, tile_rows, head_dim):
    scale = LOG2E / math.sqrt(head_dim)

    def body(q_hbm, g_hbm, kv_ref, vkt_ref, stat_ref, qgt_hbm, mix_hbm, pd_hbm,
             q_ref, g_ref, qgt_ref, mix_ref, pd_ref, in_sem, out_sem):
        loads = [
            pltpu.make_async_copy(src, dst, in_sem.at[index])
            for index, (src, dst) in enumerate(((q_hbm, q_ref), (g_hbm, g_ref)))
        ]
        for load in loads:
            load.start()
        for load in loads:
            load.wait()
        sub = lax.broadcasted_iota(jnp.int32, (tile_rows, tile_rows), 0)
        lane = lax.broadcasted_iota(jnp.int32, (tile_rows, tile_rows), 1)
        causal = sub <= lane

        def product(code):
            tile, head = code // groups, code % groups
            cols = slice(head * head_dim, (head + 1) * head_dim)
            rows = slice(tile * tile_rows, (tile + 1) * tile_rows)
            block = jnp.concatenate([q_ref[rows, cols], g_ref[rows, cols]], axis=1)
            qgt_ref[head, :, rows] = block.T
            return dot_t(kv_ref[head, : rows.stop, :], jnp.concatenate(halves(block, head_dim), axis=0))

        ahead = product(0)
        for code in range(tiles_dev * groups):
            both = ahead
            if code + 1 < tiles_dev * groups:
                ahead = product(code + 1)
            tile, head = code // groups, code % groups
            span = (tile + 1) * tile_rows
            at = tile * 2 * tile_rows
            peak = stat_ref[3, code : code + 1, :]
            inverse = stat_ref[2, code : code + 1, :]
            for part in range(tile + 1):
                chunk = slice(part * tile_rows, (part + 1) * tile_rows)
                scores = both[chunk, :tile_rows]
                if part == tile:
                    scores = jnp.where(causal, scores, masked_value)
                powers = jnp.exp2(scores * scale - peak)
                spread = powers * both[chunk, tile_rows:]
                pd_ref[head, chunk, at : at + tile_rows] = powers.astype(jnp.bfloat16)
                pd_ref[head, chunk, at + tile_rows : at + 2 * tile_rows] = spread.astype(jnp.bfloat16)
            result = jnp.dot(vkt_ref[head, :, :span], pd_ref[head, :span, at : at + 2 * tile_rows],
                             preferred_element_type=jnp.float32)
            mix_ref[head, tile, : 2 * head_dim, :] = (result[:, :tile_rows] * inverse).astype(jnp.bfloat16)
            mix_ref[head, tile, 2 * head_dim :, :] = (result[head_dim:, tile_rows:] * inverse).astype(jnp.bfloat16)
        stores = [
            pltpu.make_async_copy(mix_ref, mix_hbm, out_sem.at[tiles_dev]),
            pltpu.make_async_copy(qgt_ref, qgt_hbm, out_sem.at[tiles_dev + 1]),
        ] + [
            pltpu.make_async_copy(src, dst, out_sem.at[index])
            for index, (src, dst) in enumerate(pair_parts(pd_ref, pd_hbm, tiles_dev, tile_rows))
        ]
        for store in stores:
            store.start()
        for store in stores:
            store.wait()

    return body


def parts_of(block, kv_head, tile_rows, head_dim, scale):
    both = dot_t(kv_head, jnp.concatenate(halves(block, head_dim), axis=0))
    scores = both[:, :tile_rows]
    peak = jnp.max(scores, axis=0, keepdims=True) * scale
    powers = jnp.exp2(scores * scale - peak)
    spread = powers * both[:, tile_rows:]
    return peak, powers, spread


def serve_kernel(groups, tile_rows, head_dim, devices):
    scale = LOG2E / math.sqrt(head_dim)

    def body(picks_ref, task_ref, recv_ref, kv_ref, vkt_ref, table_ref, send_hbm, inv_ref,
             send_ref, st_ref, out_sem):
        own = picks_ref[0, 0, 0]
        st_ref[...] = jnp.zeros_like(st_ref)
        inv_ref[...] = jnp.zeros_like(inv_ref)
        heads = [None]
        blocks = [None]
        for source in range(1, devices):
            code = jnp.max(recv_ref[source, tile_rows:, :].astype(jnp.float32)[0:1, :]).astype(jnp.int32) - 1
            block = recv_ref[source, :tile_rows, :]
            heads.append(lax.rem(jnp.maximum(code, 0), groups))
            blocks.append(jnp.where((code >= 0) & (own != source), block, jnp.zeros_like(block)))
        ahead = parts_of(blocks[1], kv_ref[heads[1]], tile_rows, head_dim, scale)
        for source in range(1, devices):
            peak, powers, spread = ahead
            if source + 1 < devices:
                ahead = parts_of(blocks[source + 1], kv_ref[heads[source + 1]], tile_rows, head_dim, scale)
            total = jnp.sum(powers, axis=0, keepdims=True)
            inverse = 1.0 / total
            mean_grad = jnp.sum(spread, axis=0, keepdims=True) * inverse
            both = jnp.concatenate([powers.astype(jnp.bfloat16), spread.astype(jnp.bfloat16)], axis=1)
            result = jnp.dot(vkt_ref[heads[source]], both, preferred_element_type=jnp.float32)
            send_ref[source, : 2 * head_dim, :] = (result[:, :tile_rows] * inverse).astype(jnp.bfloat16)
            send_ref[source, 2 * head_dim : 3 * head_dim, :] = (result[head_dim:, tile_rows:] * inverse).astype(jnp.bfloat16)
            parts = split_low(peak + jnp.log2(total)) + (mean_grad,)
            for index in range(3):
                st_ref[index * devices + source : index * devices + source + 1, :] = parts[index]
            inv_ref[0, source : source + 1, :] = inverse
            inv_ref[1, source : source + 1, :] = peak
        table = st_ref[...]
        row = lax.broadcasted_iota(jnp.int32, table.shape, 0)
        mine = lax.rem(row, devices) == own
        for peer in range(devices):
            code = jnp.maximum(task_ref[peer], 0)
            entry = table_ref[code]
            wide = jnp.concatenate(
                [jnp.broadcast_to(entry[index : index + 1], (devices, tile_rows)) for index in range(3)], axis=0
            )
            send_ref[peer, 3 * head_dim :, :] = jnp.where(mine, wide, table).astype(jnp.bfloat16)
        store = pltpu.make_async_copy(send_ref, send_hbm, out_sem)
        store.start()
        store.wait()

    return body


def again_kernel(groups, tile_rows, head_dim, devices):
    scale = LOG2E / math.sqrt(head_dim)

    def body(picks_ref, recv_ref, kv_ref, inv_ref, pd_ref, qgt_ref, meta_ref):
        own = picks_ref[0, 0, 0]
        for source in range(devices):
            meta_ref[source] = recv_ref[source, tile_rows:, :].astype(jnp.float32)
        codes = [jnp.max(recv_ref[source, tile_rows:, :].astype(jnp.float32)[0:1, :]).astype(jnp.int32) - 1
                 for source in range(devices)]

        def product(source):
            block = recv_ref[source, :tile_rows, :]
            block = jnp.where((codes[source] >= 0) & (own != source), block, jnp.zeros_like(block))
            qgt_ref[source - 1] = block.T
            head = lax.rem(jnp.maximum(codes[source], 0), groups)
            return dot_t(kv_ref[head], jnp.concatenate(halves(block, head_dim), axis=0))

        ahead = product(1)
        for source in range(1, devices):
            both = ahead
            if source + 1 < devices:
                ahead = product(source + 1)
            powers = jnp.exp2(both[:, :tile_rows] * scale - inv_ref[1, source : source + 1, :])
            pd_ref[source - 1, :, :tile_rows] = powers.astype(jnp.bfloat16)
            pd_ref[source - 1, :, tile_rows:] = (powers * both[:, tile_rows:]).astype(jnp.bfloat16)

    return body


def final_kernel(tiles_dev, groups, picked, tile_rows, head_dim, devices):
    scaling = 1.0 / math.sqrt(head_dim)
    pair = 2 * tile_rows

    def body(picks_ref, task_ref, meta_ref, back_ref, qgt_in_ref, stat_ref, inv_ref,
             pd_in_ref, qgt_hbm, mix_hbm, pd_hbm, out_hbm, dq_hbm, dk_hbm, dv_hbm,
             qgt_ref, mix_ref, pd_ref, out_ref, dq_ref, dk_ref, dv_ref, acc_ref, grad_ref, more_ref,
             lse_sc, gd_sc, w_sc, d_sc, x_ref, xin_ref, in_sem, out_sem):
        own = picks_ref[0, 0, 0]
        tasks = tiles_dev * groups
        base = 3 * head_dim
        loads = [
            pltpu.make_async_copy(mix_hbm, mix_ref, in_sem.at[tiles_dev]),
            pltpu.make_async_copy(qgt_hbm, qgt_ref, in_sem.at[tiles_dev + 1]),
        ] + [
            pltpu.make_async_copy(src, dst, in_sem.at[index])
            for index, (dst, src) in enumerate(pair_parts(pd_ref, pd_hbm, tiles_dev, tile_rows))
        ]
        for load in loads:
            load.start()
        grad_ref[...] = jnp.zeros_like(grad_ref)
        more_ref[...] = jnp.zeros_like(more_ref)
        for part in range(1, tiles_dev, 2):
            rows = slice(part * tile_rows, (part + 1) * tile_rows)
            pd_ref[:, rows, (part - 1) * pair : part * pair] = jnp.zeros((groups, tile_rows, pair), jnp.bfloat16)

        lse_of = []
        gd_of = []
        for peer in range(devices):
            table = back_ref[peer, base:, :].astype(jnp.float32)
            lse_of.append(table[:devices] + table[devices : 2 * devices])
            gd_of.append(table[2 * devices :])
            lse_sc[peer] = lse_of[peer]
            gd_sc[peer] = gd_of[peer]

        ids = lax.broadcasted_iota(jnp.int32, (devices, tile_rows), 0)
        metas = [meta_ref[source] for source in range(devices)]
        rows_of = [
            jnp.concatenate([metas[source][entry : entry + 1] for source in range(devices)], axis=0).astype(jnp.int32)
            for entry in range(picked)
        ]
        codes = [None] + [jnp.max(metas[source][0:1, :]).astype(jnp.int32) - 1 for source in range(1, devices)]
        live = (rows_of[0] > 0) & (ids != own)
        chosen = []
        for peer in range(devices):
            active = ids == peer
            for entry in rows_of[1:]:
                active = active | (entry == peer)
            chosen.append(active)
        peak = jnp.full((devices, tile_rows), masked_value, jnp.float32)
        for peer in range(devices):
            peak = jnp.maximum(peak, jnp.where(chosen[peer], lse_of[peer], masked_value))
        total = jnp.zeros_like(peak)
        delta = jnp.zeros_like(peak)
        for peer in range(devices):
            power = jnp.where(chosen[peer], jnp.exp2(lse_of[peer] - peak), 0.0)
            total = total + power
            delta = delta + jnp.where(chosen[peer], power * gd_of[peer], 0.0)
        delta = delta / total
        weight = jnp.exp2(lse_sc[own] - peak) / total * inv_ref[0]
        w_sc[0] = jnp.where(live, weight, 0.0)
        w_sc[1] = jnp.where(live, -weight * delta, 0.0)

        code_ids = lax.broadcasted_iota(jnp.int32, (tasks, tile_rows), 0)
        own_lse = stat_ref[0]
        own_gd = stat_ref[1]
        peak = own_lse
        rows_lse = [lse_sc[peer, pl.ds(own, 1), :] for peer in range(devices)]
        rows_gd = [gd_sc[peer, pl.ds(own, 1), :] for peer in range(devices)]
        for peer in range(devices):
            peak = jnp.maximum(peak, jnp.where(code_ids == task_ref[peer], rows_lse[peer], masked_value))
        own_power = jnp.exp2(own_lse - peak)
        total = own_power
        delta = own_power * own_gd
        for peer in range(devices):
            here = code_ids == task_ref[peer]
            power = jnp.where(here, jnp.exp2(rows_lse[peer] - peak), 0.0)
            total = total + power
            delta = delta + jnp.where(here, power * rows_gd[peer], 0.0)
        inverse = 1.0 / total
        delta = delta * inverse
        own_weight = own_power * inverse
        d_sc[0] = peak
        d_sc[1] = inverse
        d_sc[2] = delta
        d_sc[3] = own_weight
        d_sc[4] = own_weight * stat_ref[2]
        d_sc[5] = -own_weight * stat_ref[2] * delta
        d_sc[6] = -own_weight * delta

        nothing = jnp.zeros((head_dim, tile_rows), jnp.bfloat16)
        for source in range(1, devices):
            odd = lax.rem(jnp.maximum(codes[source], 0), 2) == 1
            first = w_sc[0, source : source + 1, :]
            second = w_sc[1, source : source + 1, :]
            turned = qgt_in_ref[source - 1].astype(jnp.float32)
            g_first = (turned[head_dim:] * first).astype(jnp.bfloat16)
            q_first = (turned[:head_dim] * first).astype(jnp.bfloat16)
            q_second = (turned[:head_dim] * second).astype(jnp.bfloat16)
            xin_ref[source, :head_dim, :tile_rows] = jnp.where(odd, q_second, g_first)
            xin_ref[source, :head_dim, tile_rows:] = jnp.where(odd, q_first, nothing)
            xin_ref[source, head_dim:, :tile_rows] = jnp.where(odd, g_first, q_second)
            xin_ref[source, head_dim:, tile_rows:] = jnp.where(odd, nothing, q_first)
        for source in range(1, devices):
            head = lax.rem(jnp.maximum(codes[source], 0), groups)
            target = grad_ref if source % 2 else more_ref
            target[head] += dot_t(pd_in_ref[source - 1], xin_ref[source])

        for load in loads[:2]:
            load.wait()
        for head in range(groups):
            v_rows = slice(0, head_dim) if head % 2 == 0 else slice(head_dim, 2 * head_dim)
            k_rows = slice(head_dim, 2 * head_dim) if head % 2 == 0 else slice(0, head_dim)
            for tile in range(tiles_dev):
                code = tile * groups + head
                first = d_sc[4, code : code + 1, :]
                second = d_sc[5, code : code + 1, :]
                turned = qgt_ref[head, :, tile * tile_rows : (tile + 1) * tile_rows].astype(jnp.float32)
                early = slice(tile * pair, tile * pair + tile_rows)
                late = slice(tile * pair + tile_rows, (tile + 1) * pair)
                x_ref[head, v_rows, early] = (turned[head_dim:] * first).astype(jnp.bfloat16)
                x_ref[head, v_rows, late] = nothing
                x_ref[head, k_rows, early] = (turned[:head_dim] * second).astype(jnp.bfloat16)
                x_ref[head, k_rows, late] = (turned[:head_dim] * first).astype(jnp.bfloat16)
        for head in range(groups):
            for tile in range(tiles_dev):
                code = tile * groups + head
                first = d_sc[3, code : code + 1, :]
                second = d_sc[6, code : code + 1, :]
                mix = mix_ref[head, tile].astype(jnp.float32)
                acc_ref[0, code] = mix[:head_dim] * first
                acc_ref[1, code] = mix[2 * head_dim :] * first + mix[head_dim : 2 * head_dim] * second

        def gather(peer, carry):
            code = task_ref[peer]

            @pl.when(code >= 0)
            def _():
                at = pl.ds(code, 1)
                part_w = jnp.exp2(lse_sc[peer, pl.ds(own, 1), :] - d_sc[0, at, :]) * d_sc[1, at, :]
                shift = -part_w * d_sc[2, at, :]
                mix = back_ref[peer, : 3 * head_dim, :].astype(jnp.float32)
                acc_ref[0, code] += mix[:head_dim] * part_w
                acc_ref[1, code] += mix[2 * head_dim :] * part_w + mix[head_dim : 2 * head_dim] * shift

            return carry

        lax.fori_loop(0, own, gather, 0)

        sub = lax.broadcasted_iota(jnp.int32, (tile_rows, tile_rows), 0)
        lane = lax.broadcasted_iota(jnp.int32, (tile_rows, tile_rows), 1)
        unit = jnp.where(sub == lane, 1.0, 0.0).astype(jnp.bfloat16)
        for tile in range(tiles_dev):
            rows = slice(tile * tile_rows, (tile + 1) * tile_rows)
            for head in range(0, groups, 2):
                cols = slice(head * head_dim, (head + 2) * head_dim)
                code = tile * groups + head
                both = jnp.concatenate([acc_ref[0, code], acc_ref[0, code + 1]], axis=0).astype(jnp.bfloat16)
                out_ref[rows, cols] = dot_t(unit, both).astype(jnp.bfloat16)
                both = jnp.concatenate([acc_ref[1, code], acc_ref[1, code + 1]], axis=0)
                dq_ref[rows, cols] = dot_t(unit, (both * scaling).astype(jnp.bfloat16)).astype(jnp.bfloat16)
        stores = [
            pltpu.make_async_copy(src, dst, out_sem.at[index])
            for index, (src, dst) in enumerate(((out_ref, out_hbm), (dq_ref, dq_hbm), (dk_ref, dk_hbm), (dv_ref, dv_hbm)))
        ]
        stores[0].start()
        stores[1].start()

        for load in loads[2:]:
            load.wait()
        half = 2 * tile_rows
        lane = lax.broadcasted_iota(jnp.int32, (half, 2 * head_dim), 1)
        for head in range(0, groups, 2):
            cols = slice(head * head_dim, (head + 2) * head_dim)
            for first in range(0, tiles_dev, 2):
                rows = slice(first * tile_rows, (first + 2) * tile_rows)
                even, odd = (
                    dot_t(pd_ref[h, rows, first * pair :], x_ref[h, :, first * pair :])
                    + grad_ref[h, rows, :]
                    + more_ref[h, rows, :]
                    for h in (head, head + 1)
                )
                dv_ref[rows, cols] = jnp.where(lane < head_dim, even, odd).astype(jnp.bfloat16)
                swapped = jnp.where(lane < head_dim, odd, even) * scaling
                dk_ref[rows, cols] = pltpu.roll(swapped, head_dim, 1).astype(jnp.bfloat16)
        stores[2].start()
        stores[3].start()
        for store in stores:
            store.wait()

    return body


def fast_local(query, key, value, grad_out, picks):
    row_count, columns = query.shape
    tiles_dev, groups, picked = picks.shape
    head_dim = columns // groups
    tile_rows = row_count // tiles_dev
    devices = lax.axis_size("ctx")
    tasks = tiles_dev * groups
    smem = pl.BlockSpec(memory_space=pltpu.SMEM)
    vmem = pl.BlockSpec(memory_space=pltpu.VMEM)
    far = pl.BlockSpec(memory_space=pltpu.HBM)
    low = jnp.bfloat16
    wide = jnp.float32
    width = 2 * head_dim
    shape = jax.ShapeDtypeStruct
    dma = pltpu.SemaphoreType.DMA
    small = pltpu.CompilerParams(vmem_limit_bytes=vmem_grant)
    near = pltpu.VMEM

    def away(*arrays):
        return tuple(pltpu.with_memory_space_constraint(x, pltpu.HBM) for x in arrays)

    def keep(*arrays):
        return tuple(pltpu.with_memory_space_constraint(x, pltpu.VMEM) for x in arrays)


    send_q, task_of = pl.pallas_call(
        pack_kernel(tiles_dev, groups, picked, tile_rows, head_dim, devices),
        out_shape=(shape((devices, tile_rows + 8, width), low), shape((devices,), jnp.int32)),
        in_specs=[smem, vmem, vmem],
        out_specs=(vmem, smem),
        name="pack",
    )(picks, query, grad_out)
    recv_q = lax.all_to_all(send_q, "ctx", split_axis=0, concat_axis=0, tiled=True)

    kv, vkt, stats, table = pl.pallas_call(
        own_kernel(tiles_dev, groups, tile_rows, head_dim),
        out_shape=(
            near((groups, row_count, width), low),
            near((groups, width, row_count), low),
            near((4, tasks, tile_rows), wide),
            near((tasks, 8, tile_rows), wide),
        ),
        in_specs=[far] * 4,
        out_specs=tuple([vmem] * 4),
        scratch_shapes=[pltpu.VMEM((row_count, columns), low)] * 4 + [dma((4,))],
        compiler_params=small,
        name="own",
    )(*away(query, key, value, grad_out))

    slot = 3 * head_dim + 3 * devices
    in_shape = (devices - 1, row_count, 2 * tile_rows)
    send_b, inverse_in = pl.pallas_call(
        serve_kernel(groups, tile_rows, head_dim, devices),
        out_shape=(pltpu.HBM((devices, slot, tile_rows), low), near((2, devices, tile_rows), wide)),
        in_specs=[smem, smem, vmem, vmem, vmem, vmem],
        out_specs=(far, vmem),
        scratch_shapes=[
            pltpu.VMEM((devices, slot, tile_rows), low),
            pltpu.VMEM((3 * devices, tile_rows), wide),
            dma(()),
        ],
        compiler_params=small,
        name="serve",
    )(*away(picks, task_of), *keep(recv_q, kv, vkt, table))
    recv_b = lax.all_to_all(send_b, "ctx", split_axis=0, concat_axis=0, tiled=True)

    pairs_in, qgt_in, lists_in = pl.pallas_call(
        again_kernel(groups, tile_rows, head_dim, devices),
        out_shape=(near(in_shape, low), near((devices - 1, width, tile_rows), low), near((devices, 8, width), wide)),
        in_specs=[smem, vmem, vmem, vmem],
        out_specs=(vmem, vmem, vmem),
        compiler_params=small,
        name="again",
    )(*away(picks), *keep(recv_q, kv, inverse_in))

    mix_shape = (groups, tiles_dev, 3 * head_dim, tile_rows)
    pair_shape = (groups, row_count, 2 * row_count)
    turned_shape = (groups, width, row_count)
    qgt, mix, pairs = pl.pallas_call(
        rest_kernel(tiles_dev, groups, tile_rows, head_dim),
        out_shape=(pltpu.HBM(turned_shape, low), pltpu.HBM(mix_shape, low), pltpu.HBM(pair_shape, low)),
        in_specs=[far] * 2 + [vmem] * 3,
        out_specs=tuple([far] * 3),
        scratch_shapes=[pltpu.VMEM((row_count, columns), low)] * 2
        + [
            pltpu.VMEM(turned_shape, low),
            pltpu.VMEM(mix_shape, low),
            pltpu.VMEM(pair_shape, low),
            dma((2,)),
            dma((tiles_dev + 2,)),
        ],
        compiler_params=small,
        name="rest",
    )(*away(query, grad_out), *keep(kv, vkt, stats))

    return pl.pallas_call(
        final_kernel(tiles_dev, groups, picked, tile_rows, head_dim, devices),
        out_shape=tuple([shape((row_count, columns), low)] * 4),
        in_specs=[smem, smem] + [vmem] * 6 + [far] * 3,
        out_specs=tuple([far] * 4),
        scratch_shapes=[
            pltpu.VMEM((groups, width, row_count), low),
            pltpu.VMEM(mix_shape, low),
            pltpu.VMEM(pair_shape, low),
        ]
        + [pltpu.VMEM((row_count, columns), low)] * 4
        + [
            pltpu.VMEM((2, tasks, head_dim, tile_rows), wide),
            pltpu.VMEM((groups, row_count, width), wide),
            pltpu.VMEM((groups, row_count, width), wide),
            pltpu.VMEM((devices, devices, tile_rows), wide),
            pltpu.VMEM((devices, devices, tile_rows), wide),
            pltpu.VMEM((2, devices, tile_rows), wide),
            pltpu.VMEM((7, tasks, tile_rows), wide),
            pltpu.VMEM((groups, width, 2 * row_count), low),
            pltpu.VMEM((devices, width, 2 * tile_rows), low),
            dma((tiles_dev + 2,)),
            dma((4,)),
        ],
        compiler_params=small,
        name="final",
    )(*away(picks, task_of), *keep(lists_in, recv_b, qgt_in, stats, inverse_in, pairs_in), *away(qgt, mix, pairs))


def choose(query, key, value, grad_out, picks):
    pair_bytes = lax.axis_size("ctx") * query.shape[0] * (query.shape[0] // picks.shape[0]) * 4
    plan = fast_local if pair_bytes <= pair_budget else local
    return plan(query, key, value, grad_out, picks)


def solution(mesh):
    placed = (
        P("ctx", "head"),
        P("ctx", "head"),
        P("ctx", "head"),
        P("ctx", "head"),
        P("ctx", "head", None),
    )
    return jax.shard_map(
        choose,
        mesh=mesh,
        in_specs=placed,
        out_specs=(P("ctx", "head"), P("ctx", "head"), P("ctx", "head"), P("ctx", "head")),
        check_vma=False,
    )
```

```python
import math

import jax
import jax.numpy as jnp
from jax import lax
from jax.experimental import pallas as pl
from jax.experimental.pallas import tpu as pltpu
from jax.sharding import PartitionSpec as P

masked_value = -1e30
highest = lax.Precision.HIGHEST
LOG2E = math.log2(math.e)
pair_budget = 8 << 20
vmem_grant = 32 << 20


def attend_slots(q_slots, head_ids, k_heads, v_heads, scaling):
    key_rows = jnp.take(k_heads, head_ids, axis=0)
    value_rows = jnp.take(v_heads, head_ids, axis=0)
    scores = (
        jnp.einsum("ndq,nkd->nqk", q_slots, key_rows, preferred_element_type=jnp.float32) * scaling
    )
    peak_score = jnp.max(scores, axis=-1, keepdims=True)
    log_total = peak_score + jnp.log(jnp.sum(jnp.exp(scores - peak_score), axis=-1, keepdims=True))
    attend_low = jnp.exp(scores - log_total).astype(jnp.bfloat16)
    outputs = jnp.einsum("nqk,nkd->ndq", attend_low, value_rows, preferred_element_type=jnp.float32)
    return (outputs, log_total[..., 0])


def slot_grads(q_slots, g_slots, c_slots, lse_slots, head_ids, k_heads, v_heads, scaling):
    key_rows = jnp.take(k_heads, head_ids, axis=0)
    value_rows = jnp.take(v_heads, head_ids, axis=0)
    scores = (
        jnp.einsum("ndq,nkd->nqk", q_slots, key_rows, preferred_element_type=jnp.float32) * scaling
    )
    attend = jnp.exp(scores - lse_slots[..., None])
    attend_low = attend.astype(jnp.bfloat16)
    grad_v = jnp.einsum("nqk,ndq->nkd", attend_low, g_slots, preferred_element_type=jnp.float32)
    grad_prob = jnp.einsum("ndq,nkd->nqk", g_slots, value_rows, preferred_element_type=jnp.float32)
    dscore = (attend * (grad_prob - c_slots[..., None])).astype(jnp.bfloat16)
    grad_k = (
        jnp.einsum("nqk,ndq->nkd", dscore, q_slots, preferred_element_type=jnp.float32) * scaling
    )
    grad_q = (
        jnp.einsum("nqk,nkd->ndq", dscore, key_rows, preferred_element_type=jnp.float32) * scaling
    )
    return (grad_k, grad_v, grad_q)


def local(query, key, value, grad_out, picks):
    row_count, columns = query.shape
    tiles_dev, groups, picked = picks.shape
    head_dim = columns // groups
    tile_rows = row_count // tiles_dev
    others = picked - 1
    scaling = 1.0 / math.sqrt(head_dim)
    devices = lax.axis_size("ctx")
    own_block = lax.axis_index("ctx")
    per_group = min(8, devices)
    all_picks = lax.all_gather(picks, "ctx", axis=0, tiled=True)
    q_heads = query.reshape(row_count, groups, head_dim).transpose(1, 0, 2)
    k_heads = key.reshape(row_count, groups, head_dim).transpose(1, 0, 2)
    v_heads = value.reshape(row_count, groups, head_dim).transpose(1, 0, 2)
    q_tiles = query.reshape(tiles_dev, tile_rows, groups, head_dim)
    do_tiles = grad_out.reshape(tiles_dev, tile_rows, groups, head_dim)
    do_major = do_tiles.transpose(0, 2, 1, 3)
    positions = jnp.arange(row_count, dtype=jnp.int32)
    tile_masks = []
    for tile_step in range(tiles_dev):
        span = (tile_step + 1) * tile_rows
        query_pos = positions[tile_step * tile_rows : span]
        tile_masks.append(positions[None, :span] <= query_pos[:, None])
    targets = picks[:, :, 1:]
    active = targets != own_block
    lookup = jnp.where(active, targets, own_block).reshape(-1)
    peer_ids = jnp.arange(devices, dtype=jnp.int32)
    routing = ((targets[None] == peer_ids[:, None, None, None]) & active[None]).astype(jnp.float32)
    routing_low = routing.astype(jnp.bfloat16)
    send_q = jnp.einsum(
        "jtgi,tqgd->jdq", routing_low, q_tiles, preferred_element_type=jnp.float32
    ).astype(jnp.bfloat16)
    recv_q = lax.all_to_all(send_q, "ctx", split_axis=0, concat_axis=0, tiled=True)

    def own_forward(inputs):
        q_head, k_head, v_head = inputs
        out_list = []
        lse_list = []
        for tile_step in range(tiles_dev):
            span = (tile_step + 1) * tile_rows
            q_part = q_head[tile_step * tile_rows : span]
            scores = (
                jnp.einsum("qd,kd->qk", q_part, k_head[:span], preferred_element_type=jnp.float32)
                * scaling
            )
            scores = jnp.where(tile_masks[tile_step], scores, masked_value)
            peak_score = jnp.max(scores, axis=-1, keepdims=True)
            log_total = peak_score + jnp.log(
                jnp.sum(jnp.exp(scores - peak_score), axis=-1, keepdims=True)
            )
            attend_low = jnp.exp(scores - log_total).astype(jnp.bfloat16)
            out_list.append(jnp.dot(attend_low, v_head[:span], preferred_element_type=jnp.float32))
            lse_list.append(log_total[:, 0])
        return (jnp.concatenate(out_list, axis=0), jnp.concatenate(lse_list, axis=0))

    own_out, own_lse = lax.map(own_forward, (q_heads, k_heads, v_heads))
    sources = all_picks.reshape(devices, tiles_dev, groups, picked)[..., 1:]
    incoming = (sources == own_block) & (peer_ids[:, None, None, None] != own_block)
    live_in = jnp.any(incoming, axis=(1, 2, 3))
    group_ids = jnp.arange(groups, dtype=jnp.int32)
    head_of = jnp.sum(jnp.where(incoming, group_ids[None, None, :, None], 0), axis=(1, 2, 3))
    ranking = jnp.argsort(jnp.where(live_in, 0, 1) * devices + peer_ids)
    inverse = jnp.argsort(ranking)
    rounds = (jnp.sum(live_in.astype(jnp.int32)) + per_group - 1) // per_group
    heads_sorted = jnp.take(head_of, ranking, axis=0)
    q_sorted = jnp.take(recv_q, ranking, axis=0)

    def forward_turn(turn, totals):
        served_out, served_lse = totals
        offset = turn * per_group
        query_part = lax.dynamic_slice_in_dim(q_sorted, offset, per_group, 0)
        head_part = lax.dynamic_slice_in_dim(heads_sorted, offset, per_group, 0)
        out_part, lse_part = attend_slots(query_part, head_part, k_heads, v_heads, scaling)
        served_out = lax.dynamic_update_slice_in_dim(served_out, out_part, offset, 0)
        served_lse = lax.dynamic_update_slice_in_dim(served_lse, lse_part, offset, 0)
        return (served_out, served_lse)

    start_fwd = (
        jnp.zeros((devices, head_dim, tile_rows), jnp.float32),
        jnp.zeros((devices, tile_rows), jnp.float32),
    )
    served_out, served_lse = lax.fori_loop(0, rounds, forward_turn, start_fwd)
    back_out, back_lse = (
        lax.all_to_all(
            jnp.take(served_out, inverse, axis=0), "ctx", split_axis=0, concat_axis=0, tiled=True
        ),
        lax.all_to_all(
            jnp.take(served_lse, inverse, axis=0), "ctx", split_axis=0, concat_axis=0, tiled=True
        ),
    )
    task_out = jnp.take(back_out, lookup, axis=0).reshape(
        tiles_dev, groups, others, head_dim, tile_rows
    )
    task_lse = jnp.take(back_lse, lookup, axis=0).reshape(tiles_dev, groups, others, tile_rows)
    own_out_t = own_out.reshape(groups, tiles_dev, tile_rows, head_dim).transpose(1, 0, 2, 3)
    own_lse_t = own_lse.reshape(groups, tiles_dev, tile_rows).transpose(1, 0, 2)
    active_rows = active[..., None]
    rem_lse = jnp.where(active_rows, task_lse, masked_value)
    ceiling = jnp.maximum(own_lse_t, jnp.max(rem_lse, axis=2))
    log_total = ceiling + jnp.log(
        jnp.exp(own_lse_t - ceiling) + jnp.sum(jnp.exp(rem_lse - ceiling[:, :, None]), axis=2)
    )
    own_weight = jnp.exp(own_lse_t - log_total)
    rem_weight = jnp.where(active_rows, jnp.exp(rem_lse - log_total[:, :, None]), 0.0)
    mixed = own_weight[..., None] * own_out_t + jnp.einsum(
        "tgiq,tgidq->tgqd", rem_weight, task_out, precision=highest
    )
    out_low = mixed.astype(jnp.bfloat16)
    attn_out = out_low.transpose(0, 2, 1, 3).reshape(row_count, columns)
    row_delta = jnp.sum(do_major.astype(jnp.float32) * out_low.astype(jnp.float32), axis=-1)
    own_scaled = (own_weight[..., None] * do_major.astype(jnp.float32)).astype(jnp.bfloat16)
    own_shift = own_weight * row_delta
    g_heads = own_scaled.transpose(1, 0, 2, 3).reshape(groups, row_count, head_dim)
    c_heads = own_shift.transpose(1, 0, 2).reshape(groups, row_count)

    def own_backward(inputs):
        q_head, k_head, v_head, g_head, c_head, lse_head = inputs
        grad_k = jnp.zeros((row_count, head_dim), jnp.float32)
        grad_v = jnp.zeros((row_count, head_dim), jnp.float32)
        dq_list = []
        for tile_step in range(tiles_dev):
            first = tile_step * tile_rows
            span = (tile_step + 1) * tile_rows
            q_part = q_head[first:span]
            g_part = g_head[first:span]
            k_part = k_head[:span]
            scores = (
                jnp.einsum("qd,kd->qk", q_part, k_part, preferred_element_type=jnp.float32)
                * scaling
            )
            scores = jnp.where(tile_masks[tile_step], scores, masked_value)
            attend = jnp.exp(scores - lse_head[first:span, None])
            attend_low = attend.astype(jnp.bfloat16)
            part_dv = jnp.einsum(
                "qk,qd->kd", attend_low, g_part, preferred_element_type=jnp.float32
            )
            grad_prob = jnp.einsum(
                "qd,kd->qk", g_part, v_head[:span], preferred_element_type=jnp.float32
            )
            dscore = (attend * (grad_prob - c_head[first:span, None])).astype(jnp.bfloat16)
            part_dk = (
                jnp.einsum("qk,qd->kd", dscore, q_part, preferred_element_type=jnp.float32)
                * scaling
            )
            dq_list.append(jnp.dot(dscore, k_part, preferred_element_type=jnp.float32) * scaling)
            padding = ((0, row_count - span), (0, 0))
            grad_k = grad_k + jnp.pad(part_dk, padding)
            grad_v = grad_v + jnp.pad(part_dv, padding)
        return (grad_k, grad_v, jnp.concatenate(dq_list, axis=0))

    own_dk, own_dv, own_dq = lax.map(
        own_backward, (q_heads, k_heads, v_heads, g_heads, c_heads, own_lse)
    )
    rem_shift = rem_weight * row_delta[:, :, None]
    rem_scaled = (rem_weight[..., None] * do_major[:, :, None].astype(jnp.float32)).astype(
        jnp.bfloat16
    )
    send_g = jnp.einsum(
        "jtgi,tgiqd->jdq", routing_low, rem_scaled, preferred_element_type=jnp.float32
    )
    send_c = jnp.einsum("jtgi,tgiq->jq", routing, rem_shift, precision=highest)
    recv_g, recv_c = (
        lax.all_to_all(send_g, "ctx", split_axis=0, concat_axis=0, tiled=True),
        lax.all_to_all(send_c, "ctx", split_axis=0, concat_axis=0, tiled=True),
    )
    g_sorted = jnp.take(recv_g, ranking, axis=0).astype(jnp.bfloat16)
    c_sorted = jnp.take(recv_c, ranking, axis=0)

    def backward_turn(turn, totals):
        grad_k, grad_v, served_dq = totals
        offset = turn * per_group
        query_part = lax.dynamic_slice_in_dim(q_sorted, offset, per_group, 0)
        cot_part = lax.dynamic_slice_in_dim(g_sorted, offset, per_group, 0)
        shift_part = lax.dynamic_slice_in_dim(c_sorted, offset, per_group, 0)
        lse_part = lax.dynamic_slice_in_dim(served_lse, offset, per_group, 0)
        head_part = lax.dynamic_slice_in_dim(heads_sorted, offset, per_group, 0)
        part_dk, part_dv, part_dq = slot_grads(
            query_part, cot_part, shift_part, lse_part, head_part, k_heads, v_heads, scaling
        )
        head_onehot = (head_part[:, None] == group_ids[None, :]).astype(jnp.float32)
        grad_k = grad_k + jnp.einsum("ng,nkd->gkd", head_onehot, part_dk, precision=highest)
        grad_v = grad_v + jnp.einsum("ng,nkd->gkd", head_onehot, part_dv, precision=highest)
        served_dq = lax.dynamic_update_slice_in_dim(served_dq, part_dq, offset, 0)
        return (grad_k, grad_v, served_dq)

    zeros_heads = jnp.zeros((groups, row_count, head_dim), jnp.float32)
    start_bwd = (zeros_heads, zeros_heads, jnp.zeros((devices, head_dim, tile_rows), jnp.float32))
    rem_dk, rem_dv, served_dq = lax.fori_loop(0, rounds, backward_turn, start_bwd)
    back_dq = lax.all_to_all(
        jnp.take(served_dq, inverse, axis=0).astype(jnp.bfloat16),
        "ctx",
        split_axis=0,
        concat_axis=0,
        tiled=True,
    ).astype(jnp.float32)
    task_dq = jnp.take(back_dq, lookup, axis=0).reshape(
        tiles_dev, groups, others, head_dim, tile_rows
    )
    rem_dq = jnp.sum(jnp.where(active[..., None, None], task_dq, 0.0), axis=2)
    own_dq_t = own_dq.reshape(groups, tiles_dev, tile_rows, head_dim).transpose(1, 0, 2, 3)
    total_dq = own_dq_t + rem_dq.transpose(0, 1, 3, 2)
    grad_query = total_dq.transpose(0, 2, 1, 3).reshape(row_count, columns).astype(jnp.bfloat16)
    grad_key = (own_dk + rem_dk).transpose(1, 0, 2).reshape(row_count, columns).astype(jnp.bfloat16)
    grad_value = (
        (own_dv + rem_dv).transpose(1, 0, 2).reshape(row_count, columns).astype(jnp.bfloat16)
    )
    return (attn_out, grad_query, grad_key, grad_value)


def pair_parts(near, far, tiles_dev, tile_rows):
    for part in range(tiles_dev):
        rows = slice(part * tile_rows, (part + 1) * tile_rows)
        cols = slice(part * 2 * tile_rows, tiles_dev * 2 * tile_rows)
        yield near.at[:, rows, cols], far.at[:, rows, cols]


def dot_t(a, b):
    return lax.dot_general(a, b, (((1,), (1,)), ((), ())), preferred_element_type=jnp.float32)


def split_low(x):
    high = x.astype(jnp.bfloat16).astype(jnp.float32)
    return high, x - high


def halves(block, head_dim):
    lane = lax.broadcasted_iota(jnp.int32, block.shape, 1)
    zero = jnp.zeros_like(block)
    return jnp.where(lane < head_dim, block, zero), jnp.where(lane < head_dim, zero, block)


def pack_kernel(tiles_dev, groups, picked, tile_rows, head_dim, devices):
    def body(picks_ref, q_ref, g_ref, send_ref, task_ref):
        own = picks_ref[0, 0, 0]
        meta_rows = send_ref.shape[1] - tile_rows
        lanes = send_ref.shape[2]
        row = lax.broadcasted_iota(jnp.int32, (meta_rows, lanes), 0)
        blank = jnp.zeros((meta_rows, lanes), jnp.bfloat16)
        for peer in range(devices):
            send_ref[peer, tile_rows:, :] = blank
            task_ref[peer] = -1
        for tile in range(tiles_dev):
            rows = slice(tile * tile_rows, (tile + 1) * tile_rows)
            for head in range(groups):
                cols = slice(head * head_dim, (head + 1) * head_dim)
                block = jnp.concatenate([q_ref[rows, cols], g_ref[rows, cols]], axis=1)
                code = tile * groups + head
                meta = jnp.where(row == 0, code + 1, 0)
                for entry in range(1, picked):
                    meta = jnp.where(row == entry, picks_ref[tile, head, entry], meta)
                meta = meta.astype(jnp.float32).astype(jnp.bfloat16)
                for entry in range(1, picked):
                    target = picks_ref[tile, head, entry]
                    send_ref[target, :tile_rows, :] = block
                    send_ref[target, tile_rows:, :] = meta
                    task_ref[target] = code
        task_ref[own] = -1

    return body


def own_kernel(tiles_dev, groups, tile_rows, head_dim):
    scale = LOG2E / math.sqrt(head_dim)

    def body(q_hbm, k_hbm, v_hbm, g_hbm, kv_ref, vkt_ref, stat_ref, table_ref,
             q_ref, k_ref, v_ref, g_ref, in_sem):
        loads = [
            pltpu.make_async_copy(src, dst, in_sem.at[index])
            for index, (src, dst) in enumerate(((k_hbm, k_ref), (v_hbm, v_ref), (q_hbm, q_ref), (g_hbm, g_ref)))
        ]
        for load in loads:
            load.start()
        for load in loads:
            load.wait()
        sub = lax.broadcasted_iota(jnp.int32, (tile_rows, tile_rows), 0)
        lane = lax.broadcasted_iota(jnp.int32, (tile_rows, tile_rows), 1)
        causal = sub <= lane
        for head in range(groups):
            cols = slice(head * head_dim, (head + 1) * head_dim)
            kv_ref[head] = jnp.concatenate([k_ref[:, cols], v_ref[:, cols]], axis=1)

        def product(code):
            tile, head = code // groups, code % groups
            cols = slice(head * head_dim, (head + 1) * head_dim)
            rows = slice(tile * tile_rows, (tile + 1) * tile_rows)
            block = jnp.concatenate([q_ref[rows, cols], g_ref[rows, cols]], axis=1)
            return dot_t(kv_ref[head, : rows.stop, :], jnp.concatenate(halves(block, head_dim), axis=0))

        ahead = product(0)
        for code in range(tiles_dev * groups):
            both = ahead
            if code + 1 < tiles_dev * groups:
                ahead = product(code + 1)
            tile = code // groups
            split = tile * tile_rows
            last = jnp.where(causal, both[split:, :tile_rows], masked_value)
            peak = jnp.max(last, axis=0, keepdims=True)
            if tile:
                peak = jnp.maximum(peak, jnp.max(both[:split, :tile_rows], axis=0, keepdims=True))
            peak = peak * scale
            powers = jnp.exp2(last * scale - peak)
            total = jnp.sum(powers, axis=0, keepdims=True)
            mean_grad = jnp.sum(powers * both[split:, tile_rows:], axis=0, keepdims=True)
            if tile:
                powers = jnp.exp2(both[:split, :tile_rows] * scale - peak)
                total = total + jnp.sum(powers, axis=0, keepdims=True)
                mean_grad = mean_grad + jnp.sum(powers * both[:split, tile_rows:], axis=0, keepdims=True)
            inverse = 1.0 / total
            mean_grad = mean_grad * inverse
            lse = peak + jnp.log2(total)
            for index, value in enumerate((lse, mean_grad, inverse, peak)):
                stat_ref[index, code : code + 1, :] = value
            for index, value in enumerate(split_low(lse) + (mean_grad,)):
                table_ref[code, index : index + 1, :] = value
        for head in range(groups):
            cols = slice(head * head_dim, (head + 1) * head_dim)
            vkt_ref[head] = jnp.concatenate([v_ref[:, cols], k_ref[:, cols]], axis=1).T

    return body


def rest_kernel(tiles_dev, groups, tile_rows, head_dim):
    scale = LOG2E / math.sqrt(head_dim)

    def body(q_hbm, g_hbm, kv_ref, vkt_ref, stat_ref, qgt_hbm, mix_hbm, pd_hbm,
             q_ref, g_ref, qgt_ref, mix_ref, pd_ref, in_sem, out_sem):
        loads = [
            pltpu.make_async_copy(src, dst, in_sem.at[index])
            for index, (src, dst) in enumerate(((q_hbm, q_ref), (g_hbm, g_ref)))
        ]
        for load in loads:
            load.start()
        for load in loads:
            load.wait()
        sub = lax.broadcasted_iota(jnp.int32, (tile_rows, tile_rows), 0)
        lane = lax.broadcasted_iota(jnp.int32, (tile_rows, tile_rows), 1)
        causal = sub <= lane

        def product(code):
            tile, head = code // groups, code % groups
            cols = slice(head * head_dim, (head + 1) * head_dim)
            rows = slice(tile * tile_rows, (tile + 1) * tile_rows)
            block = jnp.concatenate([q_ref[rows, cols], g_ref[rows, cols]], axis=1)
            qgt_ref[head, :, rows] = block.T
            return dot_t(kv_ref[head, : rows.stop, :], jnp.concatenate(halves(block, head_dim), axis=0))

        ahead = product(0)
        for code in range(tiles_dev * groups):
            both = ahead
            if code + 1 < tiles_dev * groups:
                ahead = product(code + 1)
            tile, head = code // groups, code % groups
            span = (tile + 1) * tile_rows
            at = tile * 2 * tile_rows
            peak = stat_ref[3, code : code + 1, :]
            inverse = stat_ref[2, code : code + 1, :]
            for part in range(tile + 1):
                chunk = slice(part * tile_rows, (part + 1) * tile_rows)
                scores = both[chunk, :tile_rows]
                if part == tile:
                    scores = jnp.where(causal, scores, masked_value)
                powers = jnp.exp2(scores * scale - peak)
                spread = powers * both[chunk, tile_rows:]
                pd_ref[head, chunk, at : at + tile_rows] = powers.astype(jnp.bfloat16)
                pd_ref[head, chunk, at + tile_rows : at + 2 * tile_rows] = spread.astype(jnp.bfloat16)
            result = jnp.dot(vkt_ref[head, :, :span], pd_ref[head, :span, at : at + 2 * tile_rows],
                             preferred_element_type=jnp.float32)
            mix_ref[head, tile, : 2 * head_dim, :] = (result[:, :tile_rows] * inverse).astype(jnp.bfloat16)
            mix_ref[head, tile, 2 * head_dim :, :] = (result[head_dim:, tile_rows:] * inverse).astype(jnp.bfloat16)
        stores = [
            pltpu.make_async_copy(mix_ref, mix_hbm, out_sem.at[tiles_dev]),
            pltpu.make_async_copy(qgt_ref, qgt_hbm, out_sem.at[tiles_dev + 1]),
        ] + [
            pltpu.make_async_copy(src, dst, out_sem.at[index])
            for index, (src, dst) in enumerate(pair_parts(pd_ref, pd_hbm, tiles_dev, tile_rows))
        ]
        for store in stores:
            store.start()
        for store in stores:
            store.wait()

    return body


def parts_of(block, kv_head, tile_rows, head_dim, scale):
    both = dot_t(kv_head, jnp.concatenate(halves(block, head_dim), axis=0))
    scores = both[:, :tile_rows]
    peak = jnp.max(scores, axis=0, keepdims=True) * scale
    powers = jnp.exp2(scores * scale - peak)
    spread = powers * both[:, tile_rows:]
    return peak, powers, spread


def serve_kernel(groups, tile_rows, head_dim, devices):
    scale = LOG2E / math.sqrt(head_dim)

    def body(picks_ref, task_ref, recv_ref, kv_ref, vkt_ref, table_ref, send_hbm, inv_ref,
             send_ref, st_ref, out_sem):
        own = picks_ref[0, 0, 0]
        st_ref[...] = jnp.zeros_like(st_ref)
        inv_ref[...] = jnp.zeros_like(inv_ref)
        heads = [None]
        blocks = [None]
        for source in range(1, devices):
            code = jnp.max(recv_ref[source, tile_rows:, :].astype(jnp.float32)[0:1, :]).astype(jnp.int32) - 1
            block = recv_ref[source, :tile_rows, :]
            heads.append(lax.rem(jnp.maximum(code, 0), groups))
            blocks.append(jnp.where((code >= 0) & (own != source), block, jnp.zeros_like(block)))
        ahead = parts_of(blocks[1], kv_ref[heads[1]], tile_rows, head_dim, scale)
        for source in range(1, devices):
            peak, powers, spread = ahead
            if source + 1 < devices:
                ahead = parts_of(blocks[source + 1], kv_ref[heads[source + 1]], tile_rows, head_dim, scale)
            total = jnp.sum(powers, axis=0, keepdims=True)
            inverse = 1.0 / total
            mean_grad = jnp.sum(spread, axis=0, keepdims=True) * inverse
            both = jnp.concatenate([powers.astype(jnp.bfloat16), spread.astype(jnp.bfloat16)], axis=1)
            result = jnp.dot(vkt_ref[heads[source]], both, preferred_element_type=jnp.float32)
            send_ref[source, : 2 * head_dim, :] = (result[:, :tile_rows] * inverse).astype(jnp.bfloat16)
            send_ref[source, 2 * head_dim : 3 * head_dim, :] = (result[head_dim:, tile_rows:] * inverse).astype(jnp.bfloat16)
            parts = split_low(peak + jnp.log2(total)) + (mean_grad,)
            for index in range(3):
                st_ref[index * devices + source : index * devices + source + 1, :] = parts[index]
            inv_ref[0, source : source + 1, :] = inverse
            inv_ref[1, source : source + 1, :] = peak
        table = st_ref[...]
        row = lax.broadcasted_iota(jnp.int32, table.shape, 0)
        mine = lax.rem(row, devices) == own
        for peer in range(devices):
            code = jnp.maximum(task_ref[peer], 0)
            entry = table_ref[code]
            wide = jnp.concatenate(
                [jnp.broadcast_to(entry[index : index + 1], (devices, tile_rows)) for index in range(3)], axis=0
            )
            send_ref[peer, 3 * head_dim :, :] = jnp.where(mine, wide, table).astype(jnp.bfloat16)
        store = pltpu.make_async_copy(send_ref, send_hbm, out_sem)
        store.start()
        store.wait()

    return body


def again_kernel(groups, tile_rows, head_dim, devices):
    scale = LOG2E / math.sqrt(head_dim)

    def body(picks_ref, recv_ref, kv_ref, inv_ref, pd_ref, qgt_ref, meta_ref):
        own = picks_ref[0, 0, 0]
        for source in range(devices):
            meta_ref[source] = recv_ref[source, tile_rows:, :].astype(jnp.float32)
        codes = [jnp.max(recv_ref[source, tile_rows:, :].astype(jnp.float32)[0:1, :]).astype(jnp.int32) - 1
                 for source in range(devices)]

        def product(source):
            block = recv_ref[source, :tile_rows, :]
            block = jnp.where((codes[source] >= 0) & (own != source), block, jnp.zeros_like(block))
            qgt_ref[source - 1] = block.T
            head = lax.rem(jnp.maximum(codes[source], 0), groups)
            return dot_t(kv_ref[head], jnp.concatenate(halves(block, head_dim), axis=0))

        ahead = product(1)
        for source in range(1, devices):
            both = ahead
            if source + 1 < devices:
                ahead = product(source + 1)
            powers = jnp.exp2(both[:, :tile_rows] * scale - inv_ref[1, source : source + 1, :])
            pd_ref[source - 1, :, :tile_rows] = powers.astype(jnp.bfloat16)
            pd_ref[source - 1, :, tile_rows:] = (powers * both[:, tile_rows:]).astype(jnp.bfloat16)

    return body


def final_kernel(tiles_dev, groups, picked, tile_rows, head_dim, devices):
    scaling = 1.0 / math.sqrt(head_dim)
    pair = 2 * tile_rows

    def body(picks_ref, task_ref, meta_ref, back_ref, qgt_in_ref, stat_ref, inv_ref,
             pd_in_ref, qgt_hbm, mix_hbm, pd_hbm, out_hbm, dq_hbm, dk_hbm, dv_hbm,
             qgt_ref, mix_ref, pd_ref, out_ref, dq_ref, dk_ref, dv_ref, acc_ref, grad_ref, more_ref,
             lse_sc, gd_sc, w_sc, d_sc, x_ref, xin_ref, in_sem, out_sem):
        own = picks_ref[0, 0, 0]
        tasks = tiles_dev * groups
        base = 3 * head_dim
        loads = [
            pltpu.make_async_copy(mix_hbm, mix_ref, in_sem.at[tiles_dev]),
            pltpu.make_async_copy(qgt_hbm, qgt_ref, in_sem.at[tiles_dev + 1]),
        ] + [
            pltpu.make_async_copy(src, dst, in_sem.at[index])
            for index, (dst, src) in enumerate(pair_parts(pd_ref, pd_hbm, tiles_dev, tile_rows))
        ]
        for load in loads:
            load.start()
        grad_ref[...] = jnp.zeros_like(grad_ref)
        more_ref[...] = jnp.zeros_like(more_ref)

        lse_of = []
        gd_of = []
        for peer in range(devices):
            table = back_ref[peer, base:, :].astype(jnp.float32)
            lse_of.append(table[:devices] + table[devices : 2 * devices])
            gd_of.append(table[2 * devices :])
            lse_sc[peer] = lse_of[peer]
            gd_sc[peer] = gd_of[peer]

        ids = lax.broadcasted_iota(jnp.int32, (devices, tile_rows), 0)
        metas = [meta_ref[source] for source in range(devices)]
        rows_of = [
            jnp.concatenate([metas[source][entry : entry + 1] for source in range(devices)], axis=0).astype(jnp.int32)
            for entry in range(picked)
        ]
        codes = [None] + [jnp.max(metas[source][0:1, :]).astype(jnp.int32) - 1 for source in range(1, devices)]
        live = (rows_of[0] > 0) & (ids != own)
        chosen = []
        for peer in range(devices):
            active = ids == peer
            for entry in rows_of[1:]:
                active = active | (entry == peer)
            chosen.append(active)
        peak = jnp.full((devices, tile_rows), masked_value, jnp.float32)
        for peer in range(devices):
            peak = jnp.maximum(peak, jnp.where(chosen[peer], lse_of[peer], masked_value))
        total = jnp.zeros_like(peak)
        delta = jnp.zeros_like(peak)
        for peer in range(devices):
            power = jnp.where(chosen[peer], jnp.exp2(lse_of[peer] - peak), 0.0)
            total = total + power
            delta = delta + jnp.where(chosen[peer], power * gd_of[peer], 0.0)
        delta = delta / total
        weight = jnp.exp2(lse_sc[own] - peak) / total * inv_ref[0]
        w_sc[0] = jnp.where(live, weight, 0.0)
        w_sc[1] = jnp.where(live, -weight * delta, 0.0)

        code_ids = lax.broadcasted_iota(jnp.int32, (tasks, tile_rows), 0)
        own_lse = stat_ref[0]
        own_gd = stat_ref[1]
        peak = own_lse
        rows_lse = [lse_sc[peer, pl.ds(own, 1), :] for peer in range(devices)]
        rows_gd = [gd_sc[peer, pl.ds(own, 1), :] for peer in range(devices)]
        for peer in range(devices):
            peak = jnp.maximum(peak, jnp.where(code_ids == task_ref[peer], rows_lse[peer], masked_value))
        own_power = jnp.exp2(own_lse - peak)
        total = own_power
        delta = own_power * own_gd
        for peer in range(devices):
            here = code_ids == task_ref[peer]
            power = jnp.where(here, jnp.exp2(rows_lse[peer] - peak), 0.0)
            total = total + power
            delta = delta + jnp.where(here, power * rows_gd[peer], 0.0)
        inverse = 1.0 / total
        delta = delta * inverse
        own_weight = own_power * inverse
        d_sc[0] = peak
        d_sc[1] = inverse
        d_sc[2] = delta
        d_sc[3] = own_weight
        d_sc[4] = own_weight * stat_ref[2]
        d_sc[5] = -own_weight * stat_ref[2] * delta
        d_sc[6] = -own_weight * delta

        nothing = jnp.zeros((head_dim, tile_rows), jnp.bfloat16)
        for source in range(1, devices):
            odd = lax.rem(jnp.maximum(codes[source], 0), 2) == 1
            first = w_sc[0, source : source + 1, :]
            second = w_sc[1, source : source + 1, :]
            turned = qgt_in_ref[source - 1].astype(jnp.float32)
            g_first = (turned[head_dim:] * first).astype(jnp.bfloat16)
            q_first = (turned[:head_dim] * first).astype(jnp.bfloat16)
            q_second = (turned[:head_dim] * second).astype(jnp.bfloat16)
            xin_ref[source, :head_dim, :tile_rows] = jnp.where(odd, q_second, g_first)
            xin_ref[source, :head_dim, tile_rows:] = jnp.where(odd, q_first, nothing)
            xin_ref[source, head_dim:, :tile_rows] = jnp.where(odd, g_first, q_second)
            xin_ref[source, head_dim:, tile_rows:] = jnp.where(odd, nothing, q_first)
        for source in range(1, devices):
            head = lax.rem(jnp.maximum(codes[source], 0), groups)
            target = grad_ref if source % 2 else more_ref
            target[head] += dot_t(pd_in_ref[source - 1], xin_ref[source])

        for load in loads[:2]:
            load.wait()
        for head in range(groups):
            v_rows = slice(0, head_dim) if head % 2 == 0 else slice(head_dim, 2 * head_dim)
            k_rows = slice(head_dim, 2 * head_dim) if head % 2 == 0 else slice(0, head_dim)
            for tile in range(tiles_dev):
                code = tile * groups + head
                first = d_sc[4, code : code + 1, :]
                second = d_sc[5, code : code + 1, :]
                turned = qgt_ref[head, :, tile * tile_rows : (tile + 1) * tile_rows].astype(jnp.float32)
                early = slice(tile * pair, tile * pair + tile_rows)
                late = slice(tile * pair + tile_rows, (tile + 1) * pair)
                x_ref[head, v_rows, early] = (turned[head_dim:] * first).astype(jnp.bfloat16)
                x_ref[head, v_rows, late] = nothing
                x_ref[head, k_rows, early] = (turned[:head_dim] * second).astype(jnp.bfloat16)
                x_ref[head, k_rows, late] = (turned[:head_dim] * first).astype(jnp.bfloat16)
        for head in range(groups):
            for tile in range(tiles_dev):
                code = tile * groups + head
                first = d_sc[3, code : code + 1, :]
                second = d_sc[6, code : code + 1, :]
                mix = mix_ref[head, tile].astype(jnp.float32)
                acc_ref[0, code] = mix[:head_dim] * first
                acc_ref[1, code] = mix[2 * head_dim :] * first + mix[head_dim : 2 * head_dim] * second

        def gather(peer, carry):
            code = task_ref[peer]

            @pl.when(code >= 0)
            def _():
                at = pl.ds(code, 1)
                part_w = jnp.exp2(lse_sc[peer, pl.ds(own, 1), :] - d_sc[0, at, :]) * d_sc[1, at, :]
                shift = -part_w * d_sc[2, at, :]
                mix = back_ref[peer, : 3 * head_dim, :].astype(jnp.float32)
                acc_ref[0, code] += mix[:head_dim] * part_w
                acc_ref[1, code] += mix[2 * head_dim :] * part_w + mix[head_dim : 2 * head_dim] * shift

            return carry

        lax.fori_loop(0, own, gather, 0)

        sub = lax.broadcasted_iota(jnp.int32, (tile_rows, tile_rows), 0)
        lane = lax.broadcasted_iota(jnp.int32, (tile_rows, tile_rows), 1)
        unit = jnp.where(sub == lane, 1.0, 0.0).astype(jnp.bfloat16)
        for tile in range(tiles_dev):
            rows = slice(tile * tile_rows, (tile + 1) * tile_rows)
            for head in range(0, groups, 2):
                cols = slice(head * head_dim, (head + 2) * head_dim)
                code = tile * groups + head
                both = jnp.concatenate([acc_ref[0, code], acc_ref[0, code + 1]], axis=0).astype(jnp.bfloat16)
                out_ref[rows, cols] = dot_t(unit, both).astype(jnp.bfloat16)
                both = jnp.concatenate([acc_ref[1, code], acc_ref[1, code + 1]], axis=0)
                dq_ref[rows, cols] = dot_t(unit, (both * scaling).astype(jnp.bfloat16)).astype(jnp.bfloat16)
        stores = [
            pltpu.make_async_copy(src, dst, out_sem.at[index])
            for index, (src, dst) in enumerate(((out_ref, out_hbm), (dq_ref, dq_hbm), (dk_ref, dk_hbm), (dv_ref, dv_hbm)))
        ]
        stores[0].start()
        stores[1].start()

        for load in loads[2:]:
            load.wait()
        lane = lax.broadcasted_iota(jnp.int32, (tile_rows, 2 * head_dim), 1)
        for head in range(0, groups, 2):
            cols = slice(head * head_dim, (head + 2) * head_dim)
            for first in range(tiles_dev):
                rows = slice(first * tile_rows, (first + 1) * tile_rows)
                even, odd = (
                    dot_t(pd_ref[h, rows, first * pair :], x_ref[h, :, first * pair :])
                    + grad_ref[h, rows, :]
                    + more_ref[h, rows, :]
                    for h in (head, head + 1)
                )
                dv_ref[rows, cols] = jnp.where(lane < head_dim, even, odd).astype(jnp.bfloat16)
                swapped = jnp.where(lane < head_dim, odd, even) * scaling
                dk_ref[rows, cols] = pltpu.roll(swapped, head_dim, 1).astype(jnp.bfloat16)
        stores[2].start()
        stores[3].start()
        for store in stores:
            store.wait()

    return body


def fast_local(query, key, value, grad_out, picks):
    row_count, columns = query.shape
    tiles_dev, groups, picked = picks.shape
    head_dim = columns // groups
    tile_rows = row_count // tiles_dev
    devices = lax.axis_size("ctx")
    tasks = tiles_dev * groups
    smem = pl.BlockSpec(memory_space=pltpu.SMEM)
    vmem = pl.BlockSpec(memory_space=pltpu.VMEM)
    far = pl.BlockSpec(memory_space=pltpu.HBM)
    low = jnp.bfloat16
    wide = jnp.float32
    width = 2 * head_dim
    shape = jax.ShapeDtypeStruct
    dma = pltpu.SemaphoreType.DMA
    small = pltpu.CompilerParams(vmem_limit_bytes=vmem_grant)
    near = pltpu.VMEM

    def away(*arrays):
        return tuple(pltpu.with_memory_space_constraint(x, pltpu.HBM) for x in arrays)

    def keep(*arrays):
        return tuple(pltpu.with_memory_space_constraint(x, pltpu.VMEM) for x in arrays)


    send_q, task_of = pl.pallas_call(
        pack_kernel(tiles_dev, groups, picked, tile_rows, head_dim, devices),
        out_shape=(shape((devices, tile_rows + 8, width), low), shape((devices,), jnp.int32)),
        in_specs=[smem, vmem, vmem],
        out_specs=(vmem, smem),
        name="pack",
    )(picks, query, grad_out)
    recv_q = lax.all_to_all(send_q, "ctx", split_axis=0, concat_axis=0, tiled=True)

    kv, vkt, stats, table = pl.pallas_call(
        own_kernel(tiles_dev, groups, tile_rows, head_dim),
        out_shape=(
            near((groups, row_count, width), low),
            near((groups, width, row_count), low),
            near((4, tasks, tile_rows), wide),
            near((tasks, 8, tile_rows), wide),
        ),
        in_specs=[far] * 4,
        out_specs=tuple([vmem] * 4),
        scratch_shapes=[pltpu.VMEM((row_count, columns), low)] * 4 + [dma((4,))],
        compiler_params=small,
        name="own",
    )(*away(query, key, value, grad_out))

    slot = 3 * head_dim + 3 * devices
    in_shape = (devices - 1, row_count, 2 * tile_rows)
    send_b, inverse_in = pl.pallas_call(
        serve_kernel(groups, tile_rows, head_dim, devices),
        out_shape=(pltpu.HBM((devices, slot, tile_rows), low), near((2, devices, tile_rows), wide)),
        in_specs=[smem, smem, vmem, vmem, vmem, vmem],
        out_specs=(far, vmem),
        scratch_shapes=[
            pltpu.VMEM((devices, slot, tile_rows), low),
            pltpu.VMEM((3 * devices, tile_rows), wide),
            dma(()),
        ],
        compiler_params=pltpu.CompilerParams(
            vmem_limit_bytes=vmem_grant
        ),
        name="serve",
    )(*away(picks, task_of), *keep(recv_q, kv, vkt, table))
    recv_b = lax.all_to_all(send_b, "ctx", split_axis=0, concat_axis=0, tiled=True)

    pairs_in, qgt_in, lists_in = pl.pallas_call(
        again_kernel(groups, tile_rows, head_dim, devices),
        out_shape=(near(in_shape, low), near((devices - 1, width, tile_rows), low), near((devices, 8, width), wide)),
        in_specs=[smem, vmem, vmem, vmem],
        out_specs=(vmem, vmem, vmem),
        compiler_params=small,
        name="again",
    )(*away(picks), *keep(recv_q, kv, inverse_in))

    mix_shape = (groups, tiles_dev, 3 * head_dim, tile_rows)
    pair_shape = (groups, row_count, 2 * row_count)
    turned_shape = (groups, width, row_count)
    qgt, mix, pairs = pl.pallas_call(
        rest_kernel(tiles_dev, groups, tile_rows, head_dim),
        out_shape=(pltpu.HBM(turned_shape, low), pltpu.HBM(mix_shape, low), pltpu.HBM(pair_shape, low)),
        in_specs=[far] * 2 + [vmem] * 3,
        out_specs=tuple([far] * 3),
        scratch_shapes=[pltpu.VMEM((row_count, columns), low)] * 2
        + [
            pltpu.VMEM(turned_shape, low),
            pltpu.VMEM(mix_shape, low),
            pltpu.VMEM(pair_shape, low),
            dma((2,)),
            dma((tiles_dev + 2,)),
        ],
        compiler_params=small,
        name="rest",
    )(*away(query, grad_out), *keep(kv, vkt, stats))

    return pl.pallas_call(
        final_kernel(tiles_dev, groups, picked, tile_rows, head_dim, devices),
        out_shape=tuple([shape((row_count, columns), low)] * 4),
        in_specs=[smem, smem] + [vmem] * 6 + [far] * 3,
        out_specs=tuple([far] * 4),
        scratch_shapes=[
            pltpu.VMEM((groups, width, row_count), low),
            pltpu.VMEM(mix_shape, low),
            pltpu.VMEM(pair_shape, low),
        ]
        + [pltpu.VMEM((row_count, columns), low)] * 4
        + [
            pltpu.VMEM((2, tasks, head_dim, tile_rows), wide),
            pltpu.VMEM((groups, row_count, width), wide),
            pltpu.VMEM((groups, row_count, width), wide),
            pltpu.VMEM((devices, devices, tile_rows), wide),
            pltpu.VMEM((devices, devices, tile_rows), wide),
            pltpu.VMEM((2, devices, tile_rows), wide),
            pltpu.VMEM((7, tasks, tile_rows), wide),
            pltpu.VMEM((groups, width, 2 * row_count), low),
            pltpu.VMEM((devices, width, 2 * tile_rows), low),
            dma((tiles_dev + 2,)),
            dma((4,)),
        ],
        compiler_params=small,
        name="final",
    )(*away(picks, task_of), *keep(lists_in, recv_b, qgt_in, stats, inverse_in, pairs_in), *away(qgt, mix, pairs))


def choose(query, key, value, grad_out, picks):
    pair_bytes = lax.axis_size("ctx") * query.shape[0] * (query.shape[0] // picks.shape[0]) * 4
    plan = fast_local if pair_bytes <= pair_budget else local
    return plan(query, key, value, grad_out, picks)


def solution(mesh):
    placed = (
        P("ctx", "head"),
        P("ctx", "head"),
        P("ctx", "head"),
        P("ctx", "head"),
        P("ctx", "head", None),
    )
    return jax.shard_map(
        choose,
        mesh=mesh,
        in_specs=placed,
        out_specs=(P("ctx", "head"), P("ctx", "head"), P("ctx", "head"), P("ctx", "head")),
        check_vma=False,
    )
```

```python
import math

import jax
import jax.numpy as jnp
from jax import lax
from jax.experimental import pallas as pl
from jax.experimental.pallas import tpu as pltpu
from jax.sharding import PartitionSpec as P

masked_value = -1e30
highest = lax.Precision.HIGHEST
LOG2E = math.log2(math.e)
pair_budget = 8 << 20
vmem_grant = 32 << 20


def attend_slots(q_slots, head_ids, k_heads, v_heads, scaling):
    key_rows = jnp.take(k_heads, head_ids, axis=0)
    value_rows = jnp.take(v_heads, head_ids, axis=0)
    scores = (
        jnp.einsum("ndq,nkd->nqk", q_slots, key_rows, preferred_element_type=jnp.float32) * scaling
    )
    peak_score = jnp.max(scores, axis=-1, keepdims=True)
    log_total = peak_score + jnp.log(jnp.sum(jnp.exp(scores - peak_score), axis=-1, keepdims=True))
    attend_low = jnp.exp(scores - log_total).astype(jnp.bfloat16)
    outputs = jnp.einsum("nqk,nkd->ndq", attend_low, value_rows, preferred_element_type=jnp.float32)
    return (outputs, log_total[..., 0])


def slot_grads(q_slots, g_slots, c_slots, lse_slots, head_ids, k_heads, v_heads, scaling):
    key_rows = jnp.take(k_heads, head_ids, axis=0)
    value_rows = jnp.take(v_heads, head_ids, axis=0)
    scores = (
        jnp.einsum("ndq,nkd->nqk", q_slots, key_rows, preferred_element_type=jnp.float32) * scaling
    )
    attend = jnp.exp(scores - lse_slots[..., None])
    attend_low = attend.astype(jnp.bfloat16)
    grad_v = jnp.einsum("nqk,ndq->nkd", attend_low, g_slots, preferred_element_type=jnp.float32)
    grad_prob = jnp.einsum("ndq,nkd->nqk", g_slots, value_rows, preferred_element_type=jnp.float32)
    dscore = (attend * (grad_prob - c_slots[..., None])).astype(jnp.bfloat16)
    grad_k = (
        jnp.einsum("nqk,ndq->nkd", dscore, q_slots, preferred_element_type=jnp.float32) * scaling
    )
    grad_q = (
        jnp.einsum("nqk,nkd->ndq", dscore, key_rows, preferred_element_type=jnp.float32) * scaling
    )
    return (grad_k, grad_v, grad_q)


def local(query, key, value, grad_out, picks):
    row_count, columns = query.shape
    tiles_dev, groups, picked = picks.shape
    head_dim = columns // groups
    tile_rows = row_count // tiles_dev
    others = picked - 1
    scaling = 1.0 / math.sqrt(head_dim)
    devices = lax.axis_size("ctx")
    own_block = lax.axis_index("ctx")
    per_group = min(8, devices)
    all_picks = lax.all_gather(picks, "ctx", axis=0, tiled=True)
    q_heads = query.reshape(row_count, groups, head_dim).transpose(1, 0, 2)
    k_heads = key.reshape(row_count, groups, head_dim).transpose(1, 0, 2)
    v_heads = value.reshape(row_count, groups, head_dim).transpose(1, 0, 2)
    q_tiles = query.reshape(tiles_dev, tile_rows, groups, head_dim)
    do_tiles = grad_out.reshape(tiles_dev, tile_rows, groups, head_dim)
    do_major = do_tiles.transpose(0, 2, 1, 3)
    positions = jnp.arange(row_count, dtype=jnp.int32)
    tile_masks = []
    for tile_step in range(tiles_dev):
        span = (tile_step + 1) * tile_rows
        query_pos = positions[tile_step * tile_rows : span]
        tile_masks.append(positions[None, :span] <= query_pos[:, None])
    targets = picks[:, :, 1:]
    active = targets != own_block
    lookup = jnp.where(active, targets, own_block).reshape(-1)
    peer_ids = jnp.arange(devices, dtype=jnp.int32)
    routing = ((targets[None] == peer_ids[:, None, None, None]) & active[None]).astype(jnp.float32)
    routing_low = routing.astype(jnp.bfloat16)
    send_q = jnp.einsum(
        "jtgi,tqgd->jdq", routing_low, q_tiles, preferred_element_type=jnp.float32
    ).astype(jnp.bfloat16)
    recv_q = lax.all_to_all(send_q, "ctx", split_axis=0, concat_axis=0, tiled=True)

    def own_forward(inputs):
        q_head, k_head, v_head = inputs
        out_list = []
        lse_list = []
        for tile_step in range(tiles_dev):
            span = (tile_step + 1) * tile_rows
            q_part = q_head[tile_step * tile_rows : span]
            scores = (
                jnp.einsum("qd,kd->qk", q_part, k_head[:span], preferred_element_type=jnp.float32)
                * scaling
            )
            scores = jnp.where(tile_masks[tile_step], scores, masked_value)
            peak_score = jnp.max(scores, axis=-1, keepdims=True)
            log_total = peak_score + jnp.log(
                jnp.sum(jnp.exp(scores - peak_score), axis=-1, keepdims=True)
            )
            attend_low = jnp.exp(scores - log_total).astype(jnp.bfloat16)
            out_list.append(jnp.dot(attend_low, v_head[:span], preferred_element_type=jnp.float32))
            lse_list.append(log_total[:, 0])
        return (jnp.concatenate(out_list, axis=0), jnp.concatenate(lse_list, axis=0))

    own_out, own_lse = lax.map(own_forward, (q_heads, k_heads, v_heads))
    sources = all_picks.reshape(devices, tiles_dev, groups, picked)[..., 1:]
    incoming = (sources == own_block) & (peer_ids[:, None, None, None] != own_block)
    live_in = jnp.any(incoming, axis=(1, 2, 3))
    group_ids = jnp.arange(groups, dtype=jnp.int32)
    head_of = jnp.sum(jnp.where(incoming, group_ids[None, None, :, None], 0), axis=(1, 2, 3))
    ranking = jnp.argsort(jnp.where(live_in, 0, 1) * devices + peer_ids)
    inverse = jnp.argsort(ranking)
    rounds = (jnp.sum(live_in.astype(jnp.int32)) + per_group - 1) // per_group
    heads_sorted = jnp.take(head_of, ranking, axis=0)
    q_sorted = jnp.take(recv_q, ranking, axis=0)

    def forward_turn(turn, totals):
        served_out, served_lse = totals
        offset = turn * per_group
        query_part = lax.dynamic_slice_in_dim(q_sorted, offset, per_group, 0)
        head_part = lax.dynamic_slice_in_dim(heads_sorted, offset, per_group, 0)
        out_part, lse_part = attend_slots(query_part, head_part, k_heads, v_heads, scaling)
        served_out = lax.dynamic_update_slice_in_dim(served_out, out_part, offset, 0)
        served_lse = lax.dynamic_update_slice_in_dim(served_lse, lse_part, offset, 0)
        return (served_out, served_lse)

    start_fwd = (
        jnp.zeros((devices, head_dim, tile_rows), jnp.float32),
        jnp.zeros((devices, tile_rows), jnp.float32),
    )
    served_out, served_lse = lax.fori_loop(0, rounds, forward_turn, start_fwd)
    back_out, back_lse = (
        lax.all_to_all(
            jnp.take(served_out, inverse, axis=0), "ctx", split_axis=0, concat_axis=0, tiled=True
        ),
        lax.all_to_all(
            jnp.take(served_lse, inverse, axis=0), "ctx", split_axis=0, concat_axis=0, tiled=True
        ),
    )
    task_out = jnp.take(back_out, lookup, axis=0).reshape(
        tiles_dev, groups, others, head_dim, tile_rows
    )
    task_lse = jnp.take(back_lse, lookup, axis=0).reshape(tiles_dev, groups, others, tile_rows)
    own_out_t = own_out.reshape(groups, tiles_dev, tile_rows, head_dim).transpose(1, 0, 2, 3)
    own_lse_t = own_lse.reshape(groups, tiles_dev, tile_rows).transpose(1, 0, 2)
    active_rows = active[..., None]
    rem_lse = jnp.where(active_rows, task_lse, masked_value)
    ceiling = jnp.maximum(own_lse_t, jnp.max(rem_lse, axis=2))
    log_total = ceiling + jnp.log(
        jnp.exp(own_lse_t - ceiling) + jnp.sum(jnp.exp(rem_lse - ceiling[:, :, None]), axis=2)
    )
    own_weight = jnp.exp(own_lse_t - log_total)
    rem_weight = jnp.where(active_rows, jnp.exp(rem_lse - log_total[:, :, None]), 0.0)
    mixed = own_weight[..., None] * own_out_t + jnp.einsum(
        "tgiq,tgidq->tgqd", rem_weight, task_out, precision=highest
    )
    out_low = mixed.astype(jnp.bfloat16)
    attn_out = out_low.transpose(0, 2, 1, 3).reshape(row_count, columns)
    row_delta = jnp.sum(do_major.astype(jnp.float32) * out_low.astype(jnp.float32), axis=-1)
    own_scaled = (own_weight[..., None] * do_major.astype(jnp.float32)).astype(jnp.bfloat16)
    own_shift = own_weight * row_delta
    g_heads = own_scaled.transpose(1, 0, 2, 3).reshape(groups, row_count, head_dim)
    c_heads = own_shift.transpose(1, 0, 2).reshape(groups, row_count)

    def own_backward(inputs):
        q_head, k_head, v_head, g_head, c_head, lse_head = inputs
        grad_k = jnp.zeros((row_count, head_dim), jnp.float32)
        grad_v = jnp.zeros((row_count, head_dim), jnp.float32)
        dq_list = []
        for tile_step in range(tiles_dev):
            first = tile_step * tile_rows
            span = (tile_step + 1) * tile_rows
            q_part = q_head[first:span]
            g_part = g_head[first:span]
            k_part = k_head[:span]
            scores = (
                jnp.einsum("qd,kd->qk", q_part, k_part, preferred_element_type=jnp.float32)
                * scaling
            )
            scores = jnp.where(tile_masks[tile_step], scores, masked_value)
            attend = jnp.exp(scores - lse_head[first:span, None])
            attend_low = attend.astype(jnp.bfloat16)
            part_dv = jnp.einsum(
                "qk,qd->kd", attend_low, g_part, preferred_element_type=jnp.float32
            )
            grad_prob = jnp.einsum(
                "qd,kd->qk", g_part, v_head[:span], preferred_element_type=jnp.float32
            )
            dscore = (attend * (grad_prob - c_head[first:span, None])).astype(jnp.bfloat16)
            part_dk = (
                jnp.einsum("qk,qd->kd", dscore, q_part, preferred_element_type=jnp.float32)
                * scaling
            )
            dq_list.append(jnp.dot(dscore, k_part, preferred_element_type=jnp.float32) * scaling)
            padding = ((0, row_count - span), (0, 0))
            grad_k = grad_k + jnp.pad(part_dk, padding)
            grad_v = grad_v + jnp.pad(part_dv, padding)
        return (grad_k, grad_v, jnp.concatenate(dq_list, axis=0))

    own_dk, own_dv, own_dq = lax.map(
        own_backward, (q_heads, k_heads, v_heads, g_heads, c_heads, own_lse)
    )
    rem_shift = rem_weight * row_delta[:, :, None]
    rem_scaled = (rem_weight[..., None] * do_major[:, :, None].astype(jnp.float32)).astype(
        jnp.bfloat16
    )
    send_g = jnp.einsum(
        "jtgi,tgiqd->jdq", routing_low, rem_scaled, preferred_element_type=jnp.float32
    )
    send_c = jnp.einsum("jtgi,tgiq->jq", routing, rem_shift, precision=highest)
    recv_g, recv_c = (
        lax.all_to_all(send_g, "ctx", split_axis=0, concat_axis=0, tiled=True),
        lax.all_to_all(send_c, "ctx", split_axis=0, concat_axis=0, tiled=True),
    )
    g_sorted = jnp.take(recv_g, ranking, axis=0).astype(jnp.bfloat16)
    c_sorted = jnp.take(recv_c, ranking, axis=0)

    def backward_turn(turn, totals):
        grad_k, grad_v, served_dq = totals
        offset = turn * per_group
        query_part = lax.dynamic_slice_in_dim(q_sorted, offset, per_group, 0)
        cot_part = lax.dynamic_slice_in_dim(g_sorted, offset, per_group, 0)
        shift_part = lax.dynamic_slice_in_dim(c_sorted, offset, per_group, 0)
        lse_part = lax.dynamic_slice_in_dim(served_lse, offset, per_group, 0)
        head_part = lax.dynamic_slice_in_dim(heads_sorted, offset, per_group, 0)
        part_dk, part_dv, part_dq = slot_grads(
            query_part, cot_part, shift_part, lse_part, head_part, k_heads, v_heads, scaling
        )
        head_onehot = (head_part[:, None] == group_ids[None, :]).astype(jnp.float32)
        grad_k = grad_k + jnp.einsum("ng,nkd->gkd", head_onehot, part_dk, precision=highest)
        grad_v = grad_v + jnp.einsum("ng,nkd->gkd", head_onehot, part_dv, precision=highest)
        served_dq = lax.dynamic_update_slice_in_dim(served_dq, part_dq, offset, 0)
        return (grad_k, grad_v, served_dq)

    zeros_heads = jnp.zeros((groups, row_count, head_dim), jnp.float32)
    start_bwd = (zeros_heads, zeros_heads, jnp.zeros((devices, head_dim, tile_rows), jnp.float32))
    rem_dk, rem_dv, served_dq = lax.fori_loop(0, rounds, backward_turn, start_bwd)
    back_dq = lax.all_to_all(
        jnp.take(served_dq, inverse, axis=0).astype(jnp.bfloat16),
        "ctx",
        split_axis=0,
        concat_axis=0,
        tiled=True,
    ).astype(jnp.float32)
    task_dq = jnp.take(back_dq, lookup, axis=0).reshape(
        tiles_dev, groups, others, head_dim, tile_rows
    )
    rem_dq = jnp.sum(jnp.where(active[..., None, None], task_dq, 0.0), axis=2)
    own_dq_t = own_dq.reshape(groups, tiles_dev, tile_rows, head_dim).transpose(1, 0, 2, 3)
    total_dq = own_dq_t + rem_dq.transpose(0, 1, 3, 2)
    grad_query = total_dq.transpose(0, 2, 1, 3).reshape(row_count, columns).astype(jnp.bfloat16)
    grad_key = (own_dk + rem_dk).transpose(1, 0, 2).reshape(row_count, columns).astype(jnp.bfloat16)
    grad_value = (
        (own_dv + rem_dv).transpose(1, 0, 2).reshape(row_count, columns).astype(jnp.bfloat16)
    )
    return (attn_out, grad_query, grad_key, grad_value)


def pair_parts(near, far, tiles_dev, tile_rows):
    for part in range(tiles_dev):
        rows = slice(part * tile_rows, (part + 1) * tile_rows)
        cols = slice(part * 2 * tile_rows, tiles_dev * 2 * tile_rows)
        yield near.at[:, rows, cols], far.at[:, rows, cols]


def dot_t(a, b):
    return lax.dot_general(a, b, (((1,), (1,)), ((), ())), preferred_element_type=jnp.float32)


def split_low(x):
    high = x.astype(jnp.bfloat16).astype(jnp.float32)
    return high, x - high


def halves(block, head_dim):
    lane = lax.broadcasted_iota(jnp.int32, block.shape, 1)
    zero = jnp.zeros_like(block)
    return jnp.where(lane < head_dim, block, zero), jnp.where(lane < head_dim, zero, block)


def pack_kernel(tiles_dev, groups, picked, tile_rows, head_dim, devices):
    def body(picks_ref, q_ref, g_ref, send_ref, task_ref):
        own = picks_ref[0, 0, 0]
        meta_rows = send_ref.shape[1] - tile_rows
        lanes = send_ref.shape[2]
        row = lax.broadcasted_iota(jnp.int32, (meta_rows, lanes), 0)
        blank = jnp.zeros((meta_rows, lanes), jnp.bfloat16)
        for peer in range(devices):
            send_ref[peer, tile_rows:, :] = blank
            task_ref[peer] = -1
        for tile in range(tiles_dev):
            rows = slice(tile * tile_rows, (tile + 1) * tile_rows)
            for head in range(groups):
                cols = slice(head * head_dim, (head + 1) * head_dim)
                block = jnp.concatenate([q_ref[rows, cols], g_ref[rows, cols]], axis=1)
                code = tile * groups + head
                meta = jnp.where(row == 0, code + 1, 0)
                for entry in range(1, picked):
                    meta = jnp.where(row == entry, picks_ref[tile, head, entry], meta)
                meta = meta.astype(jnp.float32).astype(jnp.bfloat16)
                for entry in range(1, picked):
                    target = picks_ref[tile, head, entry]
                    send_ref[target, :tile_rows, :] = block
                    send_ref[target, tile_rows:, :] = meta
                    task_ref[target] = code
        task_ref[own] = -1

    return body


def own_kernel(tiles_dev, groups, tile_rows, head_dim, devices):
    scale = LOG2E / math.sqrt(head_dim)

    def body(picks_ref, task_ref, q_hbm, k_hbm, v_hbm, g_hbm, kv_ref, vkt_ref, stat_ref, table_ref, info_ref,
             q_ref, k_ref, v_ref, g_ref, rows_ref, in_sem):
        loads = [
            pltpu.make_async_copy(src, dst, in_sem.at[index])
            for index, (src, dst) in enumerate(((k_hbm, k_ref), (v_hbm, v_ref), (q_hbm, q_ref), (g_hbm, g_ref)))
        ]
        for load in loads:
            load.start()
        for load in loads:
            load.wait()
        sub = lax.broadcasted_iota(jnp.int32, (tile_rows, tile_rows), 0)
        lane = lax.broadcasted_iota(jnp.int32, (tile_rows, tile_rows), 1)
        causal = sub <= lane
        for head in range(groups):
            cols = slice(head * head_dim, (head + 1) * head_dim)
            kv_ref[head] = jnp.concatenate([k_ref[:, cols], v_ref[:, cols]], axis=1)

        def product(code):
            tile, head = code // groups, code % groups
            cols = slice(head * head_dim, (head + 1) * head_dim)
            rows = slice(tile * tile_rows, (tile + 1) * tile_rows)
            block = jnp.concatenate([q_ref[rows, cols], g_ref[rows, cols]], axis=1)
            return dot_t(kv_ref[head, : rows.stop, :], jnp.concatenate(halves(block, head_dim), axis=0))

        ahead = product(0)
        for code in range(tiles_dev * groups):
            both = ahead
            if code + 1 < tiles_dev * groups:
                ahead = product(code + 1)
            tile = code // groups
            split = tile * tile_rows
            last = jnp.where(causal, both[split:, :tile_rows], masked_value)
            peak = jnp.max(last, axis=0, keepdims=True)
            if tile:
                peak = jnp.maximum(peak, jnp.max(both[:split, :tile_rows], axis=0, keepdims=True))
            peak = peak * scale
            powers = jnp.exp2(last * scale - peak)
            total = jnp.sum(powers, axis=0, keepdims=True)
            mean_grad = jnp.sum(powers * both[split:, tile_rows:], axis=0, keepdims=True)
            if tile:
                powers = jnp.exp2(both[:split, :tile_rows] * scale - peak)
                total = total + jnp.sum(powers, axis=0, keepdims=True)
                mean_grad = mean_grad + jnp.sum(powers * both[:split, tile_rows:], axis=0, keepdims=True)
            inverse = 1.0 / total
            mean_grad = mean_grad * inverse
            lse = peak + jnp.log2(total)
            for index, value in enumerate((lse, mean_grad, inverse, peak)):
                stat_ref[index, code : code + 1, :] = value
            for index, value in enumerate(split_low(lse) + (mean_grad,)):
                rows_ref[code, index : index + 1, :] = value
        for head in range(groups):
            cols = slice(head * head_dim, (head + 1) * head_dim)
            vkt_ref[head] = jnp.concatenate([v_ref[:, cols], k_ref[:, cols]], axis=1).T
        sub = lax.broadcasted_iota(jnp.int32, (devices, tile_rows), 0)
        codes = jnp.full((devices, tile_rows), -1, jnp.int32)
        for peer in range(devices):
            codes = jnp.where(sub == peer, task_ref[peer], codes)
            table_ref[peer] = rows_ref[jnp.maximum(task_ref[peer], 0)]
        info_ref[:devices, :] = codes.astype(jnp.float32)
        info_ref[devices:, :] = jnp.full((devices, tile_rows), picks_ref[0, 0, 0], jnp.int32).astype(jnp.float32)

    return body


def rest_kernel(tiles_dev, groups, tile_rows, head_dim):
    scale = LOG2E / math.sqrt(head_dim)

    def body(q_hbm, g_hbm, kv_ref, vkt_ref, stat_ref, qgt_hbm, mix_hbm, pd_hbm,
             q_ref, g_ref, qgt_ref, mix_ref, pd_ref, in_sem, out_sem):
        loads = [
            pltpu.make_async_copy(src, dst, in_sem.at[index])
            for index, (src, dst) in enumerate(((q_hbm, q_ref), (g_hbm, g_ref)))
        ]
        for load in loads:
            load.start()
        for load in loads:
            load.wait()
        sub = lax.broadcasted_iota(jnp.int32, (tile_rows, tile_rows), 0)
        lane = lax.broadcasted_iota(jnp.int32, (tile_rows, tile_rows), 1)
        causal = sub <= lane

        def product(code):
            tile, head = code // groups, code % groups
            cols = slice(head * head_dim, (head + 1) * head_dim)
            rows = slice(tile * tile_rows, (tile + 1) * tile_rows)
            block = jnp.concatenate([q_ref[rows, cols], g_ref[rows, cols]], axis=1)
            qgt_ref[head, :, rows] = block.T
            return dot_t(kv_ref[head, : rows.stop, :], jnp.concatenate(halves(block, head_dim), axis=0))

        ahead = product(0)
        for code in range(tiles_dev * groups):
            both = ahead
            if code + 1 < tiles_dev * groups:
                ahead = product(code + 1)
            tile, head = code // groups, code % groups
            span = (tile + 1) * tile_rows
            at = tile * 2 * tile_rows
            peak = stat_ref[3, code : code + 1, :]
            inverse = stat_ref[2, code : code + 1, :]
            for part in range(tile + 1):
                chunk = slice(part * tile_rows, (part + 1) * tile_rows)
                scores = both[chunk, :tile_rows]
                if part == tile:
                    scores = jnp.where(causal, scores, masked_value)
                powers = jnp.exp2(scores * scale - peak)
                spread = powers * both[chunk, tile_rows:]
                pd_ref[head, chunk, at : at + tile_rows] = powers.astype(jnp.bfloat16)
                pd_ref[head, chunk, at + tile_rows : at + 2 * tile_rows] = spread.astype(jnp.bfloat16)
            result = jnp.dot(vkt_ref[head, :, :span], pd_ref[head, :span, at : at + 2 * tile_rows],
                             preferred_element_type=jnp.float32)
            mix_ref[head, tile, : 2 * head_dim, :] = (result[:, :tile_rows] * inverse).astype(jnp.bfloat16)
            mix_ref[head, tile, 2 * head_dim :, :] = (result[head_dim:, tile_rows:] * inverse).astype(jnp.bfloat16)
        stores = [
            pltpu.make_async_copy(mix_ref, mix_hbm, out_sem.at[tiles_dev]),
            pltpu.make_async_copy(qgt_ref, qgt_hbm, out_sem.at[tiles_dev + 1]),
        ] + [
            pltpu.make_async_copy(src, dst, out_sem.at[index])
            for index, (src, dst) in enumerate(pair_parts(pd_ref, pd_hbm, tiles_dev, tile_rows))
        ]
        for store in stores:
            store.start()
        for store in stores:
            store.wait()

    return body


def parts_of(block, kv_head, tile_rows, head_dim, scale):
    both = dot_t(kv_head, jnp.concatenate(halves(block, head_dim), axis=0))
    scores = both[:, :tile_rows]
    peak = jnp.max(scores, axis=0, keepdims=True) * scale
    powers = jnp.exp2(scores * scale - peak)
    spread = powers * both[:, tile_rows:]
    return peak, powers, spread


def serve_kernel(groups, tile_rows, head_dim, devices):
    scale = LOG2E / math.sqrt(head_dim)

    def body(info_ref, recv_ref, kv_ref, vkt_ref, table_ref, send_hbm, inv_ref,
             send_ref, st_ref, out_sem):
        own = jnp.max(info_ref[devices : devices + 1, :]).astype(jnp.int32)
        st_ref[...] = jnp.zeros_like(st_ref)
        inv_ref[...] = jnp.zeros_like(inv_ref)
        heads = [None]
        blocks = [None]
        for source in range(1, devices):
            code = jnp.max(recv_ref[source, tile_rows:, :].astype(jnp.float32)[0:1, :]).astype(jnp.int32) - 1
            block = recv_ref[source, :tile_rows, :]
            heads.append(lax.rem(jnp.maximum(code, 0), groups))
            blocks.append(jnp.where((code >= 0) & (own != source), block, jnp.zeros_like(block)))
        ahead = parts_of(blocks[1], kv_ref[heads[1]], tile_rows, head_dim, scale)
        for source in range(1, devices):
            peak, powers, spread = ahead
            if source + 1 < devices:
                ahead = parts_of(blocks[source + 1], kv_ref[heads[source + 1]], tile_rows, head_dim, scale)
            total = jnp.sum(powers, axis=0, keepdims=True)
            inverse = 1.0 / total
            mean_grad = jnp.sum(spread, axis=0, keepdims=True) * inverse
            both = jnp.concatenate([powers.astype(jnp.bfloat16), spread.astype(jnp.bfloat16)], axis=1)
            result = jnp.dot(vkt_ref[heads[source]], both, preferred_element_type=jnp.float32)
            send_ref[source, : 2 * head_dim, :] = (result[:, :tile_rows] * inverse).astype(jnp.bfloat16)
            send_ref[source, 2 * head_dim : 3 * head_dim, :] = (result[head_dim:, tile_rows:] * inverse).astype(jnp.bfloat16)
            parts = split_low(peak + jnp.log2(total)) + (mean_grad,)
            for index in range(3):
                st_ref[index * devices + source : index * devices + source + 1, :] = parts[index]
            inv_ref[0, source : source + 1, :] = inverse
            inv_ref[1, source : source + 1, :] = peak
        table = st_ref[...]
        row = lax.broadcasted_iota(jnp.int32, table.shape, 0)
        mine = lax.rem(row, devices) == own
        for peer in range(devices):
            entry = table_ref[peer]
            wide = jnp.concatenate(
                [jnp.broadcast_to(entry[index : index + 1], (devices, tile_rows)) for index in range(3)], axis=0
            )
            send_ref[peer, 3 * head_dim :, :] = jnp.where(mine, wide, table).astype(jnp.bfloat16)
        store = pltpu.make_async_copy(send_ref, send_hbm, out_sem)
        store.start()
        store.wait()

    return body


def again_kernel(groups, tile_rows, head_dim, devices):
    scale = LOG2E / math.sqrt(head_dim)

    def body(picks_ref, recv_ref, kv_ref, inv_ref, pd_ref, qgt_ref, meta_ref):
        own = picks_ref[0, 0, 0]
        for source in range(devices):
            meta_ref[source] = recv_ref[source, tile_rows:, :].astype(jnp.float32)
        codes = [jnp.max(recv_ref[source, tile_rows:, :].astype(jnp.float32)[0:1, :]).astype(jnp.int32) - 1
                 for source in range(devices)]

        def product(source):
            block = recv_ref[source, :tile_rows, :]
            block = jnp.where((codes[source] >= 0) & (own != source), block, jnp.zeros_like(block))
            qgt_ref[source - 1] = block.T
            head = lax.rem(jnp.maximum(codes[source], 0), groups)
            return dot_t(kv_ref[head], jnp.concatenate(halves(block, head_dim), axis=0))

        ahead = product(1)
        for source in range(1, devices):
            both = ahead
            if source + 1 < devices:
                ahead = product(source + 1)
            powers = jnp.exp2(both[:, :tile_rows] * scale - inv_ref[1, source : source + 1, :])
            pd_ref[source - 1, :, :tile_rows] = powers.astype(jnp.bfloat16)
            pd_ref[source - 1, :, tile_rows:] = (powers * both[:, tile_rows:]).astype(jnp.bfloat16)

    return body


def final_kernel(tiles_dev, groups, picked, tile_rows, head_dim, devices):
    scaling = 1.0 / math.sqrt(head_dim)
    pair = 2 * tile_rows

    def body(info_ref, meta_ref, back_ref, qgt_in_ref, stat_ref, inv_ref,
             pd_in_ref, qgt_hbm, mix_hbm, pd_hbm, out_hbm, dq_hbm, dk_hbm, dv_hbm,
             qgt_ref, mix_ref, pd_ref, out_ref, dq_ref, dk_ref, dv_ref, acc_ref, grad_ref, more_ref,
             lse_sc, gd_sc, w_sc, d_sc, x_ref, xin_ref, in_sem, out_sem):
        own = jnp.max(info_ref[devices : devices + 1, :]).astype(jnp.int32)
        given = [jnp.max(info_ref[peer : peer + 1, :]).astype(jnp.int32) for peer in range(devices)]
        tasks = tiles_dev * groups
        base = 3 * head_dim
        loads = [
            pltpu.make_async_copy(mix_hbm, mix_ref, in_sem.at[tiles_dev]),
            pltpu.make_async_copy(qgt_hbm, qgt_ref, in_sem.at[tiles_dev + 1]),
        ] + [
            pltpu.make_async_copy(src, dst, in_sem.at[index])
            for index, (dst, src) in enumerate(pair_parts(pd_ref, pd_hbm, tiles_dev, tile_rows))
        ]
        for load in loads:
            load.start()
        grad_ref[...] = jnp.zeros_like(grad_ref)
        more_ref[...] = jnp.zeros_like(more_ref)

        lse_of = []
        gd_of = []
        for peer in range(devices):
            table = back_ref[peer, base:, :].astype(jnp.float32)
            lse_of.append(table[:devices] + table[devices : 2 * devices])
            gd_of.append(table[2 * devices :])
            lse_sc[peer] = lse_of[peer]
            gd_sc[peer] = gd_of[peer]

        ids = lax.broadcasted_iota(jnp.int32, (devices, tile_rows), 0)
        metas = [meta_ref[source] for source in range(devices)]
        rows_of = [
            jnp.concatenate([metas[source][entry : entry + 1] for source in range(devices)], axis=0).astype(jnp.int32)
            for entry in range(picked)
        ]
        codes = [None] + [jnp.max(metas[source][0:1, :]).astype(jnp.int32) - 1 for source in range(1, devices)]
        live = (rows_of[0] > 0) & (ids != own)
        chosen = []
        for peer in range(devices):
            active = ids == peer
            for entry in rows_of[1:]:
                active = active | (entry == peer)
            chosen.append(active)
        peak = jnp.full((devices, tile_rows), masked_value, jnp.float32)
        for peer in range(devices):
            peak = jnp.maximum(peak, jnp.where(chosen[peer], lse_of[peer], masked_value))
        total = jnp.zeros_like(peak)
        delta = jnp.zeros_like(peak)
        for peer in range(devices):
            power = jnp.where(chosen[peer], jnp.exp2(lse_of[peer] - peak), 0.0)
            total = total + power
            delta = delta + jnp.where(chosen[peer], power * gd_of[peer], 0.0)
        delta = delta / total
        weight = jnp.exp2(lse_sc[own] - peak) / total * inv_ref[0]
        weight = jnp.where(live, weight, 0.0)
        w_sc[0] = weight
        w_sc[1] = jnp.where(live, weight * delta * -scaling, 0.0)
        w_sc[2] = weight * scaling

        code_ids = lax.broadcasted_iota(jnp.int32, (tasks, tile_rows), 0)
        own_lse = stat_ref[0]
        own_gd = stat_ref[1]
        peak = own_lse
        rows_lse = [lse_sc[peer, pl.ds(own, 1), :] for peer in range(devices)]
        rows_gd = [gd_sc[peer, pl.ds(own, 1), :] for peer in range(devices)]
        for peer in range(devices):
            peak = jnp.maximum(peak, jnp.where(code_ids == given[peer], rows_lse[peer], masked_value))
        own_power = jnp.exp2(own_lse - peak)
        total = own_power
        delta = own_power * own_gd
        for peer in range(devices):
            here = code_ids == given[peer]
            power = jnp.where(here, jnp.exp2(rows_lse[peer] - peak), 0.0)
            total = total + power
            delta = delta + jnp.where(here, power * rows_gd[peer], 0.0)
        inverse = 1.0 / total
        delta = delta * inverse
        own_weight = own_power * inverse
        d_sc[0] = peak
        d_sc[1] = inverse
        d_sc[2] = delta
        d_sc[3] = own_weight
        d_sc[4] = own_weight * stat_ref[2]
        d_sc[5] = own_weight * stat_ref[2] * delta * -scaling
        d_sc[6] = own_weight * delta * -scaling
        d_sc[7] = own_weight * scaling
        d_sc[8] = own_weight * stat_ref[2] * scaling

        nothing = jnp.zeros((head_dim, tile_rows), jnp.bfloat16)
        for source in range(1, devices):
            odd = lax.rem(jnp.maximum(codes[source], 0), 2) == 1
            first = w_sc[0, source : source + 1, :]
            second = w_sc[1, source : source + 1, :]
            turned = qgt_in_ref[source - 1].astype(jnp.float32)
            g_first = (turned[head_dim:] * first).astype(jnp.bfloat16)
            q_first = (turned[:head_dim] * w_sc[2, source : source + 1, :]).astype(jnp.bfloat16)
            q_second = (turned[:head_dim] * second).astype(jnp.bfloat16)
            xin_ref[source, :head_dim, :tile_rows] = jnp.where(odd, q_second, g_first)
            xin_ref[source, :head_dim, tile_rows:] = jnp.where(odd, q_first, nothing)
            xin_ref[source, head_dim:, :tile_rows] = jnp.where(odd, g_first, q_second)
            xin_ref[source, head_dim:, tile_rows:] = jnp.where(odd, nothing, q_first)
        for source in range(1, devices):
            head = lax.rem(jnp.maximum(codes[source], 0), groups)
            target = grad_ref if source % 2 else more_ref
            target[head] += dot_t(pd_in_ref[source - 1], xin_ref[source])

        for load in loads[:2]:
            load.wait()
        for head in range(groups):
            v_rows = slice(0, head_dim) if head % 2 == 0 else slice(head_dim, 2 * head_dim)
            k_rows = slice(head_dim, 2 * head_dim) if head % 2 == 0 else slice(0, head_dim)
            for tile in range(tiles_dev):
                code = tile * groups + head
                first = d_sc[4, code : code + 1, :]
                second = d_sc[5, code : code + 1, :]
                turned = qgt_ref[head, :, tile * tile_rows : (tile + 1) * tile_rows].astype(jnp.float32)
                early = slice(tile * pair, tile * pair + tile_rows)
                late = slice(tile * pair + tile_rows, (tile + 1) * pair)
                x_ref[head, v_rows, early] = (turned[head_dim:] * first).astype(jnp.bfloat16)
                x_ref[head, v_rows, late] = nothing
                x_ref[head, k_rows, early] = (turned[:head_dim] * second).astype(jnp.bfloat16)
                x_ref[head, k_rows, late] = (turned[:head_dim] * d_sc[8, code : code + 1, :]).astype(jnp.bfloat16)
        for head in range(groups):
            for tile in range(tiles_dev):
                code = tile * groups + head
                first = d_sc[3, code : code + 1, :]
                second = d_sc[6, code : code + 1, :]
                mix = mix_ref[head, tile].astype(jnp.float32)
                acc_ref[0, code] = mix[:head_dim] * first
                acc_ref[1, code] = mix[2 * head_dim :] * d_sc[7, code : code + 1, :] + mix[head_dim : 2 * head_dim] * second

        for peer in range(devices):
            code = given[peer]

            @pl.when(code >= 0)
            def _(peer=peer, code=code):
                at = pl.ds(code, 1)
                part_w = jnp.exp2(lse_sc[peer, pl.ds(own, 1), :] - d_sc[0, at, :]) * d_sc[1, at, :]
                scaled_w = part_w * scaling
                shift = -scaled_w * d_sc[2, at, :]
                mix = back_ref[peer, : 3 * head_dim, :].astype(jnp.float32)
                acc_ref[0, code] += mix[:head_dim] * part_w
                acc_ref[1, code] += mix[2 * head_dim :] * scaled_w + mix[head_dim : 2 * head_dim] * shift

        sub = lax.broadcasted_iota(jnp.int32, (tile_rows, tile_rows), 0)
        lane = lax.broadcasted_iota(jnp.int32, (tile_rows, tile_rows), 1)
        unit = jnp.where(sub == lane, 1.0, 0.0).astype(jnp.bfloat16)
        for tile in range(tiles_dev):
            rows = slice(tile * tile_rows, (tile + 1) * tile_rows)
            for head in range(0, groups, 2):
                cols = slice(head * head_dim, (head + 2) * head_dim)
                code = tile * groups + head
                both = jnp.concatenate([acc_ref[0, code], acc_ref[0, code + 1]], axis=0).astype(jnp.bfloat16)
                out_ref[rows, cols] = dot_t(unit, both).astype(jnp.bfloat16)
                both = jnp.concatenate([acc_ref[1, code], acc_ref[1, code + 1]], axis=0).astype(jnp.bfloat16)
                dq_ref[rows, cols] = dot_t(unit, both).astype(jnp.bfloat16)
        stores = [
            pltpu.make_async_copy(src, dst, out_sem.at[index])
            for index, (src, dst) in enumerate(((out_ref, out_hbm), (dq_ref, dq_hbm), (dk_ref, dk_hbm), (dv_ref, dv_hbm)))
        ]
        stores[0].start()
        stores[1].start()

        for load in loads[2:]:
            load.wait()
        lane = lax.broadcasted_iota(jnp.int32, (tile_rows, 2 * head_dim), 1)
        for head in range(0, groups, 2):
            cols = slice(head * head_dim, (head + 2) * head_dim)
            for first in range(tiles_dev):
                rows = slice(first * tile_rows, (first + 1) * tile_rows)
                even, odd = (
                    dot_t(pd_ref[h, rows, first * pair :], x_ref[h, :, first * pair :])
                    + grad_ref[h, rows, :]
                    + more_ref[h, rows, :]
                    for h in (head, head + 1)
                )
                dv_ref[rows, cols] = jnp.where(lane < head_dim, even, odd).astype(jnp.bfloat16)
                swapped = jnp.where(lane < head_dim, odd, even)
                dk_ref[rows, cols] = pltpu.roll(swapped, head_dim, 1).astype(jnp.bfloat16)
        stores[2].start()
        stores[3].start()
        for store in stores:
            store.wait()

    return body


def fast_local(query, key, value, grad_out, picks):
    row_count, columns = query.shape
    tiles_dev, groups, picked = picks.shape
    head_dim = columns // groups
    tile_rows = row_count // tiles_dev
    devices = lax.axis_size("ctx")
    tasks = tiles_dev * groups
    smem = pl.BlockSpec(memory_space=pltpu.SMEM)
    vmem = pl.BlockSpec(memory_space=pltpu.VMEM)
    far = pl.BlockSpec(memory_space=pltpu.HBM)
    low = jnp.bfloat16
    wide = jnp.float32
    width = 2 * head_dim
    shape = jax.ShapeDtypeStruct
    dma = pltpu.SemaphoreType.DMA
    small = pltpu.CompilerParams(vmem_limit_bytes=vmem_grant)
    near = pltpu.VMEM

    def away(*arrays):
        return tuple(pltpu.with_memory_space_constraint(x, pltpu.HBM) for x in arrays)

    def keep(*arrays):
        return tuple(pltpu.with_memory_space_constraint(x, pltpu.VMEM) for x in arrays)


    send_q, task_of = pl.pallas_call(
        pack_kernel(tiles_dev, groups, picked, tile_rows, head_dim, devices),
        out_shape=(shape((devices, tile_rows + 8, width), low), shape((devices,), jnp.int32)),
        in_specs=[smem, vmem, vmem],
        out_specs=(vmem, smem),
        name="pack",
    )(picks, query, grad_out)
    recv_q = lax.all_to_all(send_q, "ctx", split_axis=0, concat_axis=0, tiled=True)

    kv, vkt, stats, table, info = pl.pallas_call(
        own_kernel(tiles_dev, groups, tile_rows, head_dim, devices),
        out_shape=(
            near((groups, row_count, width), low),
            near((groups, width, row_count), low),
            near((4, tasks, tile_rows), wide),
            near((devices, 8, tile_rows), wide),
            near((2 * devices, tile_rows), wide),
        ),
        in_specs=[smem, smem] + [far] * 4,
        out_specs=tuple([vmem] * 5),
        scratch_shapes=[pltpu.VMEM((row_count, columns), low)] * 4
        + [pltpu.VMEM((tasks, 8, tile_rows), wide), dma((4,))],
        compiler_params=small,
        name="own",
    )(*away(picks, task_of, query, key, value, grad_out))

    slot = 3 * head_dim + 3 * devices
    in_shape = (devices - 1, row_count, 2 * tile_rows)
    send_b, inverse_in = pl.pallas_call(
        serve_kernel(groups, tile_rows, head_dim, devices),
        out_shape=(pltpu.HBM((devices, slot, tile_rows), low), near((2, devices, tile_rows), wide)),
        in_specs=[vmem] * 5,
        out_specs=(far, vmem),
        scratch_shapes=[
            pltpu.VMEM((devices, slot, tile_rows), low),
            pltpu.VMEM((3 * devices, tile_rows), wide),
            dma(()),
        ],
        compiler_params=pltpu.CompilerParams(
            vmem_limit_bytes=vmem_grant
        ),
        name="serve",
    )(*keep(info, recv_q, kv, vkt, table))
    recv_b = lax.all_to_all(send_b, "ctx", split_axis=0, concat_axis=0, tiled=True)

    pairs_in, qgt_in, lists_in = pl.pallas_call(
        again_kernel(groups, tile_rows, head_dim, devices),
        out_shape=(near(in_shape, low), near((devices - 1, width, tile_rows), low), near((devices, 8, width), wide)),
        in_specs=[smem, vmem, vmem, vmem],
        out_specs=(vmem, vmem, vmem),
        compiler_params=small,
        name="again",
    )(*away(picks), *keep(recv_q, kv, inverse_in))

    mix_shape = (groups, tiles_dev, 3 * head_dim, tile_rows)
    pair_shape = (groups, row_count, 2 * row_count)
    turned_shape = (groups, width, row_count)
    qgt, mix, pairs = pl.pallas_call(
        rest_kernel(tiles_dev, groups, tile_rows, head_dim),
        out_shape=(pltpu.HBM(turned_shape, low), pltpu.HBM(mix_shape, low), pltpu.HBM(pair_shape, low)),
        in_specs=[far] * 2 + [vmem] * 3,
        out_specs=tuple([far] * 3),
        scratch_shapes=[pltpu.VMEM((row_count, columns), low)] * 2
        + [
            pltpu.VMEM(turned_shape, low),
            pltpu.VMEM(mix_shape, low),
            pltpu.VMEM(pair_shape, low),
            dma((2,)),
            dma((tiles_dev + 2,)),
        ],
        compiler_params=small,
        name="rest",
    )(*away(query, grad_out), *keep(kv, vkt, stats))

    return pl.pallas_call(
        final_kernel(tiles_dev, groups, picked, tile_rows, head_dim, devices),
        out_shape=tuple([shape((row_count, columns), low)] * 4),
        in_specs=[vmem] * 7 + [far] * 3,
        out_specs=tuple([far] * 4),
        scratch_shapes=[
            pltpu.VMEM((groups, width, row_count), low),
            pltpu.VMEM(mix_shape, low),
            pltpu.VMEM(pair_shape, low),
        ]
        + [pltpu.VMEM((row_count, columns), low)] * 4
        + [
            pltpu.VMEM((2, tasks, head_dim, tile_rows), wide),
            pltpu.VMEM((groups, row_count, width), wide),
            pltpu.VMEM((groups, row_count, width), wide),
            pltpu.VMEM((devices, devices, tile_rows), wide),
            pltpu.VMEM((devices, devices, tile_rows), wide),
            pltpu.VMEM((3, devices, tile_rows), wide),
            pltpu.VMEM((9, tasks, tile_rows), wide),
            pltpu.VMEM((groups, width, 2 * row_count), low),
            pltpu.VMEM((devices, width, 2 * tile_rows), low),
            dma((tiles_dev + 2,)),
            dma((4,)),
        ],
        compiler_params=small,
        name="final",
    )(*keep(info, lists_in, recv_b, qgt_in, stats, inverse_in, pairs_in), *away(qgt, mix, pairs))


def choose(query, key, value, grad_out, picks):
    pair_bytes = lax.axis_size("ctx") * query.shape[0] * (query.shape[0] // picks.shape[0]) * 4
    plan = fast_local if pair_bytes <= pair_budget else local
    return plan(query, key, value, grad_out, picks)


def solution(mesh):
    placed = (
        P("ctx", "head"),
        P("ctx", "head"),
        P("ctx", "head"),
        P("ctx", "head"),
        P("ctx", "head", None),
    )
    return jax.shard_map(
        choose,
        mesh=mesh,
        in_specs=placed,
        out_specs=(P("ctx", "head"), P("ctx", "head"), P("ctx", "head"), P("ctx", "head")),
        check_vma=False,
    )
```

```python
import math

import jax
import jax.numpy as jnp
from jax import lax
from jax.experimental import pallas as pl
from jax.experimental.pallas import tpu as pltpu
from jax.sharding import PartitionSpec as P

masked_value = -1e30
highest = lax.Precision.HIGHEST
LOG2E = math.log2(math.e)
pair_budget = 8 << 20
vmem_grant = 32 << 20


def attend_slots(q_slots, head_ids, k_heads, v_heads, scaling):
    key_rows = jnp.take(k_heads, head_ids, axis=0)
    value_rows = jnp.take(v_heads, head_ids, axis=0)
    scores = (
        jnp.einsum("ndq,nkd->nqk", q_slots, key_rows, preferred_element_type=jnp.float32) * scaling
    )
    peak_score = jnp.max(scores, axis=-1, keepdims=True)
    log_total = peak_score + jnp.log(jnp.sum(jnp.exp(scores - peak_score), axis=-1, keepdims=True))
    attend_low = jnp.exp(scores - log_total).astype(jnp.bfloat16)
    outputs = jnp.einsum("nqk,nkd->ndq", attend_low, value_rows, preferred_element_type=jnp.float32)
    return (outputs, log_total[..., 0])


def slot_grads(q_slots, g_slots, c_slots, lse_slots, head_ids, k_heads, v_heads, scaling):
    key_rows = jnp.take(k_heads, head_ids, axis=0)
    value_rows = jnp.take(v_heads, head_ids, axis=0)
    scores = (
        jnp.einsum("ndq,nkd->nqk", q_slots, key_rows, preferred_element_type=jnp.float32) * scaling
    )
    attend = jnp.exp(scores - lse_slots[..., None])
    attend_low = attend.astype(jnp.bfloat16)
    grad_v = jnp.einsum("nqk,ndq->nkd", attend_low, g_slots, preferred_element_type=jnp.float32)
    grad_prob = jnp.einsum("ndq,nkd->nqk", g_slots, value_rows, preferred_element_type=jnp.float32)
    dscore = (attend * (grad_prob - c_slots[..., None])).astype(jnp.bfloat16)
    grad_k = (
        jnp.einsum("nqk,ndq->nkd", dscore, q_slots, preferred_element_type=jnp.float32) * scaling
    )
    grad_q = (
        jnp.einsum("nqk,nkd->ndq", dscore, key_rows, preferred_element_type=jnp.float32) * scaling
    )
    return (grad_k, grad_v, grad_q)


def local(query, key, value, grad_out, picks):
    row_count, columns = query.shape
    tiles_dev, groups, picked = picks.shape
    head_dim = columns // groups
    tile_rows = row_count // tiles_dev
    others = picked - 1
    scaling = 1.0 / math.sqrt(head_dim)
    devices = lax.axis_size("ctx")
    own_block = lax.axis_index("ctx")
    per_group = min(8, devices)
    all_picks = lax.all_gather(picks, "ctx", axis=0, tiled=True)
    q_heads = query.reshape(row_count, groups, head_dim).transpose(1, 0, 2)
    k_heads = key.reshape(row_count, groups, head_dim).transpose(1, 0, 2)
    v_heads = value.reshape(row_count, groups, head_dim).transpose(1, 0, 2)
    q_tiles = query.reshape(tiles_dev, tile_rows, groups, head_dim)
    do_tiles = grad_out.reshape(tiles_dev, tile_rows, groups, head_dim)
    do_major = do_tiles.transpose(0, 2, 1, 3)
    positions = jnp.arange(row_count, dtype=jnp.int32)
    tile_masks = []
    for tile_step in range(tiles_dev):
        span = (tile_step + 1) * tile_rows
        query_pos = positions[tile_step * tile_rows : span]
        tile_masks.append(positions[None, :span] <= query_pos[:, None])
    targets = picks[:, :, 1:]
    active = targets != own_block
    lookup = jnp.where(active, targets, own_block).reshape(-1)
    peer_ids = jnp.arange(devices, dtype=jnp.int32)
    routing = ((targets[None] == peer_ids[:, None, None, None]) & active[None]).astype(jnp.float32)
    routing_low = routing.astype(jnp.bfloat16)
    send_q = jnp.einsum(
        "jtgi,tqgd->jdq", routing_low, q_tiles, preferred_element_type=jnp.float32
    ).astype(jnp.bfloat16)
    recv_q = lax.all_to_all(send_q, "ctx", split_axis=0, concat_axis=0, tiled=True)

    def own_forward(inputs):
        q_head, k_head, v_head = inputs
        out_list = []
        lse_list = []
        for tile_step in range(tiles_dev):
            span = (tile_step + 1) * tile_rows
            q_part = q_head[tile_step * tile_rows : span]
            scores = (
                jnp.einsum("qd,kd->qk", q_part, k_head[:span], preferred_element_type=jnp.float32)
                * scaling
            )
            scores = jnp.where(tile_masks[tile_step], scores, masked_value)
            peak_score = jnp.max(scores, axis=-1, keepdims=True)
            log_total = peak_score + jnp.log(
                jnp.sum(jnp.exp(scores - peak_score), axis=-1, keepdims=True)
            )
            attend_low = jnp.exp(scores - log_total).astype(jnp.bfloat16)
            out_list.append(jnp.dot(attend_low, v_head[:span], preferred_element_type=jnp.float32))
            lse_list.append(log_total[:, 0])
        return (jnp.concatenate(out_list, axis=0), jnp.concatenate(lse_list, axis=0))

    own_out, own_lse = lax.map(own_forward, (q_heads, k_heads, v_heads))
    sources = all_picks.reshape(devices, tiles_dev, groups, picked)[..., 1:]
    incoming = (sources == own_block) & (peer_ids[:, None, None, None] != own_block)
    live_in = jnp.any(incoming, axis=(1, 2, 3))
    group_ids = jnp.arange(groups, dtype=jnp.int32)
    head_of = jnp.sum(jnp.where(incoming, group_ids[None, None, :, None], 0), axis=(1, 2, 3))
    ranking = jnp.argsort(jnp.where(live_in, 0, 1) * devices + peer_ids)
    inverse = jnp.argsort(ranking)
    rounds = (jnp.sum(live_in.astype(jnp.int32)) + per_group - 1) // per_group
    heads_sorted = jnp.take(head_of, ranking, axis=0)
    q_sorted = jnp.take(recv_q, ranking, axis=0)

    def forward_turn(turn, totals):
        served_out, served_lse = totals
        offset = turn * per_group
        query_part = lax.dynamic_slice_in_dim(q_sorted, offset, per_group, 0)
        head_part = lax.dynamic_slice_in_dim(heads_sorted, offset, per_group, 0)
        out_part, lse_part = attend_slots(query_part, head_part, k_heads, v_heads, scaling)
        served_out = lax.dynamic_update_slice_in_dim(served_out, out_part, offset, 0)
        served_lse = lax.dynamic_update_slice_in_dim(served_lse, lse_part, offset, 0)
        return (served_out, served_lse)

    start_fwd = (
        jnp.zeros((devices, head_dim, tile_rows), jnp.float32),
        jnp.zeros((devices, tile_rows), jnp.float32),
    )
    served_out, served_lse = lax.fori_loop(0, rounds, forward_turn, start_fwd)
    back_out, back_lse = (
        lax.all_to_all(
            jnp.take(served_out, inverse, axis=0), "ctx", split_axis=0, concat_axis=0, tiled=True
        ),
        lax.all_to_all(
            jnp.take(served_lse, inverse, axis=0), "ctx", split_axis=0, concat_axis=0, tiled=True
        ),
    )
    task_out = jnp.take(back_out, lookup, axis=0).reshape(
        tiles_dev, groups, others, head_dim, tile_rows
    )
    task_lse = jnp.take(back_lse, lookup, axis=0).reshape(tiles_dev, groups, others, tile_rows)
    own_out_t = own_out.reshape(groups, tiles_dev, tile_rows, head_dim).transpose(1, 0, 2, 3)
    own_lse_t = own_lse.reshape(groups, tiles_dev, tile_rows).transpose(1, 0, 2)
    active_rows = active[..., None]
    rem_lse = jnp.where(active_rows, task_lse, masked_value)
    ceiling = jnp.maximum(own_lse_t, jnp.max(rem_lse, axis=2))
    log_total = ceiling + jnp.log(
        jnp.exp(own_lse_t - ceiling) + jnp.sum(jnp.exp(rem_lse - ceiling[:, :, None]), axis=2)
    )
    own_weight = jnp.exp(own_lse_t - log_total)
    rem_weight = jnp.where(active_rows, jnp.exp(rem_lse - log_total[:, :, None]), 0.0)
    mixed = own_weight[..., None] * own_out_t + jnp.einsum(
        "tgiq,tgidq->tgqd", rem_weight, task_out, precision=highest
    )
    out_low = mixed.astype(jnp.bfloat16)
    attn_out = out_low.transpose(0, 2, 1, 3).reshape(row_count, columns)
    row_delta = jnp.sum(do_major.astype(jnp.float32) * out_low.astype(jnp.float32), axis=-1)
    own_scaled = (own_weight[..., None] * do_major.astype(jnp.float32)).astype(jnp.bfloat16)
    own_shift = own_weight * row_delta
    g_heads = own_scaled.transpose(1, 0, 2, 3).reshape(groups, row_count, head_dim)
    c_heads = own_shift.transpose(1, 0, 2).reshape(groups, row_count)

    def own_backward(inputs):
        q_head, k_head, v_head, g_head, c_head, lse_head = inputs
        grad_k = jnp.zeros((row_count, head_dim), jnp.float32)
        grad_v = jnp.zeros((row_count, head_dim), jnp.float32)
        dq_list = []
        for tile_step in range(tiles_dev):
            first = tile_step * tile_rows
            span = (tile_step + 1) * tile_rows
            q_part = q_head[first:span]
            g_part = g_head[first:span]
            k_part = k_head[:span]
            scores = (
                jnp.einsum("qd,kd->qk", q_part, k_part, preferred_element_type=jnp.float32)
                * scaling
            )
            scores = jnp.where(tile_masks[tile_step], scores, masked_value)
            attend = jnp.exp(scores - lse_head[first:span, None])
            attend_low = attend.astype(jnp.bfloat16)
            part_dv = jnp.einsum(
                "qk,qd->kd", attend_low, g_part, preferred_element_type=jnp.float32
            )
            grad_prob = jnp.einsum(
                "qd,kd->qk", g_part, v_head[:span], preferred_element_type=jnp.float32
            )
            dscore = (attend * (grad_prob - c_head[first:span, None])).astype(jnp.bfloat16)
            part_dk = (
                jnp.einsum("qk,qd->kd", dscore, q_part, preferred_element_type=jnp.float32)
                * scaling
            )
            dq_list.append(jnp.dot(dscore, k_part, preferred_element_type=jnp.float32) * scaling)
            padding = ((0, row_count - span), (0, 0))
            grad_k = grad_k + jnp.pad(part_dk, padding)
            grad_v = grad_v + jnp.pad(part_dv, padding)
        return (grad_k, grad_v, jnp.concatenate(dq_list, axis=0))

    own_dk, own_dv, own_dq = lax.map(
        own_backward, (q_heads, k_heads, v_heads, g_heads, c_heads, own_lse)
    )
    rem_shift = rem_weight * row_delta[:, :, None]
    rem_scaled = (rem_weight[..., None] * do_major[:, :, None].astype(jnp.float32)).astype(
        jnp.bfloat16
    )
    send_g = jnp.einsum(
        "jtgi,tgiqd->jdq", routing_low, rem_scaled, preferred_element_type=jnp.float32
    )
    send_c = jnp.einsum("jtgi,tgiq->jq", routing, rem_shift, precision=highest)
    recv_g, recv_c = (
        lax.all_to_all(send_g, "ctx", split_axis=0, concat_axis=0, tiled=True),
        lax.all_to_all(send_c, "ctx", split_axis=0, concat_axis=0, tiled=True),
    )
    g_sorted = jnp.take(recv_g, ranking, axis=0).astype(jnp.bfloat16)
    c_sorted = jnp.take(recv_c, ranking, axis=0)

    def backward_turn(turn, totals):
        grad_k, grad_v, served_dq = totals
        offset = turn * per_group
        query_part = lax.dynamic_slice_in_dim(q_sorted, offset, per_group, 0)
        cot_part = lax.dynamic_slice_in_dim(g_sorted, offset, per_group, 0)
        shift_part = lax.dynamic_slice_in_dim(c_sorted, offset, per_group, 0)
        lse_part = lax.dynamic_slice_in_dim(served_lse, offset, per_group, 0)
        head_part = lax.dynamic_slice_in_dim(heads_sorted, offset, per_group, 0)
        part_dk, part_dv, part_dq = slot_grads(
            query_part, cot_part, shift_part, lse_part, head_part, k_heads, v_heads, scaling
        )
        head_onehot = (head_part[:, None] == group_ids[None, :]).astype(jnp.float32)
        grad_k = grad_k + jnp.einsum("ng,nkd->gkd", head_onehot, part_dk, precision=highest)
        grad_v = grad_v + jnp.einsum("ng,nkd->gkd", head_onehot, part_dv, precision=highest)
        served_dq = lax.dynamic_update_slice_in_dim(served_dq, part_dq, offset, 0)
        return (grad_k, grad_v, served_dq)

    zeros_heads = jnp.zeros((groups, row_count, head_dim), jnp.float32)
    start_bwd = (zeros_heads, zeros_heads, jnp.zeros((devices, head_dim, tile_rows), jnp.float32))
    rem_dk, rem_dv, served_dq = lax.fori_loop(0, rounds, backward_turn, start_bwd)
    back_dq = lax.all_to_all(
        jnp.take(served_dq, inverse, axis=0).astype(jnp.bfloat16),
        "ctx",
        split_axis=0,
        concat_axis=0,
        tiled=True,
    ).astype(jnp.float32)
    task_dq = jnp.take(back_dq, lookup, axis=0).reshape(
        tiles_dev, groups, others, head_dim, tile_rows
    )
    rem_dq = jnp.sum(jnp.where(active[..., None, None], task_dq, 0.0), axis=2)
    own_dq_t = own_dq.reshape(groups, tiles_dev, tile_rows, head_dim).transpose(1, 0, 2, 3)
    total_dq = own_dq_t + rem_dq.transpose(0, 1, 3, 2)
    grad_query = total_dq.transpose(0, 2, 1, 3).reshape(row_count, columns).astype(jnp.bfloat16)
    grad_key = (own_dk + rem_dk).transpose(1, 0, 2).reshape(row_count, columns).astype(jnp.bfloat16)
    grad_value = (
        (own_dv + rem_dv).transpose(1, 0, 2).reshape(row_count, columns).astype(jnp.bfloat16)
    )
    return (attn_out, grad_query, grad_key, grad_value)


def fill_factor(x_ref, qgt_ref, head, tile, first, second, third, tile_rows, head_dim):
    v_rows = slice(0, head_dim) if head % 2 == 0 else slice(head_dim, 2 * head_dim)
    k_rows = slice(head_dim, 2 * head_dim) if head % 2 == 0 else slice(0, head_dim)
    turned = qgt_ref[head, :, tile * tile_rows : (tile + 1) * tile_rows].astype(jnp.float32)
    early = slice(tile * 2 * tile_rows, tile * 2 * tile_rows + tile_rows)
    late = slice(tile * 2 * tile_rows + tile_rows, (tile + 1) * 2 * tile_rows)
    x_ref[head, v_rows, early] = (turned[head_dim:] * first).astype(jnp.bfloat16)
    x_ref[head, v_rows, late] = jnp.zeros((head_dim, tile_rows), jnp.bfloat16)
    x_ref[head, k_rows, early] = (turned[:head_dim] * second).astype(jnp.bfloat16)
    x_ref[head, k_rows, late] = (turned[:head_dim] * third).astype(jnp.bfloat16)


def pair_parts(near, far, tiles_dev, tile_rows):
    for part in range(tiles_dev):
        rows = slice(part * tile_rows, (part + 1) * tile_rows)
        cols = slice(part * 2 * tile_rows, tiles_dev * 2 * tile_rows)
        yield near.at[:, rows, cols], far.at[:, rows, cols]


def dot_t(a, b):
    return lax.dot_general(a, b, (((1,), (1,)), ((), ())), preferred_element_type=jnp.float32)


def split_low(x):
    high = x.astype(jnp.bfloat16).astype(jnp.float32)
    return high, x - high


def halves(block, head_dim):
    lane = lax.broadcasted_iota(jnp.int32, block.shape, 1)
    zero = jnp.zeros_like(block)
    return jnp.where(lane < head_dim, block, zero), jnp.where(lane < head_dim, zero, block)


def pack_kernel(tiles_dev, groups, picked, tile_rows, head_dim, devices):
    def body(picks_ref, q_ref, g_ref, send_ref, task_ref):
        own = picks_ref[0, 0, 0]
        meta_rows = send_ref.shape[1] - tile_rows
        lanes = send_ref.shape[2]
        row = lax.broadcasted_iota(jnp.int32, (meta_rows, lanes), 0)
        blank = jnp.zeros((meta_rows, lanes), jnp.bfloat16)
        for peer in range(devices):
            send_ref[peer, tile_rows:, :] = blank
            task_ref[peer] = -1
        for tile in range(tiles_dev):
            rows = slice(tile * tile_rows, (tile + 1) * tile_rows)
            for head in range(groups):
                cols = slice(head * head_dim, (head + 1) * head_dim)
                block = jnp.concatenate([q_ref[rows, cols], g_ref[rows, cols]], axis=1)
                code = tile * groups + head
                meta = jnp.where(row == 0, code + 1, 0)
                for entry in range(1, picked):
                    meta = jnp.where(row == entry, picks_ref[tile, head, entry], meta)
                meta = meta.astype(jnp.float32).astype(jnp.bfloat16)
                for entry in range(1, picked):
                    target = picks_ref[tile, head, entry]
                    send_ref[target, :tile_rows, :] = block
                    send_ref[target, tile_rows:, :] = meta
                    task_ref[target] = code
        task_ref[own] = -1

    return body


def own_kernel(tiles_dev, groups, tile_rows, head_dim, devices):
    scale = LOG2E / math.sqrt(head_dim)

    def body(picks_ref, task_ref, q_hbm, k_hbm, v_hbm, g_hbm, kv_ref, vkt_ref, stat_ref, table_ref, info_ref,
             q_ref, k_ref, v_ref, g_ref, rows_ref, in_sem):
        loads = [
            pltpu.make_async_copy(src, dst, in_sem.at[index])
            for index, (src, dst) in enumerate(((k_hbm, k_ref), (v_hbm, v_ref), (q_hbm, q_ref), (g_hbm, g_ref)))
        ]
        for load in loads:
            load.start()
        for load in loads:
            load.wait()
        sub = lax.broadcasted_iota(jnp.int32, (tile_rows, tile_rows), 0)
        lane = lax.broadcasted_iota(jnp.int32, (tile_rows, tile_rows), 1)
        causal = sub <= lane
        for head in range(groups):
            cols = slice(head * head_dim, (head + 1) * head_dim)
            kv_ref[head] = jnp.concatenate([k_ref[:, cols], v_ref[:, cols]], axis=1)

        def product(code):
            tile, head = code // groups, code % groups
            cols = slice(head * head_dim, (head + 1) * head_dim)
            rows = slice(tile * tile_rows, (tile + 1) * tile_rows)
            block = jnp.concatenate([q_ref[rows, cols], g_ref[rows, cols]], axis=1)
            return dot_t(kv_ref[head, : rows.stop, :], jnp.concatenate(halves(block, head_dim), axis=0))

        ahead = product(0)
        for code in range(tiles_dev * groups):
            both = ahead
            if code + 1 < tiles_dev * groups:
                ahead = product(code + 1)
            tile = code // groups
            split = tile * tile_rows
            last = jnp.where(causal, both[split:, :tile_rows], masked_value)
            peak = jnp.max(last, axis=0, keepdims=True)
            if tile:
                peak = jnp.maximum(peak, jnp.max(both[:split, :tile_rows], axis=0, keepdims=True))
            peak = peak * scale
            powers = jnp.exp2(last * scale - peak)
            total = jnp.sum(powers, axis=0, keepdims=True)
            mean_grad = jnp.sum(powers * both[split:, tile_rows:], axis=0, keepdims=True)
            if tile:
                powers = jnp.exp2(both[:split, :tile_rows] * scale - peak)
                total = total + jnp.sum(powers, axis=0, keepdims=True)
                mean_grad = mean_grad + jnp.sum(powers * both[:split, tile_rows:], axis=0, keepdims=True)
            inverse = 1.0 / total
            mean_grad = mean_grad * inverse
            lse = peak + jnp.log2(total)
            for index, value in enumerate((lse, mean_grad, inverse, peak)):
                stat_ref[index, code : code + 1, :] = value
            for index, value in enumerate(split_low(lse) + (mean_grad,)):
                rows_ref[code, index : index + 1, :] = value
        for head in range(groups):
            cols = slice(head * head_dim, (head + 1) * head_dim)
            vkt_ref[head] = jnp.concatenate([v_ref[:, cols], k_ref[:, cols]], axis=1).T
        sub = lax.broadcasted_iota(jnp.int32, (devices, tile_rows), 0)
        codes = jnp.full((devices, tile_rows), -1, jnp.int32)
        for peer in range(devices):
            codes = jnp.where(sub == peer, task_ref[peer], codes)
            table_ref[peer] = rows_ref[jnp.maximum(task_ref[peer], 0)]
        info_ref[:devices, :] = codes.astype(jnp.float32)
        info_ref[devices:, :] = jnp.full((devices, tile_rows), picks_ref[0, 0, 0], jnp.int32).astype(jnp.float32)

    return body


def rest_kernel(tiles_dev, groups, tile_rows, head_dim, devices):
    scale = LOG2E / math.sqrt(head_dim)

    def body(q_hbm, g_hbm, kv_ref, vkt_ref, stat_ref, info_ref, qgt_hbm, mix_hbm, pd_hbm, base_hbm,
             q_ref, g_ref, qgt_ref, mix_ref, pd_ref, base_ref, x_ref, d_ref, in_sem, out_sem):
        loads = [
            pltpu.make_async_copy(src, dst, in_sem.at[index])
            for index, (src, dst) in enumerate(((q_hbm, q_ref), (g_hbm, g_ref)))
        ]
        for load in loads:
            load.start()
        for load in loads:
            load.wait()
        sub = lax.broadcasted_iota(jnp.int32, (tile_rows, tile_rows), 0)
        lane = lax.broadcasted_iota(jnp.int32, (tile_rows, tile_rows), 1)
        causal = sub <= lane

        def product(code):
            tile, head = code // groups, code % groups
            cols = slice(head * head_dim, (head + 1) * head_dim)
            rows = slice(tile * tile_rows, (tile + 1) * tile_rows)
            block = jnp.concatenate([q_ref[rows, cols], g_ref[rows, cols]], axis=1)
            qgt_ref[head, :, rows] = block.T
            return dot_t(kv_ref[head, : rows.stop, :], jnp.concatenate(halves(block, head_dim), axis=0))

        ahead = product(0)
        for code in range(tiles_dev * groups):
            both = ahead
            if code + 1 < tiles_dev * groups:
                ahead = product(code + 1)
            tile, head = code // groups, code % groups
            span = (tile + 1) * tile_rows
            at = tile * 2 * tile_rows
            peak = stat_ref[3, code : code + 1, :]
            inverse = stat_ref[2, code : code + 1, :]
            for part in range(tile + 1):
                chunk = slice(part * tile_rows, (part + 1) * tile_rows)
                scores = both[chunk, :tile_rows]
                if part == tile:
                    scores = jnp.where(causal, scores, masked_value)
                powers = jnp.exp2(scores * scale - peak)
                spread = powers * both[chunk, tile_rows:]
                pd_ref[head, chunk, at : at + tile_rows] = powers.astype(jnp.bfloat16)
                pd_ref[head, chunk, at + tile_rows : at + 2 * tile_rows] = spread.astype(jnp.bfloat16)
            result = jnp.dot(vkt_ref[head, :, :span], pd_ref[head, :span, at : at + 2 * tile_rows],
                             preferred_element_type=jnp.float32)
            mix_ref[head, tile, : 2 * head_dim, :] = (result[:, :tile_rows] * inverse).astype(jnp.bfloat16)
            mix_ref[head, tile, 2 * head_dim :, :] = (result[head_dim:, tile_rows:] * inverse).astype(jnp.bfloat16)
        ids = lax.broadcasted_iota(jnp.int32, (tiles_dev * groups, tile_rows), 0).astype(jnp.float32)
        named = ids < 0
        for peer in range(devices):
            named = named | (ids == info_ref[peer : peer + 1, :])
        alone = jnp.where(named, 0.0, stat_ref[2])
        d_ref[0] = alone
        d_ref[1] = alone * stat_ref[1] * (-1.0 / math.sqrt(head_dim))
        d_ref[2] = alone * (1.0 / math.sqrt(head_dim))
        for head in range(groups):
            for tile in range(tiles_dev):
                code = tile * groups + head
                fill_factor(x_ref, qgt_ref, head, tile, *(d_ref[i, code : code + 1, :] for i in range(3)), tile_rows, head_dim)
            for part in range(tiles_dev):
                rows = slice(part * tile_rows, (part + 1) * tile_rows)
                cols = slice(part * 2 * tile_rows, tiles_dev * 2 * tile_rows)
                base_ref[head, rows, :] = dot_t(pd_ref[head, rows, cols], x_ref[head, :, cols])
        stores = [
            pltpu.make_async_copy(mix_ref, mix_hbm, out_sem.at[tiles_dev]),
            pltpu.make_async_copy(qgt_ref, qgt_hbm, out_sem.at[tiles_dev + 1]),
            pltpu.make_async_copy(base_ref, base_hbm, out_sem.at[tiles_dev + 2]),
        ] + [
            pltpu.make_async_copy(src, dst, out_sem.at[index])
            for index, (src, dst) in enumerate(pair_parts(pd_ref, pd_hbm, tiles_dev, tile_rows))
        ]
        for store in stores:
            store.start()
        for store in stores:
            store.wait()

    return body


def parts_of(block, kv_head, tile_rows, head_dim, scale):
    both = dot_t(kv_head, jnp.concatenate(halves(block, head_dim), axis=0))
    scores = both[:, :tile_rows]
    peak = jnp.max(scores, axis=0, keepdims=True) * scale
    powers = jnp.exp2(scores * scale - peak)
    spread = powers * both[:, tile_rows:]
    return peak, powers, spread


def serve_kernel(groups, tile_rows, head_dim, devices):
    scale = LOG2E / math.sqrt(head_dim)

    def body(info_ref, recv_ref, kv_ref, vkt_ref, table_ref, send_hbm, inv_ref,
             send_ref, st_ref, out_sem):
        own = jnp.max(info_ref[devices : devices + 1, :]).astype(jnp.int32)
        st_ref[...] = jnp.zeros_like(st_ref)
        inv_ref[...] = jnp.zeros_like(inv_ref)
        heads = [None]
        blocks = [None]
        for source in range(1, devices):
            code = jnp.max(recv_ref[source, tile_rows:, :].astype(jnp.float32)[0:1, :]).astype(jnp.int32) - 1
            block = recv_ref[source, :tile_rows, :]
            heads.append(lax.rem(jnp.maximum(code, 0), groups))
            blocks.append(jnp.where((code >= 0) & (own != source), block, jnp.zeros_like(block)))
        ahead = parts_of(blocks[1], kv_ref[heads[1]], tile_rows, head_dim, scale)
        for source in range(1, devices):
            peak, powers, spread = ahead
            if source + 1 < devices:
                ahead = parts_of(blocks[source + 1], kv_ref[heads[source + 1]], tile_rows, head_dim, scale)
            total = jnp.sum(powers, axis=0, keepdims=True)
            inverse = 1.0 / total
            mean_grad = jnp.sum(spread, axis=0, keepdims=True) * inverse
            both = jnp.concatenate([powers.astype(jnp.bfloat16), spread.astype(jnp.bfloat16)], axis=1)
            result = jnp.dot(vkt_ref[heads[source]], both, preferred_element_type=jnp.float32)
            send_ref[source, : 2 * head_dim, :] = (result[:, :tile_rows] * inverse).astype(jnp.bfloat16)
            send_ref[source, 2 * head_dim : 3 * head_dim, :] = (result[head_dim:, tile_rows:] * inverse).astype(jnp.bfloat16)
            parts = split_low(peak + jnp.log2(total)) + (mean_grad,)
            for index in range(3):
                st_ref[index * devices + source : index * devices + source + 1, :] = parts[index]
            inv_ref[0, source : source + 1, :] = inverse
            inv_ref[1, source : source + 1, :] = peak
        table = st_ref[...]
        row = lax.broadcasted_iota(jnp.int32, table.shape, 0)
        mine = lax.rem(row, devices) == own
        for peer in range(devices):
            entry = table_ref[peer]
            wide = jnp.concatenate(
                [jnp.broadcast_to(entry[index : index + 1], (devices, tile_rows)) for index in range(3)], axis=0
            )
            send_ref[peer, 3 * head_dim :, :] = jnp.where(mine, wide, table).astype(jnp.bfloat16)
        store = pltpu.make_async_copy(send_ref, send_hbm, out_sem)
        store.start()
        store.wait()

    return body


def again_kernel(groups, tile_rows, head_dim, devices):
    scale = LOG2E / math.sqrt(head_dim)

    def body(picks_ref, recv_ref, kv_ref, inv_ref, pd_ref, qgt_ref, meta_ref):
        own = picks_ref[0, 0, 0]
        for source in range(devices):
            meta_ref[source] = recv_ref[source, tile_rows:, :].astype(jnp.float32)
        codes = [jnp.max(recv_ref[source, tile_rows:, :].astype(jnp.float32)[0:1, :]).astype(jnp.int32) - 1
                 for source in range(devices)]

        def product(source):
            block = recv_ref[source, :tile_rows, :]
            block = jnp.where((codes[source] >= 0) & (own != source), block, jnp.zeros_like(block))
            qgt_ref[source - 1] = block.T
            head = lax.rem(jnp.maximum(codes[source], 0), groups)
            return dot_t(kv_ref[head], jnp.concatenate(halves(block, head_dim), axis=0))

        ahead = product(1)
        for source in range(1, devices):
            both = ahead
            if source + 1 < devices:
                ahead = product(source + 1)
            powers = jnp.exp2(both[:, :tile_rows] * scale - inv_ref[1, source : source + 1, :])
            pd_ref[source - 1, :, :tile_rows] = powers.astype(jnp.bfloat16)
            pd_ref[source - 1, :, tile_rows:] = (powers * both[:, tile_rows:]).astype(jnp.bfloat16)

    return body


def final_kernel(tiles_dev, groups, picked, tile_rows, head_dim, devices):
    scaling = 1.0 / math.sqrt(head_dim)
    pair = 2 * tile_rows

    def body(info_ref, meta_ref, back_ref, qgt_in_ref, stat_ref, inv_ref,
             pd_in_ref, qgt_hbm, mix_hbm, pd_hbm, base_hbm, out_hbm, dq_hbm, dk_hbm, dv_hbm,
             qgt_ref, mix_ref, pd_ref, out_ref, dq_ref, dk_ref, dv_ref, acc_ref, base_ref, grad_ref,
             lse_sc, gd_sc, w_sc, d_sc, x_ref, xin_ref, in_sem, out_sem):
        own = jnp.max(info_ref[devices : devices + 1, :]).astype(jnp.int32)
        given = [jnp.max(info_ref[peer : peer + 1, :]).astype(jnp.int32) for peer in range(devices)]
        tasks = tiles_dev * groups
        base = 3 * head_dim
        named = []
        for code in range(tasks):
            hit = given[0] == code
            for peer in range(1, devices):
                hit = hit | (given[peer] == code)
            named.append(hit)
        loads = [
            pltpu.make_async_copy(src, dst, in_sem.at[index])
            for index, (src, dst) in enumerate(((mix_hbm, mix_ref), (qgt_hbm, qgt_ref), (base_hbm, base_ref)))
        ]
        for load in loads:
            load.start()

        def own_pairs(code):
            tile, head = code // groups, code % groups
            at = (head, slice(0, (tile + 1) * tile_rows), slice(tile * pair, (tile + 1) * pair))
            return pltpu.make_async_copy(pd_hbm.at[at], pd_ref.at[at], in_sem.at[3 + code])

        for code in range(tasks):

            @pl.when(named[code])
            def _(code=code):
                own_pairs(code).start()

        grad_ref[...] = jnp.zeros_like(grad_ref)

        lse_of = []
        gd_of = []
        for peer in range(devices):
            table = back_ref[peer, base:, :].astype(jnp.float32)
            lse_of.append(table[:devices] + table[devices : 2 * devices])
            gd_of.append(table[2 * devices :])
            lse_sc[peer] = lse_of[peer]
            gd_sc[peer] = gd_of[peer]

        ids = lax.broadcasted_iota(jnp.int32, (devices, tile_rows), 0)
        metas = [meta_ref[source] for source in range(devices)]
        rows_of = [
            jnp.concatenate([metas[source][entry : entry + 1] for source in range(devices)], axis=0).astype(jnp.int32)
            for entry in range(picked)
        ]
        codes = [None] + [jnp.max(metas[source][0:1, :]).astype(jnp.int32) - 1 for source in range(1, devices)]
        live = (rows_of[0] > 0) & (ids != own)
        chosen = []
        for peer in range(devices):
            active = ids == peer
            for entry in rows_of[1:]:
                active = active | (entry == peer)
            chosen.append(active)
        peak = jnp.full((devices, tile_rows), masked_value, jnp.float32)
        for peer in range(devices):
            peak = jnp.maximum(peak, jnp.where(chosen[peer], lse_of[peer], masked_value))
        total = jnp.zeros_like(peak)
        delta = jnp.zeros_like(peak)
        for peer in range(devices):
            power = jnp.where(chosen[peer], jnp.exp2(lse_of[peer] - peak), 0.0)
            total = total + power
            delta = delta + jnp.where(chosen[peer], power * gd_of[peer], 0.0)
        delta = delta / total
        weight = jnp.exp2(lse_sc[own] - peak) / total * inv_ref[0]
        weight = jnp.where(live, weight, 0.0)
        w_sc[0] = weight
        w_sc[1] = jnp.where(live, weight * delta * -scaling, 0.0)
        w_sc[2] = weight * scaling

        code_ids = lax.broadcasted_iota(jnp.int32, (tasks, tile_rows), 0)
        own_lse = stat_ref[0]
        own_gd = stat_ref[1]
        peak = own_lse
        rows_lse = [lse_sc[peer, pl.ds(own, 1), :] for peer in range(devices)]
        rows_gd = [gd_sc[peer, pl.ds(own, 1), :] for peer in range(devices)]
        for peer in range(devices):
            peak = jnp.maximum(peak, jnp.where(code_ids == given[peer], rows_lse[peer], masked_value))
        own_power = jnp.exp2(own_lse - peak)
        total = own_power
        delta = own_power * own_gd
        for peer in range(devices):
            here = code_ids == given[peer]
            power = jnp.where(here, jnp.exp2(rows_lse[peer] - peak), 0.0)
            total = total + power
            delta = delta + jnp.where(here, power * rows_gd[peer], 0.0)
        inverse = 1.0 / total
        delta = delta * inverse
        own_weight = own_power * inverse
        d_sc[0] = peak
        d_sc[1] = inverse
        d_sc[2] = delta
        d_sc[3] = own_weight
        d_sc[4] = own_weight * stat_ref[2]
        d_sc[5] = own_weight * stat_ref[2] * delta * -scaling
        d_sc[6] = own_weight * delta * -scaling
        d_sc[7] = own_weight * scaling
        d_sc[8] = own_weight * stat_ref[2] * scaling

        nothing = jnp.zeros((head_dim, tile_rows), jnp.bfloat16)
        for source in range(1, devices):
            odd = lax.rem(jnp.maximum(codes[source], 0), 2) == 1
            first = w_sc[0, source : source + 1, :]
            second = w_sc[1, source : source + 1, :]
            turned = qgt_in_ref[source - 1].astype(jnp.float32)
            g_first = (turned[head_dim:] * first).astype(jnp.bfloat16)
            q_first = (turned[:head_dim] * w_sc[2, source : source + 1, :]).astype(jnp.bfloat16)
            q_second = (turned[:head_dim] * second).astype(jnp.bfloat16)
            xin_ref[source, :head_dim, :tile_rows] = jnp.where(odd, q_second, g_first)
            xin_ref[source, :head_dim, tile_rows:] = jnp.where(odd, q_first, nothing)
            xin_ref[source, head_dim:, :tile_rows] = jnp.where(odd, g_first, q_second)
            xin_ref[source, head_dim:, tile_rows:] = jnp.where(odd, nothing, q_first)
        for source in range(1, devices):
            head = lax.rem(jnp.maximum(codes[source], 0), groups)
            grad_ref[head] += dot_t(pd_in_ref[source - 1], xin_ref[source])

        for load in loads:
            load.wait()
        for head in range(groups):
            for tile in range(tiles_dev):
                code = tile * groups + head
                first = d_sc[3, code : code + 1, :]
                second = d_sc[6, code : code + 1, :]
                mix = mix_ref[head, tile].astype(jnp.float32)
                acc_ref[0, code] = mix[:head_dim] * first
                acc_ref[1, code] = mix[2 * head_dim :] * d_sc[7, code : code + 1, :] + mix[head_dim : 2 * head_dim] * second

        for peer in range(devices):
            code = given[peer]

            @pl.when(code >= 0)
            def _(peer=peer, code=code):
                at = pl.ds(code, 1)
                part_w = jnp.exp2(lse_sc[peer, pl.ds(own, 1), :] - d_sc[0, at, :]) * d_sc[1, at, :]
                scaled_w = part_w * scaling
                shift = -scaled_w * d_sc[2, at, :]
                mix = back_ref[peer, : 3 * head_dim, :].astype(jnp.float32)
                acc_ref[0, code] += mix[:head_dim] * part_w
                acc_ref[1, code] += mix[2 * head_dim :] * scaled_w + mix[head_dim : 2 * head_dim] * shift

        sub = lax.broadcasted_iota(jnp.int32, (tile_rows, tile_rows), 0)
        lane = lax.broadcasted_iota(jnp.int32, (tile_rows, tile_rows), 1)
        unit = jnp.where(sub == lane, 1.0, 0.0).astype(jnp.bfloat16)
        for tile in range(tiles_dev):
            rows = slice(tile * tile_rows, (tile + 1) * tile_rows)
            for head in range(0, groups, 2):
                cols = slice(head * head_dim, (head + 2) * head_dim)
                code = tile * groups + head
                both = jnp.concatenate([acc_ref[0, code], acc_ref[0, code + 1]], axis=0).astype(jnp.bfloat16)
                out_ref[rows, cols] = dot_t(unit, both).astype(jnp.bfloat16)
                both = jnp.concatenate([acc_ref[1, code], acc_ref[1, code + 1]], axis=0).astype(jnp.bfloat16)
                dq_ref[rows, cols] = dot_t(unit, both).astype(jnp.bfloat16)
        stores = [
            pltpu.make_async_copy(src, dst, out_sem.at[index])
            for index, (src, dst) in enumerate(((out_ref, out_hbm), (dq_ref, dq_hbm), (dk_ref, dk_hbm), (dv_ref, dv_hbm)))
        ]
        stores[0].start()
        stores[1].start()

        for code in range(tasks):

            @pl.when(named[code])
            def _(code=code):
                tile, head = code // groups, code % groups
                rows = slice(0, (tile + 1) * tile_rows)
                cols = slice(tile * pair, (tile + 1) * pair)
                fill_factor(
                    x_ref, qgt_ref, head, tile, *(d_sc[i, code : code + 1, :] for i in (4, 5, 8)), tile_rows, head_dim
                )
                own_pairs(code).wait()
                base_ref[head, rows, :] += dot_t(pd_ref[head, rows, cols], x_ref[head, :, cols])

        lane = lax.broadcasted_iota(jnp.int32, (tile_rows, 2 * head_dim), 1)
        for head in range(0, groups, 2):
            cols = slice(head * head_dim, (head + 2) * head_dim)
            for first in range(tiles_dev):
                rows = slice(first * tile_rows, (first + 1) * tile_rows)
                even, odd = (base_ref[h, rows, :] + grad_ref[h, rows, :] for h in (head, head + 1))
                dv_ref[rows, cols] = jnp.where(lane < head_dim, even, odd).astype(jnp.bfloat16)
                swapped = jnp.where(lane < head_dim, odd, even)
                dk_ref[rows, cols] = pltpu.roll(swapped, head_dim, 1).astype(jnp.bfloat16)
        stores[2].start()
        stores[3].start()
        for store in stores:
            store.wait()

    return body


def fast_local(query, key, value, grad_out, picks):
    row_count, columns = query.shape
    tiles_dev, groups, picked = picks.shape
    head_dim = columns // groups
    tile_rows = row_count // tiles_dev
    devices = lax.axis_size("ctx")
    tasks = tiles_dev * groups
    smem = pl.BlockSpec(memory_space=pltpu.SMEM)
    vmem = pl.BlockSpec(memory_space=pltpu.VMEM)
    far = pl.BlockSpec(memory_space=pltpu.HBM)
    low = jnp.bfloat16
    wide = jnp.float32
    width = 2 * head_dim
    shape = jax.ShapeDtypeStruct
    dma = pltpu.SemaphoreType.DMA
    small = pltpu.CompilerParams(vmem_limit_bytes=vmem_grant)
    near = pltpu.VMEM

    def away(*arrays):
        return tuple(pltpu.with_memory_space_constraint(x, pltpu.HBM) for x in arrays)

    def keep(*arrays):
        return tuple(pltpu.with_memory_space_constraint(x, pltpu.VMEM) for x in arrays)


    send_q, task_of = pl.pallas_call(
        pack_kernel(tiles_dev, groups, picked, tile_rows, head_dim, devices),
        out_shape=(shape((devices, tile_rows + 8, width), low), shape((devices,), jnp.int32)),
        in_specs=[smem, vmem, vmem],
        out_specs=(vmem, smem),
        name="pack",
    )(picks, query, grad_out)
    recv_q = lax.all_to_all(send_q, "ctx", split_axis=0, concat_axis=0, tiled=True)

    kv, vkt, stats, table, info = pl.pallas_call(
        own_kernel(tiles_dev, groups, tile_rows, head_dim, devices),
        out_shape=(
            near((groups, row_count, width), low),
            near((groups, width, row_count), low),
            near((4, tasks, tile_rows), wide),
            near((devices, 8, tile_rows), wide),
            near((2 * devices, tile_rows), wide),
        ),
        in_specs=[smem, smem] + [far] * 4,
        out_specs=tuple([vmem] * 5),
        scratch_shapes=[pltpu.VMEM((row_count, columns), low)] * 4
        + [pltpu.VMEM((tasks, 8, tile_rows), wide), dma((4,))],
        compiler_params=small,
        name="own",
    )(*away(picks, task_of, query, key, value, grad_out))

    slot = 3 * head_dim + 3 * devices
    in_shape = (devices - 1, row_count, 2 * tile_rows)
    send_b, inverse_in = pl.pallas_call(
        serve_kernel(groups, tile_rows, head_dim, devices),
        out_shape=(pltpu.HBM((devices, slot, tile_rows), low), near((2, devices, tile_rows), wide)),
        in_specs=[vmem] * 5,
        out_specs=(far, vmem),
        scratch_shapes=[
            pltpu.VMEM((devices, slot, tile_rows), low),
            pltpu.VMEM((3 * devices, tile_rows), wide),
            dma(()),
        ],
        compiler_params=pltpu.CompilerParams(
            vmem_limit_bytes=vmem_grant
        ),
        name="serve",
    )(*keep(info, recv_q, kv, vkt, table))
    recv_b = lax.all_to_all(send_b, "ctx", split_axis=0, concat_axis=0, tiled=True)

    pairs_in, qgt_in, lists_in = pl.pallas_call(
        again_kernel(groups, tile_rows, head_dim, devices),
        out_shape=(near(in_shape, low), near((devices - 1, width, tile_rows), low), near((devices, 8, width), wide)),
        in_specs=[smem, vmem, vmem, vmem],
        out_specs=(vmem, vmem, vmem),
        compiler_params=small,
        name="again",
    )(*away(picks), *keep(recv_q, kv, inverse_in))

    mix_shape = (groups, tiles_dev, 3 * head_dim, tile_rows)
    pair_shape = (groups, row_count, 2 * row_count)
    turned_shape = (groups, width, row_count)
    base_shape = (groups, row_count, width)
    factor_shape = (groups, width, 2 * row_count)
    qgt, mix, pairs, base = pl.pallas_call(
        rest_kernel(tiles_dev, groups, tile_rows, head_dim, devices),
        out_shape=(
            pltpu.HBM(turned_shape, low),
            pltpu.HBM(mix_shape, low),
            pltpu.HBM(pair_shape, low),
            pltpu.HBM(base_shape, wide),
        ),
        in_specs=[far] * 2 + [vmem] * 4,
        out_specs=tuple([far] * 4),
        scratch_shapes=[pltpu.VMEM((row_count, columns), low)] * 2
        + [
            pltpu.VMEM(turned_shape, low),
            pltpu.VMEM(mix_shape, low),
            pltpu.VMEM(pair_shape, low),
            pltpu.VMEM(base_shape, wide),
            pltpu.VMEM(factor_shape, low),
            pltpu.VMEM((3, tasks, tile_rows), wide),
            dma((2,)),
            dma((tiles_dev + 3,)),
        ],
        compiler_params=small,
        name="rest",
    )(*away(query, grad_out), *keep(kv, vkt, stats, info))

    return pl.pallas_call(
        final_kernel(tiles_dev, groups, picked, tile_rows, head_dim, devices),
        out_shape=tuple([shape((row_count, columns), low)] * 4),
        in_specs=[vmem] * 7 + [far] * 4,
        out_specs=tuple([far] * 4),
        scratch_shapes=[
            pltpu.VMEM((groups, width, row_count), low),
            pltpu.VMEM(mix_shape, low),
            pltpu.VMEM(pair_shape, low),
        ]
        + [pltpu.VMEM((row_count, columns), low)] * 4
        + [
            pltpu.VMEM((2, tasks, head_dim, tile_rows), wide),
            pltpu.VMEM((groups, row_count, width), wide),
            pltpu.VMEM((groups, row_count, width), wide),
            pltpu.VMEM((devices, devices, tile_rows), wide),
            pltpu.VMEM((devices, devices, tile_rows), wide),
            pltpu.VMEM((3, devices, tile_rows), wide),
            pltpu.VMEM((9, tasks, tile_rows), wide),
            pltpu.VMEM((groups, width, 2 * row_count), low),
            pltpu.VMEM((devices, width, 2 * tile_rows), low),
            dma((3 + tasks,)),
            dma((4,)),
        ],
        compiler_params=small,
        name="final",
    )(*keep(info, lists_in, recv_b, qgt_in, stats, inverse_in, pairs_in), *away(qgt, mix, pairs, base))


def choose(query, key, value, grad_out, picks):
    pair_bytes = lax.axis_size("ctx") * query.shape[0] * (query.shape[0] // picks.shape[0]) * 4
    plan = fast_local if pair_bytes <= pair_budget else local
    return plan(query, key, value, grad_out, picks)


def solution(mesh):
    placed = (
        P("ctx", "head"),
        P("ctx", "head"),
        P("ctx", "head"),
        P("ctx", "head"),
        P("ctx", "head", None),
    )
    return jax.shard_map(
        choose,
        mesh=mesh,
        in_specs=placed,
        out_specs=(P("ctx", "head"), P("ctx", "head"), P("ctx", "head"), P("ctx", "head")),
        check_vma=False,
    )
```

```python
import math

import jax
import jax.numpy as jnp
from jax import lax
from jax.experimental import pallas as pl
from jax.experimental.pallas import tpu as pltpu
from jax.sharding import PartitionSpec as P

masked_value = -1e30
highest = lax.Precision.HIGHEST
LOG2E = math.log2(math.e)
pair_budget = 8 << 20
vmem_grant = 32 << 20


def attend_slots(q_slots, head_ids, k_heads, v_heads, scaling):
    key_rows = jnp.take(k_heads, head_ids, axis=0)
    value_rows = jnp.take(v_heads, head_ids, axis=0)
    scores = (
        jnp.einsum("ndq,nkd->nqk", q_slots, key_rows, preferred_element_type=jnp.float32) * scaling
    )
    peak_score = jnp.max(scores, axis=-1, keepdims=True)
    log_total = peak_score + jnp.log(jnp.sum(jnp.exp(scores - peak_score), axis=-1, keepdims=True))
    attend_low = jnp.exp(scores - log_total).astype(jnp.bfloat16)
    outputs = jnp.einsum("nqk,nkd->ndq", attend_low, value_rows, preferred_element_type=jnp.float32)
    return (outputs, log_total[..., 0])


def slot_grads(q_slots, g_slots, c_slots, lse_slots, head_ids, k_heads, v_heads, scaling):
    key_rows = jnp.take(k_heads, head_ids, axis=0)
    value_rows = jnp.take(v_heads, head_ids, axis=0)
    scores = (
        jnp.einsum("ndq,nkd->nqk", q_slots, key_rows, preferred_element_type=jnp.float32) * scaling
    )
    attend = jnp.exp(scores - lse_slots[..., None])
    attend_low = attend.astype(jnp.bfloat16)
    grad_v = jnp.einsum("nqk,ndq->nkd", attend_low, g_slots, preferred_element_type=jnp.float32)
    grad_prob = jnp.einsum("ndq,nkd->nqk", g_slots, value_rows, preferred_element_type=jnp.float32)
    dscore = (attend * (grad_prob - c_slots[..., None])).astype(jnp.bfloat16)
    grad_k = (
        jnp.einsum("nqk,ndq->nkd", dscore, q_slots, preferred_element_type=jnp.float32) * scaling
    )
    grad_q = (
        jnp.einsum("nqk,nkd->ndq", dscore, key_rows, preferred_element_type=jnp.float32) * scaling
    )
    return (grad_k, grad_v, grad_q)


def local(query, key, value, grad_out, picks):
    row_count, columns = query.shape
    tiles_dev, groups, picked = picks.shape
    head_dim = columns // groups
    tile_rows = row_count // tiles_dev
    others = picked - 1
    scaling = 1.0 / math.sqrt(head_dim)
    devices = lax.axis_size("ctx")
    own_block = lax.axis_index("ctx")
    per_group = min(8, devices)
    all_picks = lax.all_gather(picks, "ctx", axis=0, tiled=True)
    q_heads = query.reshape(row_count, groups, head_dim).transpose(1, 0, 2)
    k_heads = key.reshape(row_count, groups, head_dim).transpose(1, 0, 2)
    v_heads = value.reshape(row_count, groups, head_dim).transpose(1, 0, 2)
    q_tiles = query.reshape(tiles_dev, tile_rows, groups, head_dim)
    do_tiles = grad_out.reshape(tiles_dev, tile_rows, groups, head_dim)
    do_major = do_tiles.transpose(0, 2, 1, 3)
    positions = jnp.arange(row_count, dtype=jnp.int32)
    tile_masks = []
    for tile_step in range(tiles_dev):
        span = (tile_step + 1) * tile_rows
        query_pos = positions[tile_step * tile_rows : span]
        tile_masks.append(positions[None, :span] <= query_pos[:, None])
    targets = picks[:, :, 1:]
    active = targets != own_block
    lookup = jnp.where(active, targets, own_block).reshape(-1)
    peer_ids = jnp.arange(devices, dtype=jnp.int32)
    routing = ((targets[None] == peer_ids[:, None, None, None]) & active[None]).astype(jnp.float32)
    routing_low = routing.astype(jnp.bfloat16)
    send_q = jnp.einsum(
        "jtgi,tqgd->jdq", routing_low, q_tiles, preferred_element_type=jnp.float32
    ).astype(jnp.bfloat16)
    recv_q = lax.all_to_all(send_q, "ctx", split_axis=0, concat_axis=0, tiled=True)

    def own_forward(inputs):
        q_head, k_head, v_head = inputs
        out_list = []
        lse_list = []
        for tile_step in range(tiles_dev):
            span = (tile_step + 1) * tile_rows
            q_part = q_head[tile_step * tile_rows : span]
            scores = (
                jnp.einsum("qd,kd->qk", q_part, k_head[:span], preferred_element_type=jnp.float32)
                * scaling
            )
            scores = jnp.where(tile_masks[tile_step], scores, masked_value)
            peak_score = jnp.max(scores, axis=-1, keepdims=True)
            log_total = peak_score + jnp.log(
                jnp.sum(jnp.exp(scores - peak_score), axis=-1, keepdims=True)
            )
            attend_low = jnp.exp(scores - log_total).astype(jnp.bfloat16)
            out_list.append(jnp.dot(attend_low, v_head[:span], preferred_element_type=jnp.float32))
            lse_list.append(log_total[:, 0])
        return (jnp.concatenate(out_list, axis=0), jnp.concatenate(lse_list, axis=0))

    own_out, own_lse = lax.map(own_forward, (q_heads, k_heads, v_heads))
    sources = all_picks.reshape(devices, tiles_dev, groups, picked)[..., 1:]
    incoming = (sources == own_block) & (peer_ids[:, None, None, None] != own_block)
    live_in = jnp.any(incoming, axis=(1, 2, 3))
    group_ids = jnp.arange(groups, dtype=jnp.int32)
    head_of = jnp.sum(jnp.where(incoming, group_ids[None, None, :, None], 0), axis=(1, 2, 3))
    ranking = jnp.argsort(jnp.where(live_in, 0, 1) * devices + peer_ids)
    inverse = jnp.argsort(ranking)
    rounds = (jnp.sum(live_in.astype(jnp.int32)) + per_group - 1) // per_group
    heads_sorted = jnp.take(head_of, ranking, axis=0)
    q_sorted = jnp.take(recv_q, ranking, axis=0)

    def forward_turn(turn, totals):
        served_out, served_lse = totals
        offset = turn * per_group
        query_part = lax.dynamic_slice_in_dim(q_sorted, offset, per_group, 0)
        head_part = lax.dynamic_slice_in_dim(heads_sorted, offset, per_group, 0)
        out_part, lse_part = attend_slots(query_part, head_part, k_heads, v_heads, scaling)
        served_out = lax.dynamic_update_slice_in_dim(served_out, out_part, offset, 0)
        served_lse = lax.dynamic_update_slice_in_dim(served_lse, lse_part, offset, 0)
        return (served_out, served_lse)

    start_fwd = (
        jnp.zeros((devices, head_dim, tile_rows), jnp.float32),
        jnp.zeros((devices, tile_rows), jnp.float32),
    )
    served_out, served_lse = lax.fori_loop(0, rounds, forward_turn, start_fwd)
    back_out, back_lse = (
        lax.all_to_all(
            jnp.take(served_out, inverse, axis=0), "ctx", split_axis=0, concat_axis=0, tiled=True
        ),
        lax.all_to_all(
            jnp.take(served_lse, inverse, axis=0), "ctx", split_axis=0, concat_axis=0, tiled=True
        ),
    )
    task_out = jnp.take(back_out, lookup, axis=0).reshape(
        tiles_dev, groups, others, head_dim, tile_rows
    )
    task_lse = jnp.take(back_lse, lookup, axis=0).reshape(tiles_dev, groups, others, tile_rows)
    own_out_t = own_out.reshape(groups, tiles_dev, tile_rows, head_dim).transpose(1, 0, 2, 3)
    own_lse_t = own_lse.reshape(groups, tiles_dev, tile_rows).transpose(1, 0, 2)
    active_rows = active[..., None]
    rem_lse = jnp.where(active_rows, task_lse, masked_value)
    ceiling = jnp.maximum(own_lse_t, jnp.max(rem_lse, axis=2))
    log_total = ceiling + jnp.log(
        jnp.exp(own_lse_t - ceiling) + jnp.sum(jnp.exp(rem_lse - ceiling[:, :, None]), axis=2)
    )
    own_weight = jnp.exp(own_lse_t - log_total)
    rem_weight = jnp.where(active_rows, jnp.exp(rem_lse - log_total[:, :, None]), 0.0)
    mixed = own_weight[..., None] * own_out_t + jnp.einsum(
        "tgiq,tgidq->tgqd", rem_weight, task_out, precision=highest
    )
    out_low = mixed.astype(jnp.bfloat16)
    attn_out = out_low.transpose(0, 2, 1, 3).reshape(row_count, columns)
    row_delta = jnp.sum(do_major.astype(jnp.float32) * out_low.astype(jnp.float32), axis=-1)
    own_scaled = (own_weight[..., None] * do_major.astype(jnp.float32)).astype(jnp.bfloat16)
    own_shift = own_weight * row_delta
    g_heads = own_scaled.transpose(1, 0, 2, 3).reshape(groups, row_count, head_dim)
    c_heads = own_shift.transpose(1, 0, 2).reshape(groups, row_count)

    def own_backward(inputs):
        q_head, k_head, v_head, g_head, c_head, lse_head = inputs
        grad_k = jnp.zeros((row_count, head_dim), jnp.float32)
        grad_v = jnp.zeros((row_count, head_dim), jnp.float32)
        dq_list = []
        for tile_step in range(tiles_dev):
            first = tile_step * tile_rows
            span = (tile_step + 1) * tile_rows
            q_part = q_head[first:span]
            g_part = g_head[first:span]
            k_part = k_head[:span]
            scores = (
                jnp.einsum("qd,kd->qk", q_part, k_part, preferred_element_type=jnp.float32)
                * scaling
            )
            scores = jnp.where(tile_masks[tile_step], scores, masked_value)
            attend = jnp.exp(scores - lse_head[first:span, None])
            attend_low = attend.astype(jnp.bfloat16)
            part_dv = jnp.einsum(
                "qk,qd->kd", attend_low, g_part, preferred_element_type=jnp.float32
            )
            grad_prob = jnp.einsum(
                "qd,kd->qk", g_part, v_head[:span], preferred_element_type=jnp.float32
            )
            dscore = (attend * (grad_prob - c_head[first:span, None])).astype(jnp.bfloat16)
            part_dk = (
                jnp.einsum("qk,qd->kd", dscore, q_part, preferred_element_type=jnp.float32)
                * scaling
            )
            dq_list.append(jnp.dot(dscore, k_part, preferred_element_type=jnp.float32) * scaling)
            padding = ((0, row_count - span), (0, 0))
            grad_k = grad_k + jnp.pad(part_dk, padding)
            grad_v = grad_v + jnp.pad(part_dv, padding)
        return (grad_k, grad_v, jnp.concatenate(dq_list, axis=0))

    own_dk, own_dv, own_dq = lax.map(
        own_backward, (q_heads, k_heads, v_heads, g_heads, c_heads, own_lse)
    )
    rem_shift = rem_weight * row_delta[:, :, None]
    rem_scaled = (rem_weight[..., None] * do_major[:, :, None].astype(jnp.float32)).astype(
        jnp.bfloat16
    )
    send_g = jnp.einsum(
        "jtgi,tgiqd->jdq", routing_low, rem_scaled, preferred_element_type=jnp.float32
    )
    send_c = jnp.einsum("jtgi,tgiq->jq", routing, rem_shift, precision=highest)
    recv_g, recv_c = (
        lax.all_to_all(send_g, "ctx", split_axis=0, concat_axis=0, tiled=True),
        lax.all_to_all(send_c, "ctx", split_axis=0, concat_axis=0, tiled=True),
    )
    g_sorted = jnp.take(recv_g, ranking, axis=0).astype(jnp.bfloat16)
    c_sorted = jnp.take(recv_c, ranking, axis=0)

    def backward_turn(turn, totals):
        grad_k, grad_v, served_dq = totals
        offset = turn * per_group
        query_part = lax.dynamic_slice_in_dim(q_sorted, offset, per_group, 0)
        cot_part = lax.dynamic_slice_in_dim(g_sorted, offset, per_group, 0)
        shift_part = lax.dynamic_slice_in_dim(c_sorted, offset, per_group, 0)
        lse_part = lax.dynamic_slice_in_dim(served_lse, offset, per_group, 0)
        head_part = lax.dynamic_slice_in_dim(heads_sorted, offset, per_group, 0)
        part_dk, part_dv, part_dq = slot_grads(
            query_part, cot_part, shift_part, lse_part, head_part, k_heads, v_heads, scaling
        )
        head_onehot = (head_part[:, None] == group_ids[None, :]).astype(jnp.float32)
        grad_k = grad_k + jnp.einsum("ng,nkd->gkd", head_onehot, part_dk, precision=highest)
        grad_v = grad_v + jnp.einsum("ng,nkd->gkd", head_onehot, part_dv, precision=highest)
        served_dq = lax.dynamic_update_slice_in_dim(served_dq, part_dq, offset, 0)
        return (grad_k, grad_v, served_dq)

    zeros_heads = jnp.zeros((groups, row_count, head_dim), jnp.float32)
    start_bwd = (zeros_heads, zeros_heads, jnp.zeros((devices, head_dim, tile_rows), jnp.float32))
    rem_dk, rem_dv, served_dq = lax.fori_loop(0, rounds, backward_turn, start_bwd)
    back_dq = lax.all_to_all(
        jnp.take(served_dq, inverse, axis=0).astype(jnp.bfloat16),
        "ctx",
        split_axis=0,
        concat_axis=0,
        tiled=True,
    ).astype(jnp.float32)
    task_dq = jnp.take(back_dq, lookup, axis=0).reshape(
        tiles_dev, groups, others, head_dim, tile_rows
    )
    rem_dq = jnp.sum(jnp.where(active[..., None, None], task_dq, 0.0), axis=2)
    own_dq_t = own_dq.reshape(groups, tiles_dev, tile_rows, head_dim).transpose(1, 0, 2, 3)
    total_dq = own_dq_t + rem_dq.transpose(0, 1, 3, 2)
    grad_query = total_dq.transpose(0, 2, 1, 3).reshape(row_count, columns).astype(jnp.bfloat16)
    grad_key = (own_dk + rem_dk).transpose(1, 0, 2).reshape(row_count, columns).astype(jnp.bfloat16)
    grad_value = (
        (own_dv + rem_dv).transpose(1, 0, 2).reshape(row_count, columns).astype(jnp.bfloat16)
    )
    return (attn_out, grad_query, grad_key, grad_value)


def fill_factor(x_ref, qgt_ref, head, tile, first, second, third, tile_rows, head_dim):
    v_rows = slice(0, head_dim) if head % 2 == 0 else slice(head_dim, 2 * head_dim)
    k_rows = slice(head_dim, 2 * head_dim) if head % 2 == 0 else slice(0, head_dim)
    turned = qgt_ref[head, :, tile * tile_rows : (tile + 1) * tile_rows].astype(jnp.float32)
    early = slice(tile * 2 * tile_rows, tile * 2 * tile_rows + tile_rows)
    late = slice(tile * 2 * tile_rows + tile_rows, (tile + 1) * 2 * tile_rows)
    x_ref[head, v_rows, early] = (turned[head_dim:] * first).astype(jnp.bfloat16)
    x_ref[head, v_rows, late] = jnp.zeros((head_dim, tile_rows), jnp.bfloat16)
    x_ref[head, k_rows, early] = (turned[:head_dim] * second).astype(jnp.bfloat16)
    x_ref[head, k_rows, late] = (turned[:head_dim] * third).astype(jnp.bfloat16)


def pair_parts(near, far, tiles_dev, tile_rows):
    for part in range(tiles_dev):
        rows = slice(part * tile_rows, (part + 1) * tile_rows)
        cols = slice(part * 2 * tile_rows, tiles_dev * 2 * tile_rows)
        yield near.at[:, rows, cols], far.at[:, rows, cols]


def dot_t(a, b):
    return lax.dot_general(a, b, (((1,), (1,)), ((), ())), preferred_element_type=jnp.float32)


def split_low(x):
    high = x.astype(jnp.bfloat16).astype(jnp.float32)
    return high, x - high


def halves(block, head_dim):
    lane = lax.broadcasted_iota(jnp.int32, block.shape, 1)
    zero = jnp.zeros_like(block)
    return jnp.where(lane < head_dim, block, zero), jnp.where(lane < head_dim, zero, block)


def pack_kernel(tiles_dev, groups, picked, tile_rows, head_dim, devices):
    def body(picks_ref, q_ref, g_ref, send_ref, task_ref):
        own = picks_ref[0, 0, 0]
        meta_rows = send_ref.shape[1] - tile_rows
        lanes = send_ref.shape[2]
        row = lax.broadcasted_iota(jnp.int32, (meta_rows, lanes), 0)
        blank = jnp.zeros((meta_rows, lanes), jnp.bfloat16)
        for peer in range(devices):
            send_ref[peer, tile_rows:, :] = blank
            task_ref[peer] = -1
        for tile in range(tiles_dev):
            rows = slice(tile * tile_rows, (tile + 1) * tile_rows)
            for head in range(groups):
                cols = slice(head * head_dim, (head + 1) * head_dim)
                block = jnp.concatenate([q_ref[rows, cols], g_ref[rows, cols]], axis=1)
                code = tile * groups + head
                meta = jnp.where(row == 0, code + 1, 0)
                for entry in range(1, picked):
                    meta = jnp.where(row == entry, picks_ref[tile, head, entry], meta)
                meta = meta.astype(jnp.float32).astype(jnp.bfloat16)
                for entry in range(1, picked):
                    target = picks_ref[tile, head, entry]
                    send_ref[target, :tile_rows, :] = block
                    send_ref[target, tile_rows:, :] = meta
                    task_ref[target] = code
        task_ref[own] = -1

    return body


def own_kernel(tiles_dev, groups, tile_rows, head_dim, devices):
    scale = LOG2E / math.sqrt(head_dim)

    def body(picks_ref, task_ref, q_hbm, k_hbm, v_hbm, g_hbm, kv_ref, vkt_ref, stat_ref, table_ref, info_ref,
             q_ref, k_ref, v_ref, g_ref, rows_ref, in_sem):
        loads = [
            pltpu.make_async_copy(src, dst, in_sem.at[index])
            for index, (src, dst) in enumerate(((k_hbm, k_ref), (v_hbm, v_ref), (q_hbm, q_ref), (g_hbm, g_ref)))
        ]
        for load in loads:
            load.start()
        for load in loads:
            load.wait()
        sub = lax.broadcasted_iota(jnp.int32, (tile_rows, tile_rows), 0)
        lane = lax.broadcasted_iota(jnp.int32, (tile_rows, tile_rows), 1)
        causal = sub <= lane
        for head in range(groups):
            cols = slice(head * head_dim, (head + 1) * head_dim)
            kv_ref[head] = jnp.concatenate([k_ref[:, cols], v_ref[:, cols]], axis=1)

        def product(code):
            tile, head = code // groups, code % groups
            cols = slice(head * head_dim, (head + 1) * head_dim)
            rows = slice(tile * tile_rows, (tile + 1) * tile_rows)
            block = jnp.concatenate([q_ref[rows, cols], g_ref[rows, cols]], axis=1)
            return dot_t(kv_ref[head, : rows.stop, :], jnp.concatenate(halves(block, head_dim), axis=0))

        ahead = product(0)
        for code in range(tiles_dev * groups):
            both = ahead
            if code + 1 < tiles_dev * groups:
                ahead = product(code + 1)
            tile = code // groups
            split = tile * tile_rows
            last = jnp.where(causal, both[split:, :tile_rows], masked_value)
            peak = jnp.max(last, axis=0, keepdims=True)
            if tile:
                peak = jnp.maximum(peak, jnp.max(both[:split, :tile_rows], axis=0, keepdims=True))
            peak = peak * scale
            powers = jnp.exp2(last * scale - peak)
            total = jnp.sum(powers, axis=0, keepdims=True)
            mean_grad = jnp.sum(powers * both[split:, tile_rows:], axis=0, keepdims=True)
            if tile:
                powers = jnp.exp2(both[:split, :tile_rows] * scale - peak)
                total = total + jnp.sum(powers, axis=0, keepdims=True)
                mean_grad = mean_grad + jnp.sum(powers * both[:split, tile_rows:], axis=0, keepdims=True)
            inverse = 1.0 / total
            mean_grad = mean_grad * inverse
            lse = peak + jnp.log2(total)
            center = mean_grad.astype(jnp.bfloat16).astype(jnp.float32)
            for index, value in enumerate((lse, center, inverse, peak, mean_grad)):
                stat_ref[index, code : code + 1, :] = value
            for index, value in enumerate(split_low(lse) + (center,)):
                rows_ref[code, index : index + 1, :] = value
        for head in range(groups):
            cols = slice(head * head_dim, (head + 1) * head_dim)
            vkt_ref[head] = jnp.concatenate([v_ref[:, cols], k_ref[:, cols]], axis=1).T
        sub = lax.broadcasted_iota(jnp.int32, (devices, tile_rows), 0)
        codes = jnp.full((devices, tile_rows), -1, jnp.int32)
        for peer in range(devices):
            codes = jnp.where(sub == peer, task_ref[peer], codes)
            table_ref[peer] = rows_ref[jnp.maximum(task_ref[peer], 0)]
        info_ref[:devices, :] = codes.astype(jnp.float32)
        info_ref[devices:, :] = jnp.full((devices, tile_rows), picks_ref[0, 0, 0], jnp.int32).astype(jnp.float32)

    return body


def rest_kernel(tiles_dev, groups, tile_rows, head_dim, devices):
    scale = LOG2E / math.sqrt(head_dim)

    def body(q_hbm, g_hbm, kv_ref, vkt_ref, stat_ref, info_ref, qgt_hbm, mix_hbm, pd_hbm, base_hbm,
             q_ref, g_ref, qgt_ref, mix_ref, pd_ref, base_ref, x_ref, d_ref, in_sem, out_sem):
        loads = [
            pltpu.make_async_copy(src, dst, in_sem.at[index])
            for index, (src, dst) in enumerate(((q_hbm, q_ref), (g_hbm, g_ref)))
        ]
        for load in loads:
            load.start()
        for load in loads:
            load.wait()
        sub = lax.broadcasted_iota(jnp.int32, (tile_rows, tile_rows), 0)
        lane = lax.broadcasted_iota(jnp.int32, (tile_rows, tile_rows), 1)
        causal = sub <= lane

        def product(code):
            tile, head = code // groups, code % groups
            cols = slice(head * head_dim, (head + 1) * head_dim)
            rows = slice(tile * tile_rows, (tile + 1) * tile_rows)
            block = jnp.concatenate([q_ref[rows, cols], g_ref[rows, cols]], axis=1)
            qgt_ref[head, :, rows] = block.T
            return dot_t(kv_ref[head, : rows.stop, :], jnp.concatenate(halves(block, head_dim), axis=0))

        ahead = product(0)
        for code in range(tiles_dev * groups):
            both = ahead
            if code + 1 < tiles_dev * groups:
                ahead = product(code + 1)
            tile, head = code // groups, code % groups
            span = (tile + 1) * tile_rows
            at = tile * 2 * tile_rows
            peak = stat_ref[3, code : code + 1, :]
            inverse = stat_ref[2, code : code + 1, :]
            for part in range(tile + 1):
                chunk = slice(part * tile_rows, (part + 1) * tile_rows)
                scores = both[chunk, :tile_rows]
                if part == tile:
                    scores = jnp.where(causal, scores, masked_value)
                powers = jnp.exp2(scores * scale - peak)
                spread = powers * (both[chunk, tile_rows:] - stat_ref[1, code : code + 1, :])
                pd_ref[head, chunk, at : at + tile_rows] = powers.astype(jnp.bfloat16)
                pd_ref[head, chunk, at + tile_rows : at + 2 * tile_rows] = spread.astype(jnp.bfloat16)
            result = jnp.dot(vkt_ref[head, :, :span], pd_ref[head, :span, at : at + 2 * tile_rows],
                             preferred_element_type=jnp.float32)
            mix_ref[head, tile, : 2 * head_dim, :] = (result[:, :tile_rows] * inverse).astype(jnp.bfloat16)
            mix_ref[head, tile, 2 * head_dim :, :] = (result[head_dim:, tile_rows:] * inverse).astype(jnp.bfloat16)
        ids = lax.broadcasted_iota(jnp.int32, (tiles_dev * groups, tile_rows), 0).astype(jnp.float32)
        named = ids < 0
        for peer in range(devices):
            named = named | (ids == info_ref[peer : peer + 1, :])
        alone = jnp.where(named, 0.0, stat_ref[2])
        d_ref[0] = alone
        d_ref[1] = alone * (stat_ref[1] - stat_ref[4]) * (1.0 / math.sqrt(head_dim))
        d_ref[2] = alone * (1.0 / math.sqrt(head_dim))
        for head in range(groups):
            for tile in range(tiles_dev):
                code = tile * groups + head
                fill_factor(x_ref, qgt_ref, head, tile, *(d_ref[i, code : code + 1, :] for i in range(3)), tile_rows, head_dim)
            for part in range(tiles_dev):
                rows = slice(part * tile_rows, (part + 1) * tile_rows)
                cols = slice(part * 2 * tile_rows, tiles_dev * 2 * tile_rows)
                base_ref[head, rows, :] = dot_t(pd_ref[head, rows, cols], x_ref[head, :, cols])
        stores = [
            pltpu.make_async_copy(mix_ref, mix_hbm, out_sem.at[tiles_dev]),
            pltpu.make_async_copy(qgt_ref, qgt_hbm, out_sem.at[tiles_dev + 1]),
            pltpu.make_async_copy(base_ref, base_hbm, out_sem.at[tiles_dev + 2]),
        ] + [
            pltpu.make_async_copy(src, dst, out_sem.at[index])
            for index, (src, dst) in enumerate(pair_parts(pd_ref, pd_hbm, tiles_dev, tile_rows))
        ]
        for store in stores:
            store.start()
        for store in stores:
            store.wait()

    return body


def parts_of(block, kv_head, tile_rows, head_dim, scale):
    both = dot_t(kv_head, jnp.concatenate(halves(block, head_dim), axis=0))
    scores = both[:, :tile_rows]
    peak = jnp.max(scores, axis=0, keepdims=True) * scale
    powers = jnp.exp2(scores * scale - peak)
    return peak, powers, both[:, tile_rows:]


def serve_kernel(groups, tile_rows, head_dim, devices):
    scale = LOG2E / math.sqrt(head_dim)

    def body(info_ref, recv_ref, kv_ref, vkt_ref, table_ref, send_hbm, inv_ref,
             send_ref, st_ref, out_sem):
        own = jnp.max(info_ref[devices : devices + 1, :]).astype(jnp.int32)
        st_ref[...] = jnp.zeros_like(st_ref)
        inv_ref[...] = jnp.zeros_like(inv_ref)
        heads = [None]
        blocks = [None]
        for source in range(1, devices):
            code = jnp.max(recv_ref[source, tile_rows:, :].astype(jnp.float32)[0:1, :]).astype(jnp.int32) - 1
            block = recv_ref[source, :tile_rows, :]
            heads.append(lax.rem(jnp.maximum(code, 0), groups))
            blocks.append(jnp.where((code >= 0) & (own != source), block, jnp.zeros_like(block)))
        ahead = parts_of(blocks[1], kv_ref[heads[1]], tile_rows, head_dim, scale)
        for source in range(1, devices):
            peak, powers, grads = ahead
            if source + 1 < devices:
                ahead = parts_of(blocks[source + 1], kv_ref[heads[source + 1]], tile_rows, head_dim, scale)
            total = jnp.sum(powers, axis=0, keepdims=True)
            inverse = 1.0 / total
            mean_grad = jnp.sum(powers * grads, axis=0, keepdims=True) * inverse
            center = mean_grad.astype(jnp.bfloat16).astype(jnp.float32)
            spread = powers * (grads - center)
            both = jnp.concatenate([powers.astype(jnp.bfloat16), spread.astype(jnp.bfloat16)], axis=1)
            result = jnp.dot(vkt_ref[heads[source]], both, preferred_element_type=jnp.float32)
            send_ref[source, : 2 * head_dim, :] = (result[:, :tile_rows] * inverse).astype(jnp.bfloat16)
            send_ref[source, 2 * head_dim : 3 * head_dim, :] = (result[head_dim:, tile_rows:] * inverse).astype(jnp.bfloat16)
            parts = split_low(peak + jnp.log2(total)) + (center,)
            for index in range(3):
                st_ref[index * devices + source : index * devices + source + 1, :] = parts[index]
            inv_ref[0, source : source + 1, :] = inverse
            inv_ref[1, source : source + 1, :] = peak
            inv_ref[2, source : source + 1, :] = center
        table = st_ref[...]
        row = lax.broadcasted_iota(jnp.int32, table.shape, 0)
        mine = lax.rem(row, devices) == own
        for peer in range(devices):
            entry = table_ref[peer]
            wide = jnp.concatenate(
                [jnp.broadcast_to(entry[index : index + 1], (devices, tile_rows)) for index in range(3)], axis=0
            )
            send_ref[peer, 3 * head_dim :, :] = jnp.where(mine, wide, table).astype(jnp.bfloat16)
        store = pltpu.make_async_copy(send_ref, send_hbm, out_sem)
        store.start()
        store.wait()

    return body


def again_kernel(groups, tile_rows, head_dim, devices):
    scale = LOG2E / math.sqrt(head_dim)

    def body(picks_ref, recv_ref, kv_ref, inv_ref, pd_ref, qgt_ref, meta_ref):
        own = picks_ref[0, 0, 0]
        for source in range(devices):
            meta_ref[source] = recv_ref[source, tile_rows:, :].astype(jnp.float32)
        codes = [jnp.max(recv_ref[source, tile_rows:, :].astype(jnp.float32)[0:1, :]).astype(jnp.int32) - 1
                 for source in range(devices)]

        def product(source):
            block = recv_ref[source, :tile_rows, :]
            block = jnp.where((codes[source] >= 0) & (own != source), block, jnp.zeros_like(block))
            qgt_ref[source - 1] = block.T
            head = lax.rem(jnp.maximum(codes[source], 0), groups)
            return dot_t(kv_ref[head], jnp.concatenate(halves(block, head_dim), axis=0))

        ahead = product(1)
        for source in range(1, devices):
            both = ahead
            if source + 1 < devices:
                ahead = product(source + 1)
            powers = jnp.exp2(both[:, :tile_rows] * scale - inv_ref[1, source : source + 1, :])
            pd_ref[source - 1, :, :tile_rows] = powers.astype(jnp.bfloat16)
            pd_ref[source - 1, :, tile_rows:] = (
                powers * (both[:, tile_rows:] - inv_ref[2, source : source + 1, :])
            ).astype(jnp.bfloat16)

    return body


def final_kernel(tiles_dev, groups, picked, tile_rows, head_dim, devices):
    scaling = 1.0 / math.sqrt(head_dim)
    pair = 2 * tile_rows

    def body(info_ref, meta_ref, back_ref, qgt_in_ref, stat_ref, inv_ref,
             pd_in_ref, qgt_hbm, mix_hbm, pd_hbm, base_hbm, out_hbm, dq_hbm, dk_hbm, dv_hbm,
             qgt_ref, mix_ref, pd_ref, out_ref, dq_ref, dk_ref, dv_ref, acc_ref, base_ref, grad_ref,
             lse_sc, gd_sc, w_sc, d_sc, x_ref, xin_ref, in_sem, out_sem):
        own = jnp.max(info_ref[devices : devices + 1, :]).astype(jnp.int32)
        given = [jnp.max(info_ref[peer : peer + 1, :]).astype(jnp.int32) for peer in range(devices)]
        tasks = tiles_dev * groups
        base = 3 * head_dim
        named = []
        for code in range(tasks):
            hit = given[0] == code
            for peer in range(1, devices):
                hit = hit | (given[peer] == code)
            named.append(hit)
        loads = [
            pltpu.make_async_copy(src, dst, in_sem.at[index])
            for index, (src, dst) in enumerate(((mix_hbm, mix_ref), (qgt_hbm, qgt_ref), (base_hbm, base_ref)))
        ]
        for load in loads:
            load.start()

        def own_pairs(code):
            tile, head = code // groups, code % groups
            at = (head, slice(0, (tile + 1) * tile_rows), slice(tile * pair, (tile + 1) * pair))
            return pltpu.make_async_copy(pd_hbm.at[at], pd_ref.at[at], in_sem.at[3 + code])

        for code in range(tasks):

            @pl.when(named[code])
            def _(code=code):
                own_pairs(code).start()

        grad_ref[...] = jnp.zeros_like(grad_ref)

        lse_of = []
        gd_of = []
        for peer in range(devices):
            table = back_ref[peer, base:, :].astype(jnp.float32)
            lse_of.append(table[:devices] + table[devices : 2 * devices])
            gd_of.append(table[2 * devices :])
            lse_sc[peer] = lse_of[peer]
            gd_sc[peer] = gd_of[peer]

        ids = lax.broadcasted_iota(jnp.int32, (devices, tile_rows), 0)
        metas = [meta_ref[source] for source in range(devices)]
        rows_of = [
            jnp.concatenate([metas[source][entry : entry + 1] for source in range(devices)], axis=0).astype(jnp.int32)
            for entry in range(picked)
        ]
        codes = [None] + [jnp.max(metas[source][0:1, :]).astype(jnp.int32) - 1 for source in range(1, devices)]
        live = (rows_of[0] > 0) & (ids != own)
        chosen = []
        for peer in range(devices):
            active = ids == peer
            for entry in rows_of[1:]:
                active = active | (entry == peer)
            chosen.append(active)
        peak = jnp.full((devices, tile_rows), masked_value, jnp.float32)
        for peer in range(devices):
            peak = jnp.maximum(peak, jnp.where(chosen[peer], lse_of[peer], masked_value))
        total = jnp.zeros_like(peak)
        delta = jnp.zeros_like(peak)
        for peer in range(devices):
            power = jnp.where(chosen[peer], jnp.exp2(lse_of[peer] - peak), 0.0)
            total = total + power
            delta = delta + jnp.where(chosen[peer], power * gd_of[peer], 0.0)
        delta = delta / total
        weight = jnp.exp2(lse_sc[own] - peak) / total * inv_ref[0]
        weight = jnp.where(live, weight, 0.0)
        w_sc[0] = weight
        w_sc[1] = jnp.where(live, weight * (inv_ref[2] - delta) * scaling, 0.0)
        w_sc[2] = weight * scaling

        code_ids = lax.broadcasted_iota(jnp.int32, (tasks, tile_rows), 0)
        own_lse = stat_ref[0]
        own_gd = stat_ref[1]
        peak = own_lse
        rows_lse = [lse_sc[peer, pl.ds(own, 1), :] for peer in range(devices)]
        rows_gd = [gd_sc[peer, pl.ds(own, 1), :] for peer in range(devices)]
        for peer in range(devices):
            peak = jnp.maximum(peak, jnp.where(code_ids == given[peer], rows_lse[peer], masked_value))
        own_power = jnp.exp2(own_lse - peak)
        total = own_power
        delta = own_power * own_gd
        for peer in range(devices):
            here = code_ids == given[peer]
            power = jnp.where(here, jnp.exp2(rows_lse[peer] - peak), 0.0)
            total = total + power
            delta = delta + jnp.where(here, power * rows_gd[peer], 0.0)
        inverse = 1.0 / total
        delta = delta * inverse
        own_weight = own_power * inverse
        d_sc[0] = peak
        d_sc[1] = inverse
        d_sc[2] = delta
        d_sc[3] = own_weight
        d_sc[4] = own_weight * stat_ref[2]
        d_sc[5] = own_weight * stat_ref[2] * (own_gd - delta) * scaling
        d_sc[6] = own_weight * (own_gd - delta) * scaling
        d_sc[7] = own_weight * scaling
        d_sc[8] = own_weight * stat_ref[2] * scaling

        nothing = jnp.zeros((head_dim, tile_rows), jnp.bfloat16)
        for source in range(1, devices):
            odd = lax.rem(jnp.maximum(codes[source], 0), 2) == 1
            first = w_sc[0, source : source + 1, :]
            second = w_sc[1, source : source + 1, :]
            turned = qgt_in_ref[source - 1].astype(jnp.float32)
            g_first = (turned[head_dim:] * first).astype(jnp.bfloat16)
            q_first = (turned[:head_dim] * w_sc[2, source : source + 1, :]).astype(jnp.bfloat16)
            q_second = (turned[:head_dim] * second).astype(jnp.bfloat16)
            xin_ref[source, :head_dim, :tile_rows] = jnp.where(odd, q_second, g_first)
            xin_ref[source, :head_dim, tile_rows:] = jnp.where(odd, q_first, nothing)
            xin_ref[source, head_dim:, :tile_rows] = jnp.where(odd, g_first, q_second)
            xin_ref[source, head_dim:, tile_rows:] = jnp.where(odd, nothing, q_first)
        for source in range(1, devices):
            head = lax.rem(jnp.maximum(codes[source], 0), groups)
            grad_ref[head] += dot_t(pd_in_ref[source - 1], xin_ref[source])

        for load in loads:
            load.wait()
        for head in range(groups):
            for tile in range(tiles_dev):
                code = tile * groups + head
                first = d_sc[3, code : code + 1, :]
                second = d_sc[6, code : code + 1, :]
                mix = mix_ref[head, tile].astype(jnp.float32)
                acc_ref[0, code] = mix[:head_dim] * first
                acc_ref[1, code] = mix[2 * head_dim :] * d_sc[7, code : code + 1, :] + mix[head_dim : 2 * head_dim] * second

        for peer in range(devices):
            code = given[peer]

            @pl.when(code >= 0)
            def _(peer=peer, code=code):
                at = pl.ds(code, 1)
                part_w = jnp.exp2(lse_sc[peer, pl.ds(own, 1), :] - d_sc[0, at, :]) * d_sc[1, at, :]
                scaled_w = part_w * scaling
                shift = scaled_w * (gd_sc[peer, pl.ds(own, 1), :] - d_sc[2, at, :])
                mix = back_ref[peer, : 3 * head_dim, :].astype(jnp.float32)
                acc_ref[0, code] += mix[:head_dim] * part_w
                acc_ref[1, code] += mix[2 * head_dim :] * scaled_w + mix[head_dim : 2 * head_dim] * shift

        sub = lax.broadcasted_iota(jnp.int32, (tile_rows, tile_rows), 0)
        lane = lax.broadcasted_iota(jnp.int32, (tile_rows, tile_rows), 1)
        unit = jnp.where(sub == lane, 1.0, 0.0).astype(jnp.bfloat16)
        for tile in range(tiles_dev):
            rows = slice(tile * tile_rows, (tile + 1) * tile_rows)
            for head in range(0, groups, 2):
                cols = slice(head * head_dim, (head + 2) * head_dim)
                code = tile * groups + head
                both = jnp.concatenate([acc_ref[0, code], acc_ref[0, code + 1]], axis=0).astype(jnp.bfloat16)
                out_ref[rows, cols] = dot_t(unit, both).astype(jnp.bfloat16)
                both = jnp.concatenate([acc_ref[1, code], acc_ref[1, code + 1]], axis=0).astype(jnp.bfloat16)
                dq_ref[rows, cols] = dot_t(unit, both).astype(jnp.bfloat16)
        stores = [
            pltpu.make_async_copy(src, dst, out_sem.at[index])
            for index, (src, dst) in enumerate(((out_ref, out_hbm), (dq_ref, dq_hbm), (dk_ref, dk_hbm), (dv_ref, dv_hbm)))
        ]
        stores[0].start()
        stores[1].start()

        for code in range(tasks):

            @pl.when(named[code])
            def _(code=code):
                tile, head = code // groups, code % groups
                rows = slice(0, (tile + 1) * tile_rows)
                cols = slice(tile * pair, (tile + 1) * pair)
                fill_factor(
                    x_ref, qgt_ref, head, tile, *(d_sc[i, code : code + 1, :] for i in (4, 5, 8)), tile_rows, head_dim
                )
                own_pairs(code).wait()
                base_ref[head, rows, :] += dot_t(pd_ref[head, rows, cols], x_ref[head, :, cols])

        lane = lax.broadcasted_iota(jnp.int32, (tile_rows, 2 * head_dim), 1)
        for head in range(0, groups, 2):
            cols = slice(head * head_dim, (head + 2) * head_dim)
            for first in range(tiles_dev):
                rows = slice(first * tile_rows, (first + 1) * tile_rows)
                even, odd = (base_ref[h, rows, :] + grad_ref[h, rows, :] for h in (head, head + 1))
                dv_ref[rows, cols] = jnp.where(lane < head_dim, even, odd).astype(jnp.bfloat16)
                swapped = jnp.where(lane < head_dim, odd, even)
                dk_ref[rows, cols] = pltpu.roll(swapped, head_dim, 1).astype(jnp.bfloat16)
        stores[2].start()
        stores[3].start()
        for store in stores:
            store.wait()

    return body


def fast_local(query, key, value, grad_out, picks):
    row_count, columns = query.shape
    tiles_dev, groups, picked = picks.shape
    head_dim = columns // groups
    tile_rows = row_count // tiles_dev
    devices = lax.axis_size("ctx")
    tasks = tiles_dev * groups
    smem = pl.BlockSpec(memory_space=pltpu.SMEM)
    vmem = pl.BlockSpec(memory_space=pltpu.VMEM)
    far = pl.BlockSpec(memory_space=pltpu.HBM)
    low = jnp.bfloat16
    wide = jnp.float32
    width = 2 * head_dim
    shape = jax.ShapeDtypeStruct
    dma = pltpu.SemaphoreType.DMA
    small = pltpu.CompilerParams(vmem_limit_bytes=vmem_grant)
    near = pltpu.VMEM

    def away(*arrays):
        return tuple(pltpu.with_memory_space_constraint(x, pltpu.HBM) for x in arrays)

    def keep(*arrays):
        return tuple(pltpu.with_memory_space_constraint(x, pltpu.VMEM) for x in arrays)


    send_q, task_of = pl.pallas_call(
        pack_kernel(tiles_dev, groups, picked, tile_rows, head_dim, devices),
        out_shape=(shape((devices, tile_rows + 8, width), low), shape((devices,), jnp.int32)),
        in_specs=[smem, vmem, vmem],
        out_specs=(vmem, smem),
        name="pack",
    )(picks, query, grad_out)
    recv_q = lax.all_to_all(send_q, "ctx", split_axis=0, concat_axis=0, tiled=True)

    kv, vkt, stats, table, info = pl.pallas_call(
        own_kernel(tiles_dev, groups, tile_rows, head_dim, devices),
        out_shape=(
            near((groups, row_count, width), low),
            near((groups, width, row_count), low),
            near((5, tasks, tile_rows), wide),
            near((devices, 8, tile_rows), wide),
            near((2 * devices, tile_rows), wide),
        ),
        in_specs=[smem, smem] + [far] * 4,
        out_specs=tuple([vmem] * 5),
        scratch_shapes=[pltpu.VMEM((row_count, columns), low)] * 4
        + [pltpu.VMEM((tasks, 8, tile_rows), wide), dma((4,))],
        compiler_params=small,
        name="own",
    )(*away(picks, task_of, query, key, value, grad_out))

    slot = 3 * head_dim + 3 * devices
    in_shape = (devices - 1, row_count, 2 * tile_rows)
    send_b, inverse_in = pl.pallas_call(
        serve_kernel(groups, tile_rows, head_dim, devices),
        out_shape=(pltpu.HBM((devices, slot, tile_rows), low), near((3, devices, tile_rows), wide)),
        in_specs=[vmem] * 5,
        out_specs=(far, vmem),
        scratch_shapes=[
            pltpu.VMEM((devices, slot, tile_rows), low),
            pltpu.VMEM((3 * devices, tile_rows), wide),
            dma(()),
        ],
        compiler_params=pltpu.CompilerParams(
            vmem_limit_bytes=vmem_grant
        ),
        name="serve",
    )(*keep(info, recv_q, kv, vkt, table))
    recv_b = lax.all_to_all(send_b, "ctx", split_axis=0, concat_axis=0, tiled=True)

    pairs_in, qgt_in, lists_in = pl.pallas_call(
        again_kernel(groups, tile_rows, head_dim, devices),
        out_shape=(near(in_shape, low), near((devices - 1, width, tile_rows), low), near((devices, 8, width), wide)),
        in_specs=[smem, vmem, vmem, vmem],
        out_specs=(vmem, vmem, vmem),
        compiler_params=small,
        name="again",
    )(*away(picks), *keep(recv_q, kv, inverse_in))

    mix_shape = (groups, tiles_dev, 3 * head_dim, tile_rows)
    pair_shape = (groups, row_count, 2 * row_count)
    turned_shape = (groups, width, row_count)
    base_shape = (groups, row_count, width)
    factor_shape = (groups, width, 2 * row_count)
    qgt, mix, pairs, base = pl.pallas_call(
        rest_kernel(tiles_dev, groups, tile_rows, head_dim, devices),
        out_shape=(
            pltpu.HBM(turned_shape, low),
            pltpu.HBM(mix_shape, low),
            pltpu.HBM(pair_shape, low),
            pltpu.HBM(base_shape, wide),
        ),
        in_specs=[far] * 2 + [vmem] * 4,
        out_specs=tuple([far] * 4),
        scratch_shapes=[pltpu.VMEM((row_count, columns), low)] * 2
        + [
            pltpu.VMEM(turned_shape, low),
            pltpu.VMEM(mix_shape, low),
            pltpu.VMEM(pair_shape, low),
            pltpu.VMEM(base_shape, wide),
            pltpu.VMEM(factor_shape, low),
            pltpu.VMEM((3, tasks, tile_rows), wide),
            dma((2,)),
            dma((tiles_dev + 3,)),
        ],
        compiler_params=small,
        name="rest",
    )(*away(query, grad_out), *keep(kv, vkt, stats, info))

    return pl.pallas_call(
        final_kernel(tiles_dev, groups, picked, tile_rows, head_dim, devices),
        out_shape=tuple([shape((row_count, columns), low)] * 4),
        in_specs=[vmem] * 7 + [far] * 4,
        out_specs=tuple([far] * 4),
        scratch_shapes=[
            pltpu.VMEM((groups, width, row_count), low),
            pltpu.VMEM(mix_shape, low),
            pltpu.VMEM(pair_shape, low),
        ]
        + [pltpu.VMEM((row_count, columns), low)] * 4
        + [
            pltpu.VMEM((2, tasks, head_dim, tile_rows), wide),
            pltpu.VMEM((groups, row_count, width), wide),
            pltpu.VMEM((groups, row_count, width), wide),
            pltpu.VMEM((devices, devices, tile_rows), wide),
            pltpu.VMEM((devices, devices, tile_rows), wide),
            pltpu.VMEM((3, devices, tile_rows), wide),
            pltpu.VMEM((9, tasks, tile_rows), wide),
            pltpu.VMEM((groups, width, 2 * row_count), low),
            pltpu.VMEM((devices, width, 2 * tile_rows), low),
            dma((3 + tasks,)),
            dma((4,)),
        ],
        compiler_params=small,
        name="final",
    )(*keep(info, lists_in, recv_b, qgt_in, stats, inverse_in, pairs_in), *away(qgt, mix, pairs, base))


def choose(query, key, value, grad_out, picks):
    pair_bytes = lax.axis_size("ctx") * query.shape[0] * (query.shape[0] // picks.shape[0]) * 4
    plan = fast_local if pair_bytes <= pair_budget else local
    return plan(query, key, value, grad_out, picks)


def solution(mesh):
    placed = (
        P("ctx", "head"),
        P("ctx", "head"),
        P("ctx", "head"),
        P("ctx", "head"),
        P("ctx", "head", None),
    )
    return jax.shard_map(
        choose,
        mesh=mesh,
        in_specs=placed,
        out_specs=(P("ctx", "head"), P("ctx", "head"), P("ctx", "head"), P("ctx", "head")),
        check_vma=False,
    )
```
